256 devices in a mesh: cls: 128 (over z, y, x), dp: 2 (over core).
Axes of the slice: x: 4, y: 4, z: 8, core: 2. Of those that a mesh axis runs over, the one named last changes fastest.
Arguments:
- images: bfloat16 [4096, 4096], P(('cls', 'dp')), may hold values from -6 to 6
- references: bfloat16 [128, 72, 4096], P('cls'), may hold values from -1 to 1
- candidates: int32 [4096, 8], P(('cls', 'dp')), may hold values from 0 to 127, all different within a row; in each aligned block of 16 rows (0 to 15, 16 to 31, ...) at most 2 rows name the same one
- inv_noise: bfloat16 [4096], P(('cls', 'dp')), may hold values from 0.5 to 150
Outputs:
- class_sums: float32 [128, 72, 4096], P('cls', 'dp')
- class_weights: float32 [128, 72], P('cls', 'dp')
The draws below stay inside these ranges and needn't reach their ends.
Inputs may be any that keep to these rules, and one draw needn't show every extreme that they name: `candidates`: the classes of one row differ. In each aligned block of 16 rows (the rows of one device) no class is named by more than 2 rows, a bound that some block reaches.
All inputs are finite; a program needn't handle non-finite values.
Results may differ from the reference program's by a relative error of at most 0.006.
Values may be sent and summed in bfloat16 or wider, within the bound.
No kernel may reach another device: no remote copies, remote signals or barrier semaphores. Data moves between devices by JAX's collectives and lax.ppermute only.
A program may use at most 64 MiB of HBM per device.

```python
import math
import jax
import jax.numpy as jnp
import numpy as np
from jax import lax

PIX = 64
ROTS = 72
SHIFTS = 9
TOP = 8
P_DEV = 16
IMG = 4096
CLASSES = 128
PARTICLES = 4096
MOST = 2
N_CLS = 128
N_DP = 2


def draw_references(key, part):
    key_base, key_scale = jax.random.split(jax.random.fold_in(key, 17))
    base_draw = jax.random.normal(key_base, (CLASSES, ROTS, IMG), jnp.float32)
    row_scale = jnp.exp(jax.random.uniform(key_scale, (CLASSES, ROTS, 1), jnp.float32, jnp.log(0.5), jnp.log(2.0)))
    values = jnp.clip(base_draw * row_scale * IMG ** (-0.5), -1.0, 1.0)
    return values.astype(jnp.bfloat16)


def draw_inv_noise(key, part):
    key_base = jax.random.fold_in(jax.random.fold_in(key, 29), 0)
    values = jnp.exp(jax.random.uniform(key_base, (PARTICLES,), jnp.float32, jnp.log(0.5), jnp.log(3.0)))
    return values.astype(jnp.bfloat16)


def level_of(key, shape, shards, least, largest):
    factor_of, own = 1.0, jax.random.fold_in(key, 6)
    for dim, shards_of in shards:
        steps = jnp.exp(jax.random.uniform(jax.random.fold_in(own, dim), (shards_of,), jnp.float32, least / len(shards), largest / len(shards)))
        factor_of = factor_of * jnp.repeat(steps, shape[dim] // shards_of).reshape([-1 if axis == dim else 1 for axis in range(len(shape))])
    return factor_of


def routed_block(key, own, number, rows, count, top, reach, skew):
    order = jax.random.permutation(key, count)
    crowded, usual = portions_of(count, rows * top, reach, skew, True), portions_of(count, rows * top, reach, skew, False)
    places = jnp.arange(count)

    def named(sizes, rotation):
        used = int((sizes > 0).sum())
        fixed = max(1, used // 4)
        passed = fixed + (places - fixed + rotation * (used - fixed)) % max(1, count - fixed)
        return jnp.zeros((count,), jnp.int32).at[order[jnp.where(places < fixed, places, passed)]].set(jnp.asarray(sizes, jnp.int32))

    sizes = jnp.where(number % 4 == 0, named(crowded, number // 4), named(usual, number - number // 4 - 1))
    mixed = jax.random.permutation(jax.random.fold_in(own, 3), count)
    donor, taker = mixed[0:count // 2 * 2:2], mixed[1:count // 2 * 2:2]
    margin = jnp.minimum(sizes[donor] - 1, reach - sizes[taker]) // 2
    margin = jnp.where((donor == order[0]) | (taker == order[0]) | (sizes[taker] == 0), 0, jnp.maximum(margin, 0))
    passed = jax.random.randint(jax.random.fold_in(own, 4), (count // 2,), 0, 1 << 20) % (margin + 1)
    sizes = sizes.at[donor].add(-passed).at[taker].add(passed)
    members = jnp.searchsorted(jnp.cumsum(sizes), jnp.arange(rows * top), side="right").astype(jnp.int32)
    table = members.reshape(top, rows).T
    table = table[jax.random.permutation(jax.random.fold_in(own, 1), rows)]
    rotation = jax.random.randint(jax.random.fold_in(own, 2), (rows, 1), 0, top)
    return jnp.take_along_axis(table, (jnp.arange(top)[None, :] + rotation) % top, axis=1)


def portions_of(count, total, most, slope, full):
    weights = [(1 << 20) // math.isqrt(rank ** slope) + 1 for rank in range(1, count + 1)]
    largest = most if full else min(most, max(-(-total // count), total * weights[0] // sum(weights)))
    least = 1 if total - largest >= count - 1 else 0
    holding, rest = [largest] + [least] * (count - 1), total - largest - least * (count - 1)
    while rest > 0:
        free = [i for i in range(1, count) if holding[i] < largest] or [i for i in range(1, count) if holding[i] < most]
        pool, remaining = sum([weights[i] for i in free]), rest
        for i in free:
            addition = min(most - holding[i], max(1, remaining * weights[i] // pool), rest)
            holding[i] = holding[i] + addition
            rest = rest - addition
    return np.array(holding)


def centred(stream_key, shape, spread, limit, cuts=(), held_as=jnp.bfloat16):
    drawn = jax.random.normal(stream_key, shape, jnp.float32) * spread
    if len(cuts) > 0:
        drawn = level_of(stream_key, shape, cuts, -0.22, 0.18) * drawn
    return jnp.clip(drawn, min=-limit, max=limit).astype(held_as)


def setup_inputs(seed: int = 0) -> dict:
    key_of = jax.random.split(jax.random.key(seed), 5)
    images = centred(key_of[0], (PARTICLES, IMG), 1.0, 6.0, ((0, 256),))
    references = draw_references(jax.random.fold_in(key_of[4], 71), 0)
    candidates_keys = jax.random.split(jax.random.fold_in(key_of[2], 1), PARTICLES // P_DEV)
    candidates_turns = jax.random.permutation(jax.random.fold_in(key_of[2], 3), PARTICLES // P_DEV)
    candidates = jax.vmap(lambda own, number: routed_block(jax.random.fold_in(key_of[2], 2), own, number, P_DEV, CLASSES, TOP, MOST, 2))(candidates_keys, candidates_turns).reshape((PARTICLES, TOP))
    inv_noise = draw_inv_noise(jax.random.fold_in(key_of[4], 71), 0)
    return {"images": images, "references": references, "candidates": candidates, "inv_noise": inv_noise}


OFFSETS = ((0, 0), (1, 0), (-1, 0), (0, 1), (0, -1), (1, 1), (1, -1), (-1, 1), (-1, -1))


def shift_stack(rotated):
    square = rotated.reshape(ROTS, PIX, PIX)
    stacked = jnp.stack([jnp.roll(square, (shift_row, shift_col), axis=(1, 2)) for shift_row, shift_col in OFFSETS], axis=1)
    return stacked.reshape(ROTS * SHIFTS, IMG)


def unshift_sum(summed_back):
    square = summed_back.reshape(ROTS, SHIFTS, PIX, PIX)
    result = jnp.zeros((ROTS, PIX, PIX), jnp.float32)
    for position, offset in enumerate(OFFSETS):
        result = result + jnp.roll(square[:, position], (-offset[0], -offset[1]), axis=(1, 2))
    return result.reshape(ROTS, IMG)


def reference(images, references, candidates, inv_noise):
    capacity = MOST * N_CLS * N_DP
    rows_all = jnp.arange(PARTICLES, dtype=jnp.int32)
    member = jnp.zeros((PARTICLES, CLASSES), jnp.int32).at[rows_all[:, None], candidates].add(1)
    before = jnp.cumsum(member, axis=0) - member
    slot_rank = jnp.take_along_axis(before, candidates, axis=1)
    precision = inv_noise.astype(jnp.float32)

    def entries(class_id):
        in_class = member[:, class_id] > 0
        entry_rows = jnp.nonzero(in_class, size=capacity, fill_value=0)[0].astype(jnp.int32)
        is_live = jnp.arange(capacity, dtype=jnp.int32) < jnp.sum(in_class.astype(jnp.int32))
        return entry_rows, is_live

    def score_class(class_id):
        entry_rows, is_live = entries(class_id)
        entry_images = images[entry_rows]
        rotated = lax.dynamic_index_in_dim(references, class_id, 0, keepdims=False)
        shifted = shift_stack(rotated)
        ref_norms = jnp.sum(jnp.square(rotated.astype(jnp.float32)), axis=1)
        products = lax.dot_general(entry_images, shifted, (((1,), (1,)), ((), ())), preferred_element_type=jnp.float32)
        return precision[entry_rows][:, None] * (products - 0.5 * jnp.repeat(ref_norms, SHIFTS)[None, :])

    scores = lax.map(score_class, jnp.arange(CLASSES, dtype=jnp.int32))
    slot_peak = jnp.max(scores, axis=-1)
    slot_sum = jnp.sum(jnp.exp(scores - slot_peak[..., None]), axis=-1)
    home_peaks = slot_peak[candidates, slot_rank]
    home_sums = slot_sum[candidates, slot_rank]
    row_peak = jnp.max(home_peaks, axis=1)
    norm_total = jnp.sum(home_sums * jnp.exp(home_peaks - row_peak[:, None]), axis=1)

    def back_class(class_id):
        entry_rows, is_live = entries(class_id)
        entry_images = images[entry_rows]
        class_scores = lax.dynamic_index_in_dim(scores, class_id, 0, keepdims=False)
        entry_weights = (jnp.exp(class_scores - row_peak[entry_rows][:, None]) / norm_total[entry_rows][:, None]).astype(jnp.bfloat16)
        entry_weights = jnp.where(is_live[:, None], entry_weights, jnp.zeros_like(entry_weights))
        summed_back = lax.dot_general(entry_weights, entry_images, (((0,), (0,)), ((), ())), preferred_element_type=jnp.float32)
        weight_tot = jnp.sum(entry_weights.astype(jnp.float32), axis=0).reshape(ROTS, SHIFTS).sum(axis=1)
        return unshift_sum(summed_back), weight_tot

    class_sums, class_weights = lax.map(back_class, jnp.arange(CLASSES, dtype=jnp.int32))
    return class_sums, class_weights
```

```python
import functools
import math

import jax
import jax.numpy as jnp
from jax import lax
from jax.experimental import pallas as pl
from jax.experimental.pallas import tpu as pltpu
from jax.sharding import Mesh
from jax.sharding import PartitionSpec as P

LANES = 128
SLOTS = 2
PLANES = 8
FAR = 1e30
ROW_SHIFTS = (0, 1, -1)
COL_SHIFTS = (0, 1, -1)
MIB = 1024 * 1024
F32, BF16 = jnp.float32, jnp.bfloat16


def tile_of(t):
    return slice(t * LANES, (t + 1) * LANES)


def lane_row():
    return lax.broadcasted_iota(jnp.int32, (1, LANES), 1)


def fold_tile(load, q, tiles, low):
    first, second = load(q // 2), load(tiles // 2 + q // 2)
    half = LANES // 2
    if q % 2 == 0:
        return jnp.where(low, first, pltpu.roll(second, half, 1))
    return jnp.where(low, pltpu.roll(first, half, 1), second)


def unfold_tile(load, t, tiles, low):
    half = LANES // 2
    if t < tiles // 2:
        return jnp.where(low, load(2 * t), pltpu.roll(load(2 * t + 1), half, 1))
    first = 2 * t - tiles
    return jnp.where(low, pltpu.roll(load(first), half, 1), load(first + 1))


def pack_kernel(cand_ref, noise_ref, img_ref, send_ref, hold_ref):
    rows, top = cand_ref.shape
    planes, depth, _ = send_ref.shape
    tiles = img_ref.shape[1] // LANES
    low = lane_row() < LANES // 2
    for q in range(tiles):
        tile = fold_tile(lambda t: img_ref[:, tile_of(t)].astype(F32), q, tiles, low)
        hold_ref[q * rows : (q + 1) * rows] = tile.astype(BF16)
    row_id = lax.broadcasted_iota(jnp.int32, (rows, LANES), 0)
    lane_id = lax.broadcasted_iota(jnp.int32, (rows, LANES), 1)
    noise = jnp.sum(
        jnp.where(
            lax.broadcasted_iota(jnp.int32, (rows, rows), 0)
            == lax.broadcasted_iota(jnp.int32, (rows, rows), 1),
            noise_ref[...].astype(F32),
            0.0,
        ),
        axis=1,
        keepdims=True,
    )
    facts = jnp.where(lane_id == 0, noise, 0.0)
    facts = jnp.where(lane_id == 1, (row_id + 1).astype(F32), facts)
    hold_ref[tiles * rows :] = facts.astype(BF16)
    for plane in range(planes):
        send_ref[plane, : (tiles + 1) * rows] = hold_ref[...]
    named = [jnp.broadcast_to(cand_ref[:, k : k + 1], (rows, LANES)) for k in range(top)]
    earlier = (
        lax.broadcasted_iota(jnp.int32, (rows, rows), 0)
        > lax.broadcasted_iota(jnp.int32, (rows, rows), 1)
    ).astype(BF16)
    group = SLOTS * planes
    slot = (lane_id // planes) % SLOTS
    from_here = lane_id % planes == lax.axis_index("z")
    wide = depth // rows - tiles - 1
    for plane in range(planes):
        for part in range(wide):
            first = (plane * wide + part) * (LANES // group)
            cls = first + lane_id // group
            member = named[0] == cls
            for k in range(1, top):
                member = member | (named[k] == cls)
            before = jnp.dot(
                earlier, member.astype(F32).astype(BF16), preferred_element_type=F32
            )
            pick = member & (before == slot.astype(F32)) & from_here
            at = (tiles + 1 + part) * rows
            send_ref[plane, at : at + rows] = pick.astype(F32).astype(BF16)


def pick_kernel(recv_ref, send_ref, column_ref, pick_ref):
    planes = recv_ref.shape[0]
    owners, depth, _ = send_ref.shape
    rows = column_ref.shape[0] // planes
    tiles = column_ref.shape[1] // LANES
    wide = pick_ref.shape[1] // LANES
    for z in range(planes):
        for t in range(tiles):
            column_ref[z * rows : (z + 1) * rows, tile_of(t)] = recv_ref[
                z, t * rows : (t + 1) * rows
            ]
        for t in range(wide):
            pick_ref[z * rows : (z + 1) * rows, tile_of(t)] = recv_ref[
                z, (tiles + t) * rows : (tiles + t + 1) * rows
            ]
    pick = pick_ref[...].astype(F32).T.astype(BF16)
    group = depth // tiles
    width = 3
    for t in range(0, tiles, width):
        lanes = slice(t * LANES, (t + width) * LANES)
        got = jnp.dot(pick, column_ref[:, lanes], preferred_element_type=F32).astype(BF16)
        for i in range(width):
            for c in range(owners):
                send_ref[c, (t + i) * group : (t + i + 1) * group] = got[
                    c * group : (c + 1) * group, tile_of(i)
                ]


def shift_kernel(rot_ref, out_ref, half_ref):
    count, pixels = rot_ref.shape
    tiles = pixels // LANES
    side = LANES // 2
    groups = len(COL_SHIFTS) * count
    lane = lane_row()
    low = lane < side
    column = lane % side
    square = jnp.zeros((count, LANES), F32)
    for q in range(tiles):
        tile = fold_tile(lambda t: rot_ref[:, tile_of(t)].astype(F32), q, tiles, low)
        square = square + tile * tile
        right = jnp.where(
            column == 0, pltpu.roll(tile, LANES - side + 1, 1), pltpu.roll(tile, 1, 1)
        )
        left = jnp.where(
            column == side - 1, pltpu.roll(tile, side - 1, 1), pltpu.roll(tile, LANES - 1, 1)
        )
        for i, moved in enumerate((tile, right, left)):
            plain = moved.astype(BF16)
            for j, shift in enumerate(ROW_SHIFTS):
                to = q + shift
                value = plain
                if not 0 <= to < tiles:
                    to = to % tiles
                    value = pltpu.roll(moved, side, 1).astype(BF16)
                at = j * groups + i * count
                out_ref[at : at + count, tile_of(to)] = value
    half = 0.5 * jnp.sum(square, axis=1, keepdims=True)
    half_ref[...] = jnp.broadcast_to(half, half_ref.shape)


def score_kernel(recv_ref, shifted_ref, half_ref, x_ref, s_ref, tile_ref, *, pad):
    owners, depth, _ = recv_ref.shape
    tiles = x_ref.shape[1] // LANES - 2
    group = depth // (tiles + 1)
    slots = owners * group
    groups = s_ref.shape[0]
    count = half_ref.shape[0]
    for c in range(owners):
        for t in range(tiles):
            x_ref[c * group : (c + 1) * group, tile_of(t + 1)] = recv_ref[
                c, t * group : (t + 1) * group
            ]
    half_turn = LANES // 2
    x_ref[:, tile_of(0)] = pltpu.roll(x_ref[:, tile_of(tiles)].astype(F32), half_turn, 1).astype(
        BF16
    )
    x_ref[:, tile_of(tiles + 1)] = pltpu.roll(x_ref[:, tile_of(1)].astype(F32), half_turn, 1).astype(
        BF16
    )
    facts = recv_ref[:, tiles * group :, :].reshape(slots, LANES)
    choose = (
        lax.broadcasted_iota(jnp.int32, (16, LANES), 0)
        == lax.broadcasted_iota(jnp.int32, (16, LANES), 1)
    ).astype(F32).astype(BF16)
    turned = lax.dot_general(
        choose, facts, (((1,), (1,)), ((), ())), preferred_element_type=F32
    )
    noise, number = turned[0:1], turned[1:2]
    products = lax.dot_general(
        shifted_ref[...],
        x_ref[:, LANES : (tiles + 1) * LANES],
        (((1,), (1,)), ((), ())),
        preferred_element_type=F32,
    )
    half = half_ref[:, 0:1]
    row = lax.broadcasted_iota(jnp.int32, half.shape, 0)
    half = jnp.where(row % (count // 2) >= count // 2 - pad, FAR, half)
    half = jnp.concatenate([half] * len(COL_SHIFTS), axis=0)
    peak = None
    for i in range(len(ROW_SHIFTS)):
        scores = noise * (products[i * groups : (i + 1) * groups] - half)
        s_ref[:, i * slots : (i + 1) * slots] = scores
        top = jnp.max(scores, axis=0, keepdims=True)
        peak = top if peak is None else jnp.maximum(peak, top)
    total = jnp.zeros_like(peak)
    for i in range(len(ROW_SHIFTS)):
        scores = s_ref[:, i * slots : (i + 1) * slots]
        total = total + jnp.sum(jnp.exp(scores - peak), axis=0, keepdims=True)
    parts = slots // LANES
    for i, value in enumerate((peak, total, number)):
        for h in range(parts):
            tile_ref[i * parts + h : i * parts + h + 1] = value[:, tile_of(h)]
    tile_ref[3 * parts :] = jnp.zeros_like(tile_ref[3 * parts :])


def sum_kernel(s_ref, x_ref, mine_ref, all_ref, keep_ref, give_ref, w_ref, y_ref):
    groups = s_ref.shape[0]
    slots = x_ref.shape[0]
    pixels = x_ref.shape[1] - 2 * LANES
    owners = all_ref.shape[0] // 8
    count = groups // len(COL_SHIFTS)
    half_count = count // 2
    parts = slots // LANES
    side = LANES // 2
    lane = lane_row()
    second = (lane // PLANES) % SLOTS == 1

    def partner(row):
        return jnp.where(second, pltpu.roll(row, PLANES, 1), pltpu.roll(row, LANES - PLANES, 1))

    peaks, scales = [], []
    for h in range(parts):
        own = mine_ref[2 * parts + h : 2 * parts + h + 1]
        across = partner(own)
        shown = [all_ref[pl.ds(i * parts + h, owners, stride=8), :] for i in range(3)]
        found = []
        for slot in range(SLOTS):
            target = jnp.where(second == (slot == 1), own, across)
            same = shown[2] == target
            peak = jnp.max(jnp.where(same, shown[0], -jnp.inf), axis=0, keepdims=True)
            peak = jnp.maximum(peak, partner(peak))
            part = shown[1] * jnp.exp(jnp.minimum(shown[0] - peak, 0.0))
            total = jnp.sum(jnp.where(same, part, 0.0), axis=0, keepdims=True)
            found.append((peak, total + partner(total)))
        peaks.append(jnp.where(second, found[1][0], found[0][0]))
        total = jnp.where(second, found[1][1], found[0][1])
        scales.append(jnp.where(own > 0, 1.0 / total, 0.0))
    peak = jnp.concatenate(peaks, axis=1)
    scale = jnp.concatenate(scales, axis=1)
    row_total = jnp.zeros((groups, 1), F32)
    for i in range(len(ROW_SHIFTS)):
        part = slice(i * slots, (i + 1) * slots)
        weights = (jnp.exp(jnp.minimum(s_ref[:, part] - peak, 0.0)) * scale).astype(BF16)
        w_ref[:, part] = weights
        row_total = row_total + jnp.sum(weights.astype(F32), axis=1, keepdims=True)
    class_total = sum(row_total[i * count : (i + 1) * count] for i in range(len(COL_SHIFTS)))
    keep_ref[:, pixels:] = jnp.broadcast_to(class_total[:half_count], (half_count, LANES))
    give_ref[:, pixels:] = jnp.broadcast_to(class_total[half_count:], (half_count, LANES))
    width = y_ref.shape[1]
    column = lane % side
    for first in range(0, pixels, width):
        y_ref[...] = sum(
            jnp.dot(
                w_ref[:, i * slots : (i + 1) * slots],
                x_ref[:, (1 + shift) * LANES + first : (1 + shift) * LANES + first + width],
                preferred_element_type=F32,
            )
            for i, shift in enumerate(ROW_SHIFTS)
        )
        for t in range(width // LANES):
            plain = y_ref[:count, tile_of(t)]
            right = y_ref[count : 2 * count, tile_of(t)]
            left = y_ref[2 * count :, tile_of(t)]
            back = jnp.where(
                column == side - 1,
                pltpu.roll(right, side - 1, 1),
                pltpu.roll(right, LANES - 1, 1),
            )
            forth = jnp.where(
                column == 0, pltpu.roll(left, LANES - side + 1, 1), pltpu.roll(left, 1, 1)
            )
            moved = plain + back + forth
            at = slice(first + t * LANES, first + (t + 1) * LANES)
            keep_ref[:, at] = moved[:half_count]
            give_ref[:, at] = moved[half_count:]


def finish_kernel(keep_ref, other_ref, sums_ref, totals_ref):
    rots = totals_ref.shape[1]
    tiles = sums_ref.shape[0] // rots
    low = lane_row() < LANES // 2

    def load(t):
        return keep_ref[:rots, tile_of(t)] + other_ref[:rots, tile_of(t)]

    for t in range(tiles):
        sums_ref[pl.ds(t, rots, stride=tiles), :] = unfold_tile(load, t, tiles, low)
    total = load(tiles)
    here = lax.broadcasted_iota(jnp.int32, (rots, LANES), 0) == lax.broadcasted_iota(
        jnp.int32, (rots, LANES), 1
    )
    totals_ref[...] = jnp.sum(jnp.where(here, total, 0.0), axis=0, keepdims=True)[:, :rots]


def call(kernel, out_shape, count, limit, scratch=(), flops=0, moved=0):
    in_vmem = pl.BlockSpec(memory_space=pltpu.VMEM)
    return pl.pallas_call(
        kernel,
        out_shape=out_shape,
        in_specs=[in_vmem] * count,
        out_specs=jax.tree.map(lambda _: in_vmem, out_shape),
        scratch_shapes=list(scratch),
        cost_estimate=pl.CostEstimate(flops=flops, bytes_accessed=moved, transcendentals=0),
        compiler_params=pltpu.CompilerParams(vmem_limit_bytes=limit * MIB),
    )


def on_device(images, references, candidates, inv_noise):
    rows, top = candidates.shape
    cls_dev, rots, pixels = references.shape
    planes, owners = lax.axis_size("z"), lax.axis_size("xy")
    side = math.isqrt(pixels)
    tiles = pixels // LANES
    group = SLOTS * planes
    slots = owners * group
    assert cls_dev == 1 and planes == PLANES and LANES == 2 * side and rows == group
    wide = slots // LANES
    shape = jax.ShapeDtypeStruct
    exchange = functools.partial(lax.all_to_all, split_axis=0, concat_axis=0, tiled=True)

    packed = call(
        pack_kernel,
        shape((planes, (tiles + 1 + wide) * rows, LANES), BF16),
        3,
        8,
        [pltpu.VMEM(((tiles + 1) * rows, LANES), BF16)],
        moved=2 * MIB,
    )(candidates, inv_noise[None, :], images)
    column = exchange(packed, "z")

    half_rots = rots // 2
    half_count = -(-half_rots // 8) * 8
    own = references[0]
    flipped = jnp.where(
        lax.axis_index("dp") == 0, own, jnp.concatenate([own[half_rots:], own[:half_rots]], axis=0)
    )
    pad = half_count - half_rots
    padded = jnp.pad(flipped.reshape(2, half_rots, pixels), ((0, 0), (0, pad), (0, 0)))
    count = 2 * half_count
    groups = len(COL_SHIFTS) * count
    shifted, half_norm = call(
        shift_kernel,
        (shape((len(ROW_SHIFTS) * groups, pixels), BF16), shape((count, LANES), F32)),
        1,
        12,
        moved=12 * MIB,
    )(padded.reshape(count, pixels))

    picked = call(
        pick_kernel,
        shape((owners, (tiles + 1) * group, LANES), BF16),
        1,
        12,
        [
            pltpu.VMEM((planes * rows, (tiles + 1) * LANES), BF16),
            pltpu.VMEM((planes * rows, slots), BF16),
        ],
        moved=3 * MIB,
    )(column)
    received = exchange(picked, "xy")
    work = 2 * len(ROW_SHIFTS) * groups * slots * pixels
    x, scores, tile = call(
        functools.partial(score_kernel, pad=pad),
        (
            shape((slots, pixels + 2 * LANES), BF16),
            shape((groups, len(ROW_SHIFTS) * slots), F32),
            shape((8, LANES), F32),
        ),
        3,
        24,
        flops=work,
        moved=10 * MIB,
    )(received, shifted, half_norm)
    by_plane = exchange(jnp.broadcast_to(tile[None], (planes, 8, LANES)), "z")
    by_plane = by_plane.reshape(1, planes * 8, LANES)
    everyone = exchange(jnp.broadcast_to(by_plane, (owners, planes * 8, LANES)), "xy")
    half_shape = shape((half_count, pixels + LANES), F32)
    keep, give = call(
        sum_kernel,
        (half_shape, half_shape),
        4,
        24,
        [
            pltpu.VMEM((groups, len(ROW_SHIFTS) * slots), BF16),
            pltpu.VMEM((groups, 4 * LANES), F32),
        ],
        flops=work,
        moved=5 * MIB,
    )(scores, x, tile, everyone.reshape(owners * planes * 8, LANES))
    other = lax.ppermute(give, "dp", [(0, 1), (1, 0)])
    sums, totals = call(
        finish_kernel,
        (shape((half_rots * tiles, LANES), F32), shape((1, half_rots), F32)),
        2,
        8,
        moved=2 * MIB,
    )(keep, other)
    return sums.reshape(1, half_rots, pixels), totals


def solution(mesh):
    split = (PLANES, mesh.shape["cls"] // PLANES, mesh.shape["dp"])
    cube = Mesh(mesh.devices.reshape(split), ("z", "xy", "dp"))
    every = ("z", "xy", "dp")
    by_class = ("z", "xy")
    return jax.shard_map(
        on_device,
        mesh=cube,
        in_specs=(P(every, None), P(by_class, None, None), P(every, None), P(every)),
        out_specs=(P(by_class, "dp", None), P(by_class, "dp")),
        check_vma=False,
    )
```

```python
import functools
import math

import jax
import jax.numpy as jnp
from jax import lax
from jax.experimental import pallas as pl
from jax.experimental.pallas import tpu as pltpu
from jax.sharding import Mesh
from jax.sharding import PartitionSpec as P

LANES = 128
SLOTS = 2
PLANES = 8
FAR = 1e30
ROW_SHIFTS = (0, 1, -1)
COL_SHIFTS = (0, 1, -1)
MIB = 1024 * 1024
F32, BF16 = jnp.float32, jnp.bfloat16


def tile_of(t):
    return slice(t * LANES, (t + 1) * LANES)


def lane_row():
    return lax.broadcasted_iota(jnp.int32, (1, LANES), 1)


def fold_tile(load, q, tiles, low):
    first, second = load(q // 2), load(tiles // 2 + q // 2)
    half = LANES // 2
    if q % 2 == 0:
        return jnp.where(low, first, pltpu.roll(second, half, 1))
    return jnp.where(low, pltpu.roll(first, half, 1), second)


def unfold_tile(load, t, tiles, low):
    half = LANES // 2
    if t < tiles // 2:
        return jnp.where(low, load(2 * t), pltpu.roll(load(2 * t + 1), half, 1))
    first = 2 * t - tiles
    return jnp.where(low, pltpu.roll(load(first), half, 1), load(first + 1))


def pack_kernel(cand_ref, noise_ref, img_ref, send_ref):
    top, rows = cand_ref.shape
    tiles = img_ref.shape[1] // LANES
    low = lane_row() < LANES // 2
    row_id = lax.broadcasted_iota(jnp.int32, (rows, LANES), 0)
    lane_id = lax.broadcasted_iota(jnp.int32, (rows, LANES), 1)
    diagonal = lax.broadcasted_iota(jnp.int32, (rows, rows), 0) == lax.broadcasted_iota(
        jnp.int32, (rows, rows), 1
    )
    noise = jnp.sum(
        jnp.where(diagonal, noise_ref[...].astype(F32), 0.0), axis=1, keepdims=True
    )
    place = lax.broadcasted_iota(jnp.int32, (top, LANES), 1) == (
        lax.broadcasted_iota(jnp.int32, (top, LANES), 0) + 2
    )
    facts = lax.dot_general(
        cand_ref[...].astype(F32).astype(BF16),
        place.astype(F32).astype(BF16),
        (((0,), (0,)), ((), ())),
        preferred_element_type=F32,
    )
    facts = jnp.where(lane_id == 0, noise, facts)
    facts = jnp.where(lane_id == 1, (row_id + 1).astype(F32), facts)
    send_ref[tiles * rows :] = facts.astype(BF16)
    for q in range(tiles):
        tile = fold_tile(lambda t: img_ref[:, tile_of(t)].astype(F32), q, tiles, low)
        send_ref[q * rows : (q + 1) * rows] = tile.astype(BF16)


def pick_kernel(*refs, steps, top):
    recv_refs, send_ref, column_ref = refs[: len(steps)], refs[-2], refs[-1]
    planes = len(steps) - 1
    owners, depth, _ = send_ref.shape
    rows = column_ref.shape[0] // planes
    tiles = column_ref.shape[1] // LANES
    group = depth // tiles
    slots = owners * group
    cut = recv_refs[-2].shape[0] // rows
    for j in range(planes):
        for t in range(tiles):
            from_ref, at = recv_refs[j], t
            if j == planes - 1 and t >= cut:
                from_ref, at = recv_refs[j + 1], t - cut
            column_ref[j * rows : (j + 1) * rows, tile_of(t)] = from_ref[
                at * rows : (at + 1) * rows
            ]
    count = planes * rows
    facts = column_ref[:, tile_of(tiles - 1)].astype(F32)
    here = lax.axis_index("z")
    row = lax.broadcasted_iota(jnp.int32, (count, 1), 0)
    sender = jnp.zeros((count, 1), jnp.int32)
    for j in range(planes):
        plane = lax.rem(here + steps[j] + planes, planes)
        sender = jnp.where(row // rows == j, plane, sender)
    lane = lax.broadcasted_iota(jnp.int32, (1, slots), 1)
    cls = (here * owners + lane // group).astype(F32)
    member = facts[:, 2:3] == cls
    for k in range(1, top):
        member = member | (facts[:, 2 + k : 3 + k] == cls)
    one, other = (lax.broadcasted_iota(jnp.int32, (count, count), i) for i in range(2))
    earlier = (one > other) & (one // rows == other // rows)
    before = jnp.dot(
        earlier.astype(F32).astype(BF16),
        member.astype(F32).astype(BF16),
        preferred_element_type=F32,
    )
    slot = (lane // planes) % SLOTS
    pick = member & (before == slot.astype(F32)) & (lane % planes == sender)
    pick = pick.astype(F32).T.astype(BF16)
    width = 3
    for t in range(0, tiles, width):
        lanes = slice(t * LANES, (t + width) * LANES)
        got = jnp.dot(pick, column_ref[:, lanes], preferred_element_type=F32).astype(BF16)
        for i in range(width):
            for c in range(owners):
                send_ref[c, (t + i) * group : (t + i + 1) * group] = got[
                    c * group : (c + 1) * group, tile_of(i)
                ]


def shift_kernel(from_ref, out_ref, half_ref, rot_ref):
    count, pixels = rot_ref.shape
    rots = from_ref.shape[0]
    half_count, half_rots = count // 2, rots // 2
    to = lax.broadcasted_iota(jnp.int32, (count, rots), 0)
    place = jnp.where(to < half_count, to, to - half_count + half_rots)
    real = to % half_count < half_rots
    place = jnp.where(place < rots, place, 0)
    own_first = lax.axis_index("dp") * half_rots
    place = jnp.where(place + own_first < rots, place + own_first, place + own_first - rots)
    chosen = (place == lax.broadcasted_iota(jnp.int32, (count, rots), 1)) & real
    rot_ref[...] = jnp.dot(
        chosen.astype(F32).astype(BF16), from_ref[...], preferred_element_type=F32
    )
    tiles = pixels // LANES
    side = LANES // 2
    groups = len(COL_SHIFTS) * count
    lane = lane_row()
    low = lane < side
    column = lane % side
    square = jnp.zeros((count, LANES), F32)
    for q in range(tiles):
        tile = fold_tile(lambda t: rot_ref[:, tile_of(t)], q, tiles, low)
        square = square + tile * tile
        right = jnp.where(
            column == 0, pltpu.roll(tile, LANES - side + 1, 1), pltpu.roll(tile, 1, 1)
        )
        left = jnp.where(
            column == side - 1, pltpu.roll(tile, side - 1, 1), pltpu.roll(tile, LANES - 1, 1)
        )
        for i, moved in enumerate((tile, right, left)):
            plain = moved.astype(BF16)
            for j, shift in enumerate(ROW_SHIFTS):
                to = q + shift
                value = plain
                if not 0 <= to < tiles:
                    to = to % tiles
                    value = pltpu.roll(moved, side, 1).astype(BF16)
                at = j * groups + i * count
                out_ref[at : at + count, tile_of(to)] = value
    half = 0.5 * jnp.sum(square, axis=1, keepdims=True)
    half_ref[...] = jnp.broadcast_to(half, half_ref.shape)


def score_kernel(recv_ref, shifted_ref, half_ref, x_ref, s_ref, tile_ref, *, pad):
    owners, depth, _ = recv_ref.shape
    tiles = x_ref.shape[1] // LANES - 2
    group = depth // (tiles + 1)
    slots = owners * group
    groups = s_ref.shape[0]
    count = half_ref.shape[0]
    for c in range(owners):
        for t in range(tiles):
            x_ref[c * group : (c + 1) * group, tile_of(t + 1)] = recv_ref[
                c, t * group : (t + 1) * group
            ]
    half_turn = LANES // 2
    x_ref[:, tile_of(0)] = pltpu.roll(x_ref[:, tile_of(tiles)].astype(F32), half_turn, 1).astype(
        BF16
    )
    x_ref[:, tile_of(tiles + 1)] = pltpu.roll(x_ref[:, tile_of(1)].astype(F32), half_turn, 1).astype(
        BF16
    )
    facts = recv_ref[:, tiles * group :, :].reshape(slots, LANES)
    choose = (
        lax.broadcasted_iota(jnp.int32, (16, LANES), 0)
        == lax.broadcasted_iota(jnp.int32, (16, LANES), 1)
    ).astype(F32).astype(BF16)
    turned = lax.dot_general(
        choose, facts, (((1,), (1,)), ((), ())), preferred_element_type=F32
    )
    noise, number = turned[0:1], turned[1:2]
    products = lax.dot_general(
        shifted_ref[...],
        x_ref[:, LANES : (tiles + 1) * LANES],
        (((1,), (1,)), ((), ())),
        preferred_element_type=F32,
    )
    half = half_ref[:, 0:1]
    row = lax.broadcasted_iota(jnp.int32, half.shape, 0)
    half = jnp.where(row % (count // 2) >= count // 2 - pad, FAR, half)
    half = jnp.concatenate([half] * len(COL_SHIFTS), axis=0)
    peak = None
    for i in range(len(ROW_SHIFTS)):
        scores = noise * (products[i * groups : (i + 1) * groups] - half)
        s_ref[:, i * slots : (i + 1) * slots] = scores
        top = jnp.max(scores, axis=0, keepdims=True)
        peak = top if peak is None else jnp.maximum(peak, top)
    total = jnp.zeros_like(peak)
    for i in range(len(ROW_SHIFTS)):
        scores = s_ref[:, i * slots : (i + 1) * slots]
        total = total + jnp.sum(jnp.exp(scores - peak), axis=0, keepdims=True)
    parts = slots // LANES
    for i, value in enumerate((peak, total, number)):
        for h in range(parts):
            tile_ref[i * parts + h : i * parts + h + 1] = value[:, tile_of(h)]
    tile_ref[3 * parts :] = jnp.zeros_like(tile_ref[3 * parts :])


def sum_kernel(s_ref, x_ref, mine_ref, all_ref, keep_ref, give_ref, w_ref, y_ref):
    groups = s_ref.shape[0]
    slots = x_ref.shape[0]
    pixels = x_ref.shape[1] - 2 * LANES
    owners = all_ref.shape[0] // 8
    count = groups // len(COL_SHIFTS)
    half_count = count // 2
    parts = slots // LANES
    side = LANES // 2
    lane = lane_row()
    second = (lane // PLANES) % SLOTS == 1

    def partner(row):
        return jnp.where(second, pltpu.roll(row, PLANES, 1), pltpu.roll(row, LANES - PLANES, 1))

    peaks, scales = [], []
    for h in range(parts):
        own = mine_ref[2 * parts + h : 2 * parts + h + 1]
        across = partner(own)
        shown = [all_ref[pl.ds(i * parts + h, owners, stride=8), :] for i in range(3)]
        found = []
        for slot in range(SLOTS):
            target = jnp.where(second == (slot == 1), own, across)
            same = shown[2] == target
            peak = jnp.max(jnp.where(same, shown[0], -jnp.inf), axis=0, keepdims=True)
            peak = jnp.maximum(peak, partner(peak))
            part = shown[1] * jnp.exp(jnp.minimum(shown[0] - peak, 0.0))
            total = jnp.sum(jnp.where(same, part, 0.0), axis=0, keepdims=True)
            found.append((peak, total + partner(total)))
        peaks.append(jnp.where(second, found[1][0], found[0][0]))
        total = jnp.where(second, found[1][1], found[0][1])
        scales.append(jnp.where(own > 0, 1.0 / total, 0.0))
    peak = jnp.concatenate(peaks, axis=1)
    scale = jnp.concatenate(scales, axis=1)
    row_total = jnp.zeros((groups, 1), F32)
    for i in range(len(ROW_SHIFTS)):
        part = slice(i * slots, (i + 1) * slots)
        weights = (jnp.exp(jnp.minimum(s_ref[:, part] - peak, 0.0)) * scale).astype(BF16)
        w_ref[:, part] = weights
        row_total = row_total + jnp.sum(weights.astype(F32), axis=1, keepdims=True)
    class_total = sum(row_total[i * count : (i + 1) * count] for i in range(len(COL_SHIFTS)))
    keep_ref[:, pixels:] = jnp.broadcast_to(class_total[:half_count], (half_count, LANES))
    give_ref[:, pixels:] = jnp.broadcast_to(class_total[half_count:], (half_count, LANES))
    width = y_ref.shape[1]
    column = lane % side
    for first in range(0, pixels, width):
        y_ref[...] = sum(
            jnp.dot(
                w_ref[:, i * slots : (i + 1) * slots],
                x_ref[:, (1 + shift) * LANES + first : (1 + shift) * LANES + first + width],
                preferred_element_type=F32,
            )
            for i, shift in enumerate(ROW_SHIFTS)
        )
        for t in range(width // LANES):
            plain = y_ref[:count, tile_of(t)]
            right = y_ref[count : 2 * count, tile_of(t)]
            left = y_ref[2 * count :, tile_of(t)]
            back = jnp.where(
                column == side - 1,
                pltpu.roll(right, side - 1, 1),
                pltpu.roll(right, LANES - 1, 1),
            )
            forth = jnp.where(
                column == 0, pltpu.roll(left, LANES - side + 1, 1), pltpu.roll(left, 1, 1)
            )
            moved = plain + back + forth
            at = slice(first + t * LANES, first + (t + 1) * LANES)
            keep_ref[:, at] = moved[:half_count]
            give_ref[:, at] = moved[half_count:]


def finish_kernel(keep_ref, other_ref, sums_ref, totals_ref):
    rots = totals_ref.shape[1]
    tiles = sums_ref.shape[0] // rots
    low = lane_row() < LANES // 2

    def load(t):
        return keep_ref[:rots, tile_of(t)] + other_ref[:rots, tile_of(t)]

    for t in range(tiles):
        sums_ref[pl.ds(t, rots, stride=tiles), :] = unfold_tile(load, t, tiles, low)
    total = load(tiles)
    here = lax.broadcasted_iota(jnp.int32, (rots, LANES), 0) == lax.broadcasted_iota(
        jnp.int32, (rots, LANES), 1
    )
    totals_ref[...] = jnp.sum(jnp.where(here, total, 0.0), axis=0, keepdims=True)[:, :rots]


def call(kernel, out_shape, count, limit, scratch=(), flops=0, moved=0, space=pltpu.VMEM):
    in_vmem = pl.BlockSpec(memory_space=pltpu.VMEM)
    return pl.pallas_call(
        kernel,
        out_shape=out_shape,
        in_specs=[pl.BlockSpec(memory_space=space)] * count,
        out_specs=jax.tree.map(lambda _: in_vmem, out_shape),
        scratch_shapes=list(scratch),
        cost_estimate=pl.CostEstimate(flops=flops, bytes_accessed=moved, transcendentals=0),
        compiler_params=pltpu.CompilerParams(vmem_limit_bytes=limit * MIB),
    )


def on_device(images, references, candidates, inv_noise):
    rows, top = candidates.shape
    cls_dev, rots, pixels = references.shape
    planes, owners = lax.axis_size("z"), lax.axis_size("xy")
    side = math.isqrt(pixels)
    tiles = pixels // LANES
    group = SLOTS * planes
    slots = owners * group
    assert cls_dev == 1 and planes == PLANES and LANES == 2 * side and rows == group
    shape = jax.ShapeDtypeStruct
    exchange = functools.partial(lax.all_to_all, split_axis=0, concat_axis=0, tiled=True)

    packed = call(
        pack_kernel,
        shape(((tiles + 1) * rows, LANES), BF16),
        3,
        4,
        moved=MIB // 4,
    )(candidates.T, inv_noise[None, :], images)
    up = [(i, (i + 1) % planes) for i in range(planes)]
    down = [((i + 1) % planes, i) for i in range(planes)]
    rising = falling = packed
    column, steps = [packed], [0]
    for step in range(1, planes // 2):
        rising = lax.ppermute(rising, "z", up)
        falling = lax.ppermute(falling, "z", down)
        column += [rising, falling]
        steps += [-step, step]
    cut = (tiles + 1) // 2 * rows
    column += [
        lax.ppermute(rising[:cut], "z", up),
        lax.ppermute(falling[cut:], "z", down),
    ]
    steps += [planes // 2] * 2

    half_rots = rots // 2
    half_count = -(-half_rots // 8) * 8
    pad = half_count - half_rots
    count = 2 * half_count
    groups = len(COL_SHIFTS) * count
    shifted, half_norm = call(
        shift_kernel,
        (shape((len(ROW_SHIFTS) * groups, pixels), BF16), shape((count, LANES), F32)),
        1,
        6,
        [pltpu.VMEM((count, pixels), F32)],
        moved=12 * MIB,
    )(references[0])
    column, shifted, half_norm = lax.optimization_barrier((column, shifted, half_norm))
    picked = call(
        functools.partial(pick_kernel, steps=steps, top=top),
        shape((owners, (tiles + 1) * group, LANES), BF16),
        len(column),
        6,
        [pltpu.VMEM((planes * rows, (tiles + 1) * LANES), BF16)],
        moved=3 * MIB,
    )(*column)
    received = exchange(picked, "xy")
    work = 2 * len(ROW_SHIFTS) * groups * slots * pixels
    x, scores, tile = call(
        functools.partial(score_kernel, pad=pad),
        (
            shape((slots, pixels + 2 * LANES), BF16),
            shape((groups, len(ROW_SHIFTS) * slots), F32),
            shape((8, LANES), F32),
        ),
        3,
        8,
        flops=work,
        moved=10 * MIB,
    )(received, shifted, half_norm)
    by_plane = exchange(jnp.broadcast_to(tile[None], (planes, 8, LANES)), "z")
    by_plane = by_plane.reshape(1, planes * 8, LANES)
    everyone = exchange(jnp.broadcast_to(by_plane, (owners, planes * 8, LANES)), "xy")
    half_shape = shape((half_count, pixels + LANES), F32)
    keep, give = call(
        sum_kernel,
        (half_shape, half_shape),
        4,
        8,
        [
            pltpu.VMEM((groups, len(ROW_SHIFTS) * slots), BF16),
            pltpu.VMEM((groups, 4 * LANES), F32),
        ],
        flops=work,
        moved=5 * MIB,
    )(scores, x, tile, everyone.reshape(owners * planes * 8, LANES))
    other = lax.ppermute(give, "dp", [(0, 1), (1, 0)])
    sums, totals = call(
        finish_kernel,
        (shape((half_rots * tiles, LANES), F32), shape((1, half_rots), F32)),
        2,
        8,
        moved=2 * MIB,
    )(keep, other)
    return sums.reshape(1, half_rots, pixels), totals


def solution(mesh):
    split = (PLANES, mesh.shape["cls"] // PLANES, mesh.shape["dp"])
    cube = Mesh(mesh.devices.reshape(split), ("z", "xy", "dp"))
    every = ("z", "xy", "dp")
    by_class = ("z", "xy")
    return jax.shard_map(
        on_device,
        mesh=cube,
        in_specs=(P(every, None), P(by_class, None, None), P(every, None), P(every)),
        out_specs=(P(by_class, "dp", None), P(by_class, "dp")),
        check_vma=False,
    )
```

```python
import functools
import math

import jax
import jax.numpy as jnp
from jax import lax
from jax.experimental import pallas as pl
from jax.experimental.pallas import tpu as pltpu
from jax.sharding import Mesh
from jax.sharding import PartitionSpec as P

LANES = 128
SLOTS = 2
PLANES = 8
FAR = 1e30
ROW_SHIFTS = (0, 1, -1)
COL_SHIFTS = (0, 1, -1)
MIB = 1024 * 1024
F32, BF16 = jnp.float32, jnp.bfloat16


def tile_of(t):
    return slice(t * LANES, (t + 1) * LANES)


def lane_row():
    return lax.broadcasted_iota(jnp.int32, (1, LANES), 1)


def fold_tile(load, q, tiles, low):
    first, second = load(q // 2), load(tiles // 2 + q // 2)
    half = LANES // 2
    if q % 2 == 0:
        return jnp.where(low, first, pltpu.roll(second, half, 1))
    return jnp.where(low, pltpu.roll(first, half, 1), second)


def unfold_tile(load, t, tiles, low):
    half = LANES // 2
    if t < tiles // 2:
        return jnp.where(low, load(2 * t), pltpu.roll(load(2 * t + 1), half, 1))
    first = 2 * t - tiles
    return jnp.where(low, pltpu.roll(load(first), half, 1), load(first + 1))


def pack_kernel(cand_ref, noise_ref, img_ref, send_ref, late_ref):
    top, rows = cand_ref.shape
    early = send_ref.shape[0] // rows
    tiles = img_ref.shape[1] // LANES
    low = lane_row() < LANES // 2
    row_id = lax.broadcasted_iota(jnp.int32, (rows, LANES), 0)
    lane_id = lax.broadcasted_iota(jnp.int32, (rows, LANES), 1)
    diagonal = lax.broadcasted_iota(jnp.int32, (rows, rows), 0) == lax.broadcasted_iota(
        jnp.int32, (rows, rows), 1
    )
    noise = jnp.sum(
        jnp.where(diagonal, noise_ref[...].astype(F32), 0.0), axis=1, keepdims=True
    )
    place = lax.broadcasted_iota(jnp.int32, (top, LANES), 1) == (
        lax.broadcasted_iota(jnp.int32, (top, LANES), 0) + 2
    )
    facts = lax.dot_general(
        cand_ref[...].astype(F32).astype(BF16),
        place.astype(F32).astype(BF16),
        (((0,), (0,)), ((), ())),
        preferred_element_type=F32,
    )
    facts = jnp.where(lane_id == 0, noise, facts)
    facts = jnp.where(lane_id == 1, (row_id + 1).astype(F32), facts)
    late_ref[(tiles - early) * rows :] = facts.astype(BF16)
    for q in range(tiles):
        tile = fold_tile(lambda t: img_ref[:, tile_of(t)].astype(F32), q, tiles, low)
        to_ref, at = (send_ref, q) if q < early else (late_ref, q - early)
        to_ref[at * rows : (at + 1) * rows] = tile.astype(BF16)


def pick_kernel(*refs, steps, top):
    planes = len(steps)
    recv_refs, send_ref, column_ref = refs[: 2 * planes], refs[-2], refs[-1]
    owners, depth, _ = send_ref.shape
    rows = column_ref.shape[0] // planes
    tiles = column_ref.shape[1] // LANES
    group = depth // tiles
    slots = owners * group
    cut = recv_refs[0].shape[0] // rows
    for j in range(planes):
        for t in range(tiles):
            from_ref, at = recv_refs[2 * j], t
            if t >= cut:
                from_ref, at = recv_refs[2 * j + 1], t - cut
            column_ref[j * rows : (j + 1) * rows, tile_of(t)] = from_ref[
                at * rows : (at + 1) * rows
            ]
    count = planes * rows
    facts = column_ref[:, tile_of(tiles - 1)].astype(F32)
    here = lax.axis_index("z")
    row = lax.broadcasted_iota(jnp.int32, (count, 1), 0)
    sender = jnp.zeros((count, 1), jnp.int32)
    for j in range(planes):
        plane = lax.rem(here + steps[j] + planes, planes)
        sender = jnp.where(row // rows == j, plane, sender)
    lane = lax.broadcasted_iota(jnp.int32, (1, slots), 1)
    cls = (here * owners + lane // group).astype(F32)
    member = facts[:, 2:3] == cls
    for k in range(1, top):
        member = member | (facts[:, 2 + k : 3 + k] == cls)
    one, other = (lax.broadcasted_iota(jnp.int32, (count, count), i) for i in range(2))
    earlier = (one > other) & (one // rows == other // rows)
    before = jnp.dot(
        earlier.astype(F32).astype(BF16),
        member.astype(F32).astype(BF16),
        preferred_element_type=F32,
    )
    slot = (lane // planes) % SLOTS
    pick = member & (before == slot.astype(F32)) & (lane % planes == sender)
    pick = pick.astype(F32).T.astype(BF16)
    width = 3
    for t in range(0, tiles, width):
        lanes = slice(t * LANES, (t + width) * LANES)
        got = jnp.dot(pick, column_ref[:, lanes], preferred_element_type=F32).astype(BF16)
        for i in range(width):
            for c in range(owners):
                send_ref[c, (t + i) * group : (t + i + 1) * group] = got[
                    c * group : (c + 1) * group, tile_of(i)
                ]


def shift_kernel(from_ref, out_ref, half_ref, rot_ref):
    count, pixels = rot_ref.shape
    rots = from_ref.shape[0]
    half_count, half_rots = count // 2, rots // 2
    to = lax.broadcasted_iota(jnp.int32, (count, rots), 0)
    place = jnp.where(to < half_count, to, to - half_count + half_rots)
    real = to % half_count < half_rots
    own_first = lax.axis_index("dp") * half_rots
    place = jnp.where(place + own_first < rots, place + own_first, place + own_first - rots)
    chosen = (place == lax.broadcasted_iota(jnp.int32, (count, rots), 1)) & real
    picked = jnp.dot(chosen.astype(F32).astype(BF16), from_ref[...], preferred_element_type=F32)
    half = 0.5 * jnp.sum(picked * picked, axis=1, keepdims=True)
    half_ref[...] = jnp.broadcast_to(half, half_ref.shape)
    rot_ref[...] = picked.astype(BF16)
    tiles = pixels // LANES
    side = LANES // 2
    groups = len(COL_SHIFTS) * count
    source = lax.broadcasted_iota(jnp.int32, (2 * LANES, LANES), 0)
    lane = lax.broadcasted_iota(jnp.int32, (2 * LANES, LANES), 1)
    moves = []
    for parity in range(2):
        for shift in COL_SHIFTS:
            col = (lane - shift + side) % side
            home = (lane // side) * LANES + parity * side + col
            moves.append((source == home).astype(F32).astype(BF16))
    moves = jnp.concatenate(moves, axis=1)
    turn = ((lane[:LANES] + side) % LANES == source[:LANES]).astype(F32).astype(BF16)
    for h in range(tiles // 2):
        pair = jnp.concatenate(
            [rot_ref[:, tile_of(h)], rot_ref[:, tile_of(tiles // 2 + h)]], axis=1
        )
        moved = jnp.dot(pair, moves, preferred_element_type=F32).astype(BF16)
        for parity in range(2):
            for i in range(len(COL_SHIFTS)):
                plain = moved[:, tile_of(parity * len(COL_SHIFTS) + i)]
                for j, shift in enumerate(ROW_SHIFTS):
                    at = 2 * h + parity + shift
                    value = plain
                    if not 0 <= at < tiles:
                        at = at % tiles
                        value = jnp.dot(plain, turn, preferred_element_type=F32).astype(BF16)
                    first = j * groups + i * count
                    out_ref[first : first + count, tile_of(at)] = value


def score_kernel(recv_ref, shifted_ref, half_ref, x_ref, s_ref, tile_ref, *, pad):
    owners, depth, _ = recv_ref.shape
    tiles = x_ref.shape[1] // LANES - 2
    group = depth // (tiles + 1)
    slots = owners * group
    groups = s_ref.shape[0]
    count = half_ref.shape[0]
    for c in range(owners):
        for t in range(tiles):
            x_ref[c * group : (c + 1) * group, tile_of(t + 1)] = recv_ref[
                c, t * group : (t + 1) * group
            ]
    half_turn = LANES // 2
    x_ref[:, tile_of(0)] = pltpu.roll(x_ref[:, tile_of(tiles)].astype(F32), half_turn, 1).astype(
        BF16
    )
    x_ref[:, tile_of(tiles + 1)] = pltpu.roll(x_ref[:, tile_of(1)].astype(F32), half_turn, 1).astype(
        BF16
    )
    facts = recv_ref[:, tiles * group :, :].reshape(slots, LANES)
    choose = (
        lax.broadcasted_iota(jnp.int32, (16, LANES), 0)
        == lax.broadcasted_iota(jnp.int32, (16, LANES), 1)
    ).astype(F32).astype(BF16)
    turned = lax.dot_general(
        choose, facts, (((1,), (1,)), ((), ())), preferred_element_type=F32
    )
    noise, number = turned[0:1], turned[1:2]
    products = lax.dot_general(
        shifted_ref[...],
        x_ref[:, LANES : (tiles + 1) * LANES],
        (((1,), (1,)), ((), ())),
        preferred_element_type=F32,
    )
    half = half_ref[:, 0:1]
    row = lax.broadcasted_iota(jnp.int32, half.shape, 0)
    half = jnp.where(row % (count // 2) >= count // 2 - pad, FAR, half)
    half = jnp.concatenate([half] * len(COL_SHIFTS), axis=0)
    peak = None
    for i in range(len(ROW_SHIFTS)):
        scores = noise * (products[i * groups : (i + 1) * groups] - half)
        s_ref[:, i * slots : (i + 1) * slots] = scores
        top = jnp.max(scores, axis=0, keepdims=True)
        peak = top if peak is None else jnp.maximum(peak, top)
    total = jnp.zeros_like(peak)
    for i in range(len(ROW_SHIFTS)):
        scores = s_ref[:, i * slots : (i + 1) * slots]
        total = total + jnp.sum(jnp.exp(scores - peak), axis=0, keepdims=True)
    parts = slots // LANES
    for i, value in enumerate((peak, total, number)):
        for h in range(parts):
            tile_ref[i * parts + h : i * parts + h + 1] = value[:, tile_of(h)]
    tile_ref[3 * parts :] = jnp.zeros_like(tile_ref[3 * parts :])


def sum_kernel(s_ref, x_ref, mine_ref, all_ref, keep_ref, give_ref, w_ref, y_ref):
    groups = s_ref.shape[0]
    slots = x_ref.shape[0]
    pixels = x_ref.shape[1] - 2 * LANES
    owners = all_ref.shape[0] // 8
    count = groups // len(COL_SHIFTS)
    half_count = count // 2
    parts = slots // LANES
    side = LANES // 2
    lane = lane_row()
    second = (lane // PLANES) % SLOTS == 1

    def partner(row):
        return jnp.where(second, pltpu.roll(row, PLANES, 1), pltpu.roll(row, LANES - PLANES, 1))

    peaks, scales = [], []
    for h in range(parts):
        own = mine_ref[2 * parts + h : 2 * parts + h + 1]
        across = partner(own)
        shown = [all_ref[pl.ds(i * parts + h, owners, stride=8), :] for i in range(3)]
        found = []
        for slot in range(SLOTS):
            target = jnp.where(second == (slot == 1), own, across)
            same = shown[2] == target
            peak = jnp.max(jnp.where(same, shown[0], -jnp.inf), axis=0, keepdims=True)
            peak = jnp.maximum(peak, partner(peak))
            part = shown[1] * jnp.exp(jnp.minimum(shown[0] - peak, 0.0))
            total = jnp.sum(jnp.where(same, part, 0.0), axis=0, keepdims=True)
            found.append((peak, total + partner(total)))
        peaks.append(jnp.where(second, found[1][0], found[0][0]))
        total = jnp.where(second, found[1][1], found[0][1])
        scales.append(jnp.where(own > 0, 1.0 / total, 0.0))
    peak = jnp.concatenate(peaks, axis=1)
    scale = jnp.concatenate(scales, axis=1)
    row_total = jnp.zeros((groups, 1), F32)
    for i in range(len(ROW_SHIFTS)):
        part = slice(i * slots, (i + 1) * slots)
        weights = (jnp.exp(jnp.minimum(s_ref[:, part] - peak, 0.0)) * scale).astype(BF16)
        w_ref[:, part] = weights
        row_total = row_total + jnp.sum(weights.astype(F32), axis=1, keepdims=True)
    class_total = sum(row_total[i * count : (i + 1) * count] for i in range(len(COL_SHIFTS)))
    keep_ref[:, pixels:] = jnp.broadcast_to(class_total[:half_count], (half_count, LANES))
    give_ref[:, pixels:] = jnp.broadcast_to(class_total[half_count:], (half_count, LANES))
    width = y_ref.shape[1]
    column = lane % side
    for first in range(0, pixels, width):
        y_ref[...] = sum(
            jnp.dot(
                w_ref[:, i * slots : (i + 1) * slots],
                x_ref[:, (1 + shift) * LANES + first : (1 + shift) * LANES + first + width],
                preferred_element_type=F32,
            )
            for i, shift in enumerate(ROW_SHIFTS)
        )
        for t in range(width // LANES):
            plain = y_ref[:count, tile_of(t)]
            right = y_ref[count : 2 * count, tile_of(t)]
            left = y_ref[2 * count :, tile_of(t)]
            back = jnp.where(
                column == side - 1,
                pltpu.roll(right, side - 1, 1),
                pltpu.roll(right, LANES - 1, 1),
            )
            forth = jnp.where(
                column == 0, pltpu.roll(left, LANES - side + 1, 1), pltpu.roll(left, 1, 1)
            )
            moved = plain + back + forth
            at = slice(first + t * LANES, first + (t + 1) * LANES)
            keep_ref[:, at] = moved[:half_count]
            give_ref[:, at] = moved[half_count:]


def finish_kernel(keep_ref, other_ref, sums_ref, totals_ref):
    rots = totals_ref.shape[1]
    tiles = sums_ref.shape[0] // rots
    low = lane_row() < LANES // 2

    def load(t):
        return keep_ref[:rots, tile_of(t)] + other_ref[:rots, tile_of(t)]

    for t in range(tiles):
        sums_ref[pl.ds(t, rots, stride=tiles), :] = unfold_tile(load, t, tiles, low)
    total = load(tiles)
    here = lax.broadcasted_iota(jnp.int32, (rots, LANES), 0) == lax.broadcasted_iota(
        jnp.int32, (rots, LANES), 1
    )
    totals_ref[...] = jnp.sum(jnp.where(here, total, 0.0), axis=0, keepdims=True)[:, :rots]


def call(kernel, out_shape, count, limit, scratch=(), flops=0, moved=0, space=pltpu.VMEM):
    in_vmem = pl.BlockSpec(memory_space=pltpu.VMEM)
    return pl.pallas_call(
        kernel,
        out_shape=out_shape,
        in_specs=[pl.BlockSpec(memory_space=space)] * count,
        out_specs=jax.tree.map(lambda _: in_vmem, out_shape),
        scratch_shapes=list(scratch),
        cost_estimate=pl.CostEstimate(flops=flops, bytes_accessed=moved, transcendentals=0),
        compiler_params=pltpu.CompilerParams(vmem_limit_bytes=limit * MIB),
    )


def on_device(images, references, candidates, inv_noise):
    rows, top = candidates.shape
    cls_dev, rots, pixels = references.shape
    planes, owners = lax.axis_size("z"), lax.axis_size("xy")
    side = math.isqrt(pixels)
    tiles = pixels // LANES
    group = SLOTS * planes
    slots = owners * group
    assert cls_dev == 1 and planes == PLANES and LANES == 2 * side and rows == group
    shape = jax.ShapeDtypeStruct
    exchange = functools.partial(lax.all_to_all, split_axis=0, concat_axis=0, tiled=True)

    cut = (tiles + 1) // 2
    packed = call(
        pack_kernel,
        (shape((cut * rows, LANES), BF16), shape(((tiles + 1 - cut) * rows, LANES), BF16)),
        3,
        56,
        moved=MIB // 4,
    )(candidates.T, inv_noise[None, :], images)
    up = [(i, (i + 1) % planes) for i in range(planes)]
    down = [((i + 1) % planes, i) for i in range(planes)]

    def move(parts, way):
        return [lax.ppermute(part, "z", way) for part in parts]

    rising, falling = move(packed, up), move(packed, down)
    half_rots = rots // 2
    half_count = -(-half_rots // 8) * 8
    pad = half_count - half_rots
    count = 2 * half_count
    groups = len(COL_SHIFTS) * count
    shifted, half_norm = call(
        shift_kernel,
        (shape((len(ROW_SHIFTS) * groups, pixels), BF16), shape((count, LANES), F32)),
        1,
        6,
        [pltpu.VMEM((count, pixels), BF16)],
        moved=12 * MIB,
    )(references[0])
    rising, falling, shifted, half_norm = lax.optimization_barrier(
        (rising, falling, shifted, half_norm)
    )
    column, steps = [*packed, *rising, *falling], [0, -1, 1]
    for step in range(2, planes // 2):
        rising, falling = move(rising, up), move(falling, down)
        column += [*rising, *falling]
        steps += [-step, step]
    column += [*move(rising[:1], up), *move(falling[1:], down)]
    steps.append(planes // 2)
    picked = call(
        functools.partial(pick_kernel, steps=steps, top=top),
        shape((owners, (tiles + 1) * group, LANES), BF16),
        len(column),
        6,
        [pltpu.VMEM((planes * rows, (tiles + 1) * LANES), BF16)],
        moved=3 * MIB,
    )(*column)
    received = exchange(picked, "xy")
    work = 2 * len(ROW_SHIFTS) * groups * slots * pixels
    x, scores, tile = call(
        functools.partial(score_kernel, pad=pad),
        (
            shape((slots, pixels + 2 * LANES), BF16),
            shape((groups, len(ROW_SHIFTS) * slots), F32),
            shape((8, LANES), F32),
        ),
        3,
        8,
        flops=work,
        moved=10 * MIB,
    )(received, shifted, half_norm)
    by_plane = exchange(jnp.broadcast_to(tile[None], (planes, 8, LANES)), "z")
    by_plane = by_plane.reshape(1, planes * 8, LANES)
    everyone = exchange(jnp.broadcast_to(by_plane, (owners, planes * 8, LANES)), "xy")
    half_shape = shape((half_count, pixels + LANES), F32)
    keep, give = call(
        sum_kernel,
        (half_shape, half_shape),
        4,
        8,
        [
            pltpu.VMEM((groups, len(ROW_SHIFTS) * slots), BF16),
            pltpu.VMEM((groups, 4 * LANES), F32),
        ],
        flops=work,
        moved=5 * MIB,
    )(scores, x, tile, everyone.reshape(owners * planes * 8, LANES))
    other = lax.ppermute(give, "dp", [(0, 1), (1, 0)])
    sums, totals = call(
        finish_kernel,
        (shape((half_rots * tiles, LANES), F32), shape((1, half_rots), F32)),
        2,
        8,
        moved=2 * MIB,
    )(keep, other)
    return sums.reshape(1, half_rots, pixels), totals


def solution(mesh):
    split = (PLANES, mesh.shape["cls"] // PLANES, mesh.shape["dp"])
    cube = Mesh(mesh.devices.reshape(split), ("z", "xy", "dp"))
    every = ("z", "xy", "dp")
    by_class = ("z", "xy")
    return jax.shard_map(
        on_device,
        mesh=cube,
        in_specs=(P(every, None), P(by_class, None, None), P(every, None), P(every)),
        out_specs=(P(by_class, "dp", None), P(by_class, "dp")),
        check_vma=False,
    )
```

```python
import functools
import math

import jax
import jax.numpy as jnp
from jax import lax
from jax.experimental import pallas as pl
from jax.experimental.pallas import tpu as pltpu
from jax.sharding import Mesh
from jax.sharding import PartitionSpec as P

LANES = 128
SLOTS = 2
PLANES = 8
FAR = 1e30
ROW_SHIFTS = (0, 1, -1)
COL_SHIFTS = (0, 1, -1)
MIB = 1024 * 1024
F32, BF16 = jnp.float32, jnp.bfloat16


def tile_of(t):
    return slice(t * LANES, (t + 1) * LANES)


def lane_row():
    return lax.broadcasted_iota(jnp.int32, (1, LANES), 1)


def fold_tile(load, q, tiles, low):
    first, second = load(q // 2), load(tiles // 2 + q // 2)
    half = LANES // 2
    if q % 2 == 0:
        return jnp.where(low, first, pltpu.roll(second, half, 1))
    return jnp.where(low, pltpu.roll(first, half, 1), second)


def unfold_tile(load, t, tiles, low):
    half = LANES // 2
    if t < tiles // 2:
        return jnp.where(low, load(2 * t), pltpu.roll(load(2 * t + 1), half, 1))
    first = 2 * t - tiles
    return jnp.where(low, pltpu.roll(load(first), half, 1), load(first + 1))


def pack_kernel(cand_ref, noise_ref, img_ref, send_ref):
    top, rows = cand_ref.shape
    tiles = img_ref.shape[1] // LANES
    low = lane_row() < LANES // 2
    row_id = lax.broadcasted_iota(jnp.int32, (rows, LANES), 0)
    lane_id = lax.broadcasted_iota(jnp.int32, (rows, LANES), 1)
    diagonal = lax.broadcasted_iota(jnp.int32, (rows, rows), 0) == lax.broadcasted_iota(
        jnp.int32, (rows, rows), 1
    )
    noise = jnp.sum(
        jnp.where(diagonal, noise_ref[...].astype(F32), 0.0), axis=1, keepdims=True
    )
    place = lax.broadcasted_iota(jnp.int32, (top, LANES), 1) == (
        lax.broadcasted_iota(jnp.int32, (top, LANES), 0) + 2
    )
    facts = lax.dot_general(
        cand_ref[...].astype(F32).astype(BF16),
        place.astype(F32).astype(BF16),
        (((0,), (0,)), ((), ())),
        preferred_element_type=F32,
    )
    facts = jnp.where(lane_id == 0, noise, facts)
    facts = jnp.where(lane_id == 1, (row_id + 1).astype(F32), facts)
    send_ref[tiles * rows :] = facts.astype(BF16)
    for q in range(tiles):
        tile = fold_tile(lambda t: img_ref[:, tile_of(t)].astype(F32), q, tiles, low)
        send_ref[q * rows : (q + 1) * rows] = tile.astype(BF16)


def pick_kernel(*refs, steps, top):
    planes = len(steps) - 1
    recv_refs, send_ref, column_ref = refs[: len(steps)], refs[-2], refs[-1]
    owners, depth, _ = send_ref.shape
    rows = column_ref.shape[0] // planes
    tiles = column_ref.shape[1] // LANES
    group = depth // tiles
    slots = owners * group
    cut = recv_refs[-2].shape[0] // rows
    for j in range(planes):
        for t in range(tiles):
            from_ref, at = recv_refs[j], t
            if j == planes - 1 and t >= cut:
                from_ref, at = recv_refs[j + 1], t - cut
            column_ref[j * rows : (j + 1) * rows, tile_of(t)] = from_ref[
                at * rows : (at + 1) * rows
            ]
    count = planes * rows
    facts = column_ref[:, tile_of(tiles - 1)].astype(F32)
    here = lax.axis_index("z")
    row = lax.broadcasted_iota(jnp.int32, (count, 1), 0)
    sender = jnp.zeros((count, 1), jnp.int32)
    for j in range(planes):
        plane = lax.rem(here + steps[j] + planes, planes)
        sender = jnp.where(row // rows == j, plane, sender)
    lane = lax.broadcasted_iota(jnp.int32, (1, slots), 1)
    cls = (here * owners + lane // group).astype(F32)
    member = facts[:, 2:3] == cls
    for k in range(1, top):
        member = member | (facts[:, 2 + k : 3 + k] == cls)
    one, other = (lax.broadcasted_iota(jnp.int32, (count, count), i) for i in range(2))
    earlier = (one > other) & (one // rows == other // rows)
    before = jnp.dot(
        earlier.astype(F32).astype(BF16),
        member.astype(F32).astype(BF16),
        preferred_element_type=F32,
    )
    slot = (lane // planes) % SLOTS
    pick = member & (before == slot.astype(F32)) & (lane % planes == sender)
    pick = pick.astype(F32).T.astype(BF16)
    width = 3
    for t in range(0, tiles, width):
        lanes = slice(t * LANES, (t + width) * LANES)
        got = jnp.dot(pick, column_ref[:, lanes], preferred_element_type=F32).astype(BF16)
        for i in range(width):
            for c in range(owners):
                send_ref[c, (t + i) * group : (t + i + 1) * group] = got[
                    c * group : (c + 1) * group, tile_of(i)
                ]


def shift_kernel(from_ref, out_ref, half_ref, rot_ref):
    count, pixels = rot_ref.shape
    rots = from_ref.shape[0]
    half_count, half_rots = count // 2, rots // 2
    to = lax.broadcasted_iota(jnp.int32, (count, rots), 0)
    place = jnp.where(to < half_count, to, to - half_count + half_rots)
    real = to % half_count < half_rots
    own_first = lax.axis_index("dp") * half_rots
    place = jnp.where(place + own_first < rots, place + own_first, place + own_first - rots)
    chosen = (place == lax.broadcasted_iota(jnp.int32, (count, rots), 1)) & real
    picked = jnp.dot(chosen.astype(F32).astype(BF16), from_ref[...], preferred_element_type=F32)
    half = 0.5 * jnp.sum(picked * picked, axis=1, keepdims=True)
    half_ref[...] = jnp.broadcast_to(half, half_ref.shape)
    rot_ref[...] = picked.astype(BF16)
    tiles = pixels // LANES
    side = LANES // 2
    groups = len(COL_SHIFTS) * count
    source = lax.broadcasted_iota(jnp.int32, (2 * LANES, LANES), 0)
    lane = lax.broadcasted_iota(jnp.int32, (2 * LANES, LANES), 1)
    moves = []
    for parity in range(2):
        for shift in COL_SHIFTS:
            col = (lane - shift + side) % side
            home = (lane // side) * LANES + parity * side + col
            moves.append((source == home).astype(F32).astype(BF16))
    moves = jnp.concatenate(moves, axis=1)
    turn = ((lane[:LANES] + side) % LANES == source[:LANES]).astype(F32).astype(BF16)
    for h in range(tiles // 2):
        pair = jnp.concatenate(
            [rot_ref[:, tile_of(h)], rot_ref[:, tile_of(tiles // 2 + h)]], axis=1
        )
        moved = jnp.dot(pair, moves, preferred_element_type=F32).astype(BF16)
        for parity in range(2):
            for i in range(len(COL_SHIFTS)):
                plain = moved[:, tile_of(parity * len(COL_SHIFTS) + i)]
                for j, shift in enumerate(ROW_SHIFTS):
                    at = 2 * h + parity + shift
                    value = plain
                    if not 0 <= at < tiles:
                        at = at % tiles
                        value = jnp.dot(plain, turn, preferred_element_type=F32).astype(BF16)
                    first = j * groups + i * count
                    out_ref[first : first + count, tile_of(at)] = value


def score_kernel(recv_ref, shifted_ref, half_ref, x_ref, s_ref, tile_ref, *, pad):
    owners, depth, _ = recv_ref.shape
    tiles = x_ref.shape[1] // LANES - 2
    group = depth // (tiles + 1)
    slots = owners * group
    groups = s_ref.shape[0]
    count = half_ref.shape[0]
    for c in range(owners):
        for t in range(tiles):
            x_ref[c * group : (c + 1) * group, tile_of(t + 1)] = recv_ref[
                c, t * group : (t + 1) * group
            ]
    half_turn = LANES // 2
    x_ref[:, tile_of(0)] = pltpu.roll(x_ref[:, tile_of(tiles)].astype(F32), half_turn, 1).astype(
        BF16
    )
    x_ref[:, tile_of(tiles + 1)] = pltpu.roll(x_ref[:, tile_of(1)].astype(F32), half_turn, 1).astype(
        BF16
    )
    facts = recv_ref[:, tiles * group :, :].reshape(slots, LANES)
    choose = (
        lax.broadcasted_iota(jnp.int32, (16, LANES), 0)
        == lax.broadcasted_iota(jnp.int32, (16, LANES), 1)
    ).astype(F32).astype(BF16)
    turned = lax.dot_general(
        choose, facts, (((1,), (1,)), ((), ())), preferred_element_type=F32
    )
    noise, number = turned[0:1], turned[1:2]
    products = lax.dot_general(
        shifted_ref[...],
        x_ref[:, LANES : (tiles + 1) * LANES],
        (((1,), (1,)), ((), ())),
        preferred_element_type=F32,
    )
    half = half_ref[:, 0:1]
    row = lax.broadcasted_iota(jnp.int32, half.shape, 0)
    half = jnp.where(row % (count // 2) >= count // 2 - pad, FAR, half)
    half = jnp.concatenate([half] * len(COL_SHIFTS), axis=0)
    peak = None
    for i in range(len(ROW_SHIFTS)):
        scores = noise * (products[i * groups : (i + 1) * groups] - half)
        s_ref[:, i * slots : (i + 1) * slots] = scores
        top = jnp.max(scores, axis=0, keepdims=True)
        peak = top if peak is None else jnp.maximum(peak, top)
    total = jnp.zeros_like(peak)
    for i in range(len(ROW_SHIFTS)):
        scores = s_ref[:, i * slots : (i + 1) * slots]
        total = total + jnp.sum(jnp.exp(scores - peak), axis=0, keepdims=True)
    parts = slots // LANES
    for i, value in enumerate((peak, total, number)):
        for h in range(parts):
            tile_ref[i * parts + h : i * parts + h + 1] = value[:, tile_of(h)]
    tile_ref[3 * parts :] = jnp.zeros_like(tile_ref[3 * parts :])


def sum_kernel(s_ref, x_ref, mine_ref, all_ref, keep_ref, give_ref, w_ref, y_ref):
    groups = s_ref.shape[0]
    slots = x_ref.shape[0]
    pixels = x_ref.shape[1] - 2 * LANES
    owners = all_ref.shape[0] // 8
    count = groups // len(COL_SHIFTS)
    half_count = count // 2
    parts = slots // LANES
    side = LANES // 2
    lane = lane_row()
    second = (lane // PLANES) % SLOTS == 1

    def partner(row):
        return jnp.where(second, pltpu.roll(row, PLANES, 1), pltpu.roll(row, LANES - PLANES, 1))

    peaks, scales = [], []
    for h in range(parts):
        own = mine_ref[2 * parts + h : 2 * parts + h + 1]
        across = partner(own)
        shown = [all_ref[pl.ds(i * parts + h, owners, stride=8), :] for i in range(3)]
        found = []
        for slot in range(SLOTS):
            target = jnp.where(second == (slot == 1), own, across)
            same = shown[2] == target
            peak = jnp.max(jnp.where(same, shown[0], -jnp.inf), axis=0, keepdims=True)
            peak = jnp.maximum(peak, partner(peak))
            part = shown[1] * jnp.exp(jnp.minimum(shown[0] - peak, 0.0))
            total = jnp.sum(jnp.where(same, part, 0.0), axis=0, keepdims=True)
            found.append((peak, total + partner(total)))
        peaks.append(jnp.where(second, found[1][0], found[0][0]))
        total = jnp.where(second, found[1][1], found[0][1])
        scales.append(jnp.where(own > 0, 1.0 / total, 0.0))
    peak = jnp.concatenate(peaks, axis=1)
    scale = jnp.concatenate(scales, axis=1)
    row_total = jnp.zeros((groups, 1), F32)
    for i in range(len(ROW_SHIFTS)):
        part = slice(i * slots, (i + 1) * slots)
        weights = (jnp.exp(jnp.minimum(s_ref[:, part] - peak, 0.0)) * scale).astype(BF16)
        w_ref[:, part] = weights
        row_total = row_total + jnp.sum(weights.astype(F32), axis=1, keepdims=True)
    class_total = sum(row_total[i * count : (i + 1) * count] for i in range(len(COL_SHIFTS)))
    keep_ref[:, pixels:] = jnp.broadcast_to(class_total[:half_count], (half_count, LANES))
    give_ref[:, pixels:] = jnp.broadcast_to(class_total[half_count:], (half_count, LANES))
    width = y_ref.shape[1]
    column = lane % side
    for first in range(0, pixels, width):
        y_ref[...] = sum(
            jnp.dot(
                w_ref[:, i * slots : (i + 1) * slots],
                x_ref[:, (1 + shift) * LANES + first : (1 + shift) * LANES + first + width],
                preferred_element_type=F32,
            )
            for i, shift in enumerate(ROW_SHIFTS)
        )
        for t in range(width // LANES):
            plain = y_ref[:count, tile_of(t)]
            right = y_ref[count : 2 * count, tile_of(t)]
            left = y_ref[2 * count :, tile_of(t)]
            back = jnp.where(
                column == side - 1,
                pltpu.roll(right, side - 1, 1),
                pltpu.roll(right, LANES - 1, 1),
            )
            forth = jnp.where(
                column == 0, pltpu.roll(left, LANES - side + 1, 1), pltpu.roll(left, 1, 1)
            )
            moved = plain + back + forth
            at = slice(first + t * LANES, first + (t + 1) * LANES)
            keep_ref[:, at] = moved[:half_count]
            give_ref[:, at] = moved[half_count:]


def finish_kernel(keep_ref, other_ref, sums_ref, totals_ref):
    rots = totals_ref.shape[1]
    tiles = sums_ref.shape[0] // rots
    low = lane_row() < LANES // 2

    def load(t):
        return keep_ref[:rots, tile_of(t)] + other_ref[:rots, tile_of(t)]

    for t in range(tiles):
        sums_ref[pl.ds(t, rots, stride=tiles), :] = unfold_tile(load, t, tiles, low)
    total = load(tiles)
    here = lax.broadcasted_iota(jnp.int32, (rots, LANES), 0) == lax.broadcasted_iota(
        jnp.int32, (rots, LANES), 1
    )
    totals_ref[...] = jnp.sum(jnp.where(here, total, 0.0), axis=0, keepdims=True)[:, :rots]


def call(kernel, out_shape, count, limit, scratch=(), flops=0, moved=0, space=pltpu.VMEM):
    in_vmem = pl.BlockSpec(memory_space=pltpu.VMEM)
    return pl.pallas_call(
        kernel,
        out_shape=out_shape,
        in_specs=[pl.BlockSpec(memory_space=space)] * count,
        out_specs=jax.tree.map(lambda _: in_vmem, out_shape),
        scratch_shapes=list(scratch),
        cost_estimate=pl.CostEstimate(flops=flops, bytes_accessed=moved, transcendentals=0),
        compiler_params=pltpu.CompilerParams(vmem_limit_bytes=limit * MIB),
    )


def on_device(images, references, candidates, inv_noise):
    rows, top = candidates.shape
    cls_dev, rots, pixels = references.shape
    planes, owners = lax.axis_size("z"), lax.axis_size("xy")
    side = math.isqrt(pixels)
    tiles = pixels // LANES
    group = SLOTS * planes
    slots = owners * group
    assert cls_dev == 1 and planes == PLANES and LANES == 2 * side and rows == group
    shape = jax.ShapeDtypeStruct
    exchange = functools.partial(lax.all_to_all, split_axis=0, concat_axis=0, tiled=True)

    packed = call(
        pack_kernel,
        shape(((tiles + 1) * rows, LANES), BF16),
        3,
        4,
        moved=MIB // 4,
    )(candidates.T, inv_noise[None, :], images)

    def move(part, step):
        return lax.ppermute(part, "z", [(i, (i + step) % planes) for i in range(planes)])

    near = [move(packed, step) for step in (1, -1)]
    next_near = [move(packed, step) for step in (2, -2)]
    half_rots = rots // 2
    half_count = -(-half_rots // 8) * 8
    pad = half_count - half_rots
    count = 2 * half_count
    groups = len(COL_SHIFTS) * count
    shifted, half_norm = call(
        shift_kernel,
        (shape((len(ROW_SHIFTS) * groups, pixels), BF16), shape((count, LANES), F32)),
        1,
        6,
        [pltpu.VMEM((count, pixels), BF16)],
        moved=12 * MIB,
    )(references[0])
    next_near, shifted, half_norm = lax.optimization_barrier((next_near, shifted, half_norm))
    cut = (tiles + 1) // 2 * rows
    far = [move(next_near[0], 1), move(next_near[1], -1)]
    far += [move(next_near[0][:cut], 2), move(next_near[1][cut:], -2)]
    column = [packed, *near, *next_near, *far]
    steps = [0, -1, 1, -2, 2, -3, 3, 4, 4]
    picked = call(
        functools.partial(pick_kernel, steps=steps, top=top),
        shape((owners, (tiles + 1) * group, LANES), BF16),
        len(column),
        6,
        [pltpu.VMEM((planes * rows, (tiles + 1) * LANES), BF16)],
        moved=3 * MIB,
    )(*column)
    received = exchange(picked, "xy")
    work = 2 * len(ROW_SHIFTS) * groups * slots * pixels
    x, scores, tile = call(
        functools.partial(score_kernel, pad=pad),
        (
            shape((slots, pixels + 2 * LANES), BF16),
            shape((groups, len(ROW_SHIFTS) * slots), F32),
            shape((8, LANES), F32),
        ),
        3,
        8,
        flops=work,
        moved=10 * MIB,
    )(received, shifted, half_norm)
    by_plane = exchange(jnp.broadcast_to(tile[None], (planes, 8, LANES)), "z")
    by_plane = by_plane.reshape(1, planes * 8, LANES)
    everyone = exchange(jnp.broadcast_to(by_plane, (owners, planes * 8, LANES)), "xy")
    half_shape = shape((half_count, pixels + LANES), F32)
    keep, give = call(
        sum_kernel,
        (half_shape, half_shape),
        4,
        8,
        [
            pltpu.VMEM((groups, len(ROW_SHIFTS) * slots), BF16),
            pltpu.VMEM((groups, 4 * LANES), F32),
        ],
        flops=work,
        moved=5 * MIB,
    )(scores, x, tile, everyone.reshape(owners * planes * 8, LANES))
    other = lax.ppermute(give, "dp", [(0, 1), (1, 0)])
    sums, totals = call(
        finish_kernel,
        (shape((half_rots * tiles, LANES), F32), shape((1, half_rots), F32)),
        2,
        8,
        moved=2 * MIB,
    )(keep, other)
    return sums.reshape(1, half_rots, pixels), totals


def solution(mesh):
    split = (PLANES, mesh.shape["cls"] // PLANES, mesh.shape["dp"])
    cube = Mesh(mesh.devices.reshape(split), ("z", "xy", "dp"))
    every = ("z", "xy", "dp")
    by_class = ("z", "xy")
    return jax.shard_map(
        on_device,
        mesh=cube,
        in_specs=(P(every, None), P(by_class, None, None), P(every, None), P(every)),
        out_specs=(P(by_class, "dp", None), P(by_class, "dp")),
        check_vma=False,
    )
```

```python
import functools
import math

import jax
import jax.numpy as jnp
from jax import lax
from jax.experimental import pallas as pl
from jax.experimental.pallas import tpu as pltpu
from jax.sharding import Mesh
from jax.sharding import PartitionSpec as P

LANES = 128
SLOTS = 2
PLANES = 8
FAR = 1e30
ROW_SHIFTS = (0, 1, -1)
COL_SHIFTS = (0, 1, -1)
MIB = 1024 * 1024
F32, BF16 = jnp.float32, jnp.bfloat16


def tile_of(t):
    return slice(t * LANES, (t + 1) * LANES)


def lane_row():
    return lax.broadcasted_iota(jnp.int32, (1, LANES), 1)


def fold_tile(load, q, tiles, low):
    first, second = load(q // 2), load(tiles // 2 + q // 2)
    half = LANES // 2
    if q % 2 == 0:
        return jnp.where(low, first, pltpu.roll(second, half, 1))
    return jnp.where(low, pltpu.roll(first, half, 1), second)


def unfold_tile(load, t, tiles, low):
    half = LANES // 2
    if t < tiles // 2:
        return jnp.where(low, load(2 * t), pltpu.roll(load(2 * t + 1), half, 1))
    first = 2 * t - tiles
    return jnp.where(low, pltpu.roll(load(first), half, 1), load(first + 1))


def pack_kernel(cand_ref, noise_ref, img_ref, send_ref):
    top, rows = cand_ref.shape
    tiles = img_ref.shape[1] // LANES
    low = lane_row() < LANES // 2
    row_id = lax.broadcasted_iota(jnp.int32, (rows, LANES), 0)
    lane_id = lax.broadcasted_iota(jnp.int32, (rows, LANES), 1)
    diagonal = lax.broadcasted_iota(jnp.int32, (rows, rows), 0) == lax.broadcasted_iota(
        jnp.int32, (rows, rows), 1
    )
    noise = jnp.sum(
        jnp.where(diagonal, noise_ref[...].astype(F32), 0.0), axis=1, keepdims=True
    )
    place = lax.broadcasted_iota(jnp.int32, (top, LANES), 1) == (
        lax.broadcasted_iota(jnp.int32, (top, LANES), 0) + 2
    )
    facts = lax.dot_general(
        cand_ref[...].astype(F32).astype(BF16),
        place.astype(F32).astype(BF16),
        (((0,), (0,)), ((), ())),
        preferred_element_type=F32,
    )
    facts = jnp.where(lane_id == 0, noise, facts)
    facts = jnp.where(lane_id == 1, (row_id + 1).astype(F32), facts)
    send_ref[tiles * rows :] = facts.astype(BF16)
    for q in range(tiles):
        tile = fold_tile(lambda t: img_ref[:, tile_of(t)].astype(F32), q, tiles, low)
        send_ref[q * rows : (q + 1) * rows] = tile.astype(BF16)


def pick_kernel(*refs, steps, top):
    planes = len(steps) - 1
    recv_refs, send_ref, column_ref = refs[: len(steps)], refs[-2], refs[-1]
    owners, depth, _ = send_ref.shape
    rows = column_ref.shape[0] // planes
    tiles = column_ref.shape[1] // LANES
    group = depth // tiles
    slots = owners * group
    cut = recv_refs[-2].shape[0] // rows
    for j in range(planes):
        for t in range(tiles):
            from_ref, at = recv_refs[j], t
            if j == planes - 1 and t >= cut:
                from_ref, at = recv_refs[j + 1], t - cut
            column_ref[j * rows : (j + 1) * rows, tile_of(t)] = from_ref[
                at * rows : (at + 1) * rows
            ]
    count = planes * rows
    facts = column_ref[:, tile_of(tiles - 1)].astype(F32)
    here = lax.axis_index("z")
    row = lax.broadcasted_iota(jnp.int32, (count, 1), 0)
    sender = jnp.zeros((count, 1), jnp.int32)
    for j in range(planes):
        plane = lax.rem(here + steps[j] + planes, planes)
        sender = jnp.where(row // rows == j, plane, sender)
    lane = lax.broadcasted_iota(jnp.int32, (1, slots), 1)
    cls = (here * owners + lane // group).astype(F32)
    member = facts[:, 2:3] == cls
    for k in range(1, top):
        member = member | (facts[:, 2 + k : 3 + k] == cls)
    one, other = (lax.broadcasted_iota(jnp.int32, (count, count), i) for i in range(2))
    earlier = (one > other) & (one // rows == other // rows)
    before = jnp.dot(
        earlier.astype(F32).astype(BF16),
        member.astype(F32).astype(BF16),
        preferred_element_type=F32,
    )
    slot = (lane // planes) % SLOTS
    pick = member & (before == slot.astype(F32)) & (lane % planes == sender)
    pick = pick.astype(F32).T.astype(BF16)
    width = 3
    for t in range(0, tiles, width):
        lanes = slice(t * LANES, (t + width) * LANES)
        got = jnp.dot(pick, column_ref[:, lanes], preferred_element_type=F32).astype(BF16)
        for i in range(width):
            for c in range(owners):
                send_ref[c, (t + i) * group : (t + i + 1) * group] = got[
                    c * group : (c + 1) * group, tile_of(i)
                ]


def shift_kernel(from_ref, out_ref, half_ref, rot_ref):
    count, pixels = rot_ref.shape
    rots = from_ref.shape[0]
    half_count, half_rots = count // 2, rots // 2
    to = lax.broadcasted_iota(jnp.int32, (count, rots), 0)
    place = jnp.where(to < half_count, to, to - half_count + half_rots)
    real = to % half_count < half_rots
    own_first = lax.axis_index("dp") * half_rots
    place = jnp.where(place + own_first < rots, place + own_first, place + own_first - rots)
    chosen = (place == lax.broadcasted_iota(jnp.int32, (count, rots), 1)) & real
    picked = jnp.dot(chosen.astype(F32).astype(BF16), from_ref[...], preferred_element_type=F32)
    half = 0.5 * jnp.sum(picked * picked, axis=1, keepdims=True)
    half_ref[...] = jnp.broadcast_to(half, half_ref.shape)
    rot_ref[...] = picked.astype(BF16)
    tiles = pixels // LANES
    side = LANES // 2
    groups = len(COL_SHIFTS) * count
    source = lax.broadcasted_iota(jnp.int32, (2 * LANES, LANES), 0)
    lane = lax.broadcasted_iota(jnp.int32, (2 * LANES, LANES), 1)
    moves = []
    for parity in range(2):
        for shift in COL_SHIFTS:
            col = (lane - shift + side) % side
            home = (lane // side) * LANES + parity * side + col
            moves.append((source == home).astype(F32).astype(BF16))
    moves = jnp.concatenate(moves, axis=1)
    turn = ((lane[:LANES] + side) % LANES == source[:LANES]).astype(F32).astype(BF16)
    for h in range(tiles // 2):
        pair = jnp.concatenate(
            [rot_ref[:, tile_of(h)], rot_ref[:, tile_of(tiles // 2 + h)]], axis=1
        )
        moved = jnp.dot(pair, moves, preferred_element_type=F32).astype(BF16)
        for parity in range(2):
            for i in range(len(COL_SHIFTS)):
                plain = moved[:, tile_of(parity * len(COL_SHIFTS) + i)]
                for j, shift in enumerate(ROW_SHIFTS):
                    at = 2 * h + parity + shift
                    value = plain
                    if not 0 <= at < tiles:
                        at = at % tiles
                        value = jnp.dot(plain, turn, preferred_element_type=F32).astype(BF16)
                    first = j * groups + i * count
                    out_ref[first : first + count, tile_of(at)] = value


def score_kernel(recv_ref, shifted_ref, half_ref, x_ref, s_ref, tile_ref, *, pad):
    owners, depth, _ = recv_ref.shape
    tiles = x_ref.shape[1] // LANES - 2
    group = depth // (tiles + 1)
    slots = owners * group
    groups = s_ref.shape[0]
    count = half_ref.shape[0]
    for c in range(owners):
        for t in range(tiles):
            x_ref[c * group : (c + 1) * group, tile_of(t + 1)] = recv_ref[
                c, t * group : (t + 1) * group
            ]
    half_turn = LANES // 2
    x_ref[:, tile_of(0)] = pltpu.roll(x_ref[:, tile_of(tiles)].astype(F32), half_turn, 1).astype(
        BF16
    )
    x_ref[:, tile_of(tiles + 1)] = pltpu.roll(x_ref[:, tile_of(1)].astype(F32), half_turn, 1).astype(
        BF16
    )
    facts = recv_ref[:, tiles * group :, :].reshape(slots, LANES)
    choose = (
        lax.broadcasted_iota(jnp.int32, (16, LANES), 0)
        == lax.broadcasted_iota(jnp.int32, (16, LANES), 1)
    ).astype(F32).astype(BF16)
    turned = lax.dot_general(
        choose, facts, (((1,), (1,)), ((), ())), preferred_element_type=F32
    )
    noise, number = turned[0:1], turned[1:2]
    products = lax.dot_general(
        shifted_ref[...],
        x_ref[:, LANES : (tiles + 1) * LANES],
        (((1,), (1,)), ((), ())),
        preferred_element_type=F32,
    )
    half = half_ref[:, 0:1]
    row = lax.broadcasted_iota(jnp.int32, half.shape, 0)
    half = jnp.where(row % (count // 2) >= count // 2 - pad, FAR, half)
    half = jnp.concatenate([half] * len(COL_SHIFTS), axis=0)
    peak = None
    for i in range(len(ROW_SHIFTS)):
        scores = noise * (products[i * groups : (i + 1) * groups] - half)
        s_ref[:, i * slots : (i + 1) * slots] = scores
        top = jnp.max(scores, axis=0, keepdims=True)
        peak = top if peak is None else jnp.maximum(peak, top)
    total = jnp.zeros_like(peak)
    for i in range(len(ROW_SHIFTS)):
        scores = s_ref[:, i * slots : (i + 1) * slots]
        total = total + jnp.sum(jnp.exp(scores - peak), axis=0, keepdims=True)
    parts = slots // LANES
    for i, value in enumerate((peak, total, number)):
        for h in range(parts):
            tile_ref[i * parts + h : i * parts + h + 1] = value[:, tile_of(h)]
    tile_ref[3 * parts :] = jnp.zeros_like(tile_ref[3 * parts :])


def sum_half(w_ref, x_ref, out_ref, y_ref):
    slots = x_ref.shape[0]
    pixels = x_ref.shape[1] - 2 * LANES
    count = y_ref.shape[0] // len(COL_SHIFTS)
    side = LANES // 2
    width = y_ref.shape[1]
    column = lane_row() % side
    for first in range(0, pixels, width):
        y_ref[...] = sum(
            jnp.dot(
                w_ref[:, i * slots : (i + 1) * slots],
                x_ref[:, (1 + shift) * LANES + first : (1 + shift) * LANES + first + width],
                preferred_element_type=F32,
            )
            for i, shift in enumerate(ROW_SHIFTS)
        )
        for t in range(width // LANES):
            plain = y_ref[:count, tile_of(t)]
            right = y_ref[count : 2 * count, tile_of(t)]
            left = y_ref[2 * count :, tile_of(t)]
            back = jnp.where(
                column == side - 1,
                pltpu.roll(right, side - 1, 1),
                pltpu.roll(right, LANES - 1, 1),
            )
            forth = jnp.where(
                column == 0, pltpu.roll(left, LANES - side + 1, 1), pltpu.roll(left, 1, 1)
            )
            out_ref[:, first + t * LANES : first + (t + 1) * LANES] = plain + back + forth


def give_kernel(s_ref, x_ref, mine_ref, all_ref, give_ref, w_ref, total_ref, w_give_ref, y_ref):
    groups = s_ref.shape[0]
    slots = x_ref.shape[0]
    pixels = x_ref.shape[1] - 2 * LANES
    owners = all_ref.shape[0] // 8
    count = groups // len(COL_SHIFTS)
    half_count = count // 2
    parts = slots // LANES
    lane = lane_row()
    second = (lane // PLANES) % SLOTS == 1

    def partner(row):
        return jnp.where(second, pltpu.roll(row, PLANES, 1), pltpu.roll(row, LANES - PLANES, 1))

    peaks, scales = [], []
    for h in range(parts):
        own = mine_ref[2 * parts + h : 2 * parts + h + 1]
        across = partner(own)
        shown = [all_ref[pl.ds(i * parts + h, owners, stride=8), :] for i in range(3)]
        found = []
        for slot in range(SLOTS):
            target = jnp.where(second == (slot == 1), own, across)
            same = shown[2] == target
            peak = jnp.max(jnp.where(same, shown[0], -jnp.inf), axis=0, keepdims=True)
            peak = jnp.maximum(peak, partner(peak))
            part = shown[1] * jnp.exp(jnp.minimum(shown[0] - peak, 0.0))
            total = jnp.sum(jnp.where(same, part, 0.0), axis=0, keepdims=True)
            found.append((peak, total + partner(total)))
        peaks.append(jnp.where(second, found[1][0], found[0][0]))
        total = jnp.where(second, found[1][1], found[0][1])
        scales.append(jnp.where(own > 0, 1.0 / total, 0.0))
    peak = jnp.concatenate(peaks, axis=1)
    scale = jnp.concatenate(scales, axis=1)
    for half, to_ref, sums_ref in ((0, w_ref, total_ref), (1, w_give_ref, give_ref.at[:, pixels:])):
        class_total = jnp.zeros((half_count, 1), F32)
        for i in range(len(ROW_SHIFTS)):
            part = slice(i * slots, (i + 1) * slots)
            for j in range(len(COL_SHIFTS)):
                first = j * count + half * half_count
                weights = s_ref[first : first + half_count, part]
                weights = jnp.exp(jnp.minimum(weights - peak, 0.0)) * scale
                weights = weights.astype(BF16).astype(F32)
                class_total = class_total + jnp.sum(weights, axis=1, keepdims=True)
                y_ref[j * half_count : (j + 1) * half_count, :slots] = weights
            to_ref[:, part] = y_ref[:, :slots].astype(BF16)
        sums_ref[...] = jnp.broadcast_to(class_total, (half_count, LANES))
    sum_half(w_give_ref, x_ref, give_ref, y_ref)


def keep_kernel(w_ref, x_ref, keep_ref, y_ref):
    sum_half(w_ref, x_ref, keep_ref, y_ref)


def finish_kernel(keep_ref, total_ref, other_ref, sums_ref, totals_ref):
    rots = totals_ref.shape[1]
    tiles = sums_ref.shape[0] // rots
    low = lane_row() < LANES // 2

    def load(t):
        return keep_ref[:rots, tile_of(t)] + other_ref[:rots, tile_of(t)]

    for t in range(tiles):
        sums_ref[pl.ds(t, rots, stride=tiles), :] = unfold_tile(load, t, tiles, low)
    total = total_ref[:rots] + other_ref[:rots, tile_of(tiles)]
    here = lax.broadcasted_iota(jnp.int32, (rots, LANES), 0) == lax.broadcasted_iota(
        jnp.int32, (rots, LANES), 1
    )
    totals_ref[...] = jnp.sum(jnp.where(here, total, 0.0), axis=0, keepdims=True)[:, :rots]


def call(kernel, out_shape, count, limit, scratch=(), flops=0, moved=0, space=pltpu.VMEM):
    in_vmem = pl.BlockSpec(memory_space=pltpu.VMEM)
    return pl.pallas_call(
        kernel,
        out_shape=out_shape,
        in_specs=[pl.BlockSpec(memory_space=space)] * count,
        out_specs=jax.tree.map(lambda _: in_vmem, out_shape),
        scratch_shapes=list(scratch),
        cost_estimate=pl.CostEstimate(flops=flops, bytes_accessed=moved, transcendentals=0),
        compiler_params=pltpu.CompilerParams(vmem_limit_bytes=limit * MIB),
    )


def on_device(images, references, candidates, inv_noise):
    rows, top = candidates.shape
    cls_dev, rots, pixels = references.shape
    planes, owners = lax.axis_size("z"), lax.axis_size("xy")
    side = math.isqrt(pixels)
    tiles = pixels // LANES
    group = SLOTS * planes
    slots = owners * group
    assert cls_dev == 1 and planes == PLANES and LANES == 2 * side and rows == group
    shape = jax.ShapeDtypeStruct
    exchange = functools.partial(lax.all_to_all, split_axis=0, concat_axis=0, tiled=True)

    packed = call(
        pack_kernel,
        shape(((tiles + 1) * rows, LANES), BF16),
        3,
        4,
        moved=MIB // 4,
    )(candidates.T, inv_noise[None, :], images)

    def move(part, step):
        return lax.ppermute(part, "z", [(i, (i + step) % planes) for i in range(planes)])

    near = [move(packed, step) for step in (1, -1)]
    next_near = [move(packed, step) for step in (2, -2)]
    half_rots = rots // 2
    half_count = -(-half_rots // 8) * 8
    pad = half_count - half_rots
    count = 2 * half_count
    groups = len(COL_SHIFTS) * count
    shifted, half_norm = call(
        shift_kernel,
        (shape((len(ROW_SHIFTS) * groups, pixels), BF16), shape((count, LANES), F32)),
        1,
        6,
        [pltpu.VMEM((count, pixels), BF16)],
        moved=12 * MIB,
    )(references[0])
    next_near, shifted, half_norm = lax.optimization_barrier((next_near, shifted, half_norm))
    cut = (tiles + 1) // 2 * rows
    far = [move(next_near[0], 1), move(next_near[1], -1)]
    far += [move(next_near[0][:cut], 2), move(next_near[1][cut:], -2)]
    column = [packed, *near, *next_near, *far]
    steps = [0, -1, 1, -2, 2, -3, 3, 4, 4]
    picked = call(
        functools.partial(pick_kernel, steps=steps, top=top),
        shape((owners, (tiles + 1) * group, LANES), BF16),
        len(column),
        6,
        [pltpu.VMEM((planes * rows, (tiles + 1) * LANES), BF16)],
        moved=3 * MIB,
    )(*column)
    received = exchange(picked, "xy")
    work = 2 * len(ROW_SHIFTS) * groups * slots * pixels
    x, scores, tile = call(
        functools.partial(score_kernel, pad=pad),
        (
            shape((slots, pixels + 2 * LANES), BF16),
            shape((groups, len(ROW_SHIFTS) * slots), F32),
            shape((8, LANES), F32),
        ),
        3,
        8,
        flops=work,
        moved=10 * MIB,
    )(received, shifted, half_norm)
    by_plane = exchange(jnp.broadcast_to(tile[None], (planes, 8, LANES)), "z")
    by_plane = by_plane.reshape(1, planes * 8, LANES)
    everyone = exchange(jnp.broadcast_to(by_plane, (owners, planes * 8, LANES)), "xy")
    weight_shape = (groups // 2, len(ROW_SHIFTS) * slots)
    scratch = pltpu.VMEM((groups // 2, 4 * LANES), F32)
    give, weights, total = call(
        give_kernel,
        (
            shape((half_count, pixels + LANES), F32),
            shape(weight_shape, BF16),
            shape((half_count, LANES), F32),
        ),
        4,
        8,
        [pltpu.VMEM(weight_shape, BF16), scratch],
        flops=work // 2,
        moved=5 * MIB,
    )(scores, x, tile, everyone.reshape(owners * planes * 8, LANES))
    other = lax.ppermute(give, "dp", [(0, 1), (1, 0)])
    keep = call(
        keep_kernel,
        shape((half_count, pixels), F32),
        2,
        8,
        [scratch],
        flops=work // 2,
        moved=4 * MIB,
    )(weights, x)
    sums, totals = call(
        finish_kernel,
        (shape((half_rots * tiles, LANES), F32), shape((1, half_rots), F32)),
        3,
        8,
        moved=2 * MIB,
    )(keep, total, other)
    return sums.reshape(1, half_rots, pixels), totals


def solution(mesh):
    split = (PLANES, mesh.shape["cls"] // PLANES, mesh.shape["dp"])
    cube = Mesh(mesh.devices.reshape(split), ("z", "xy", "dp"))
    every = ("z", "xy", "dp")
    by_class = ("z", "xy")
    return jax.shard_map(
        on_device,
        mesh=cube,
        in_specs=(P(every, None), P(by_class, None, None), P(every, None), P(every)),
        out_specs=(P(by_class, "dp", None), P(by_class, "dp")),
        check_vma=False,
    )
```

```python
import functools
import math

import jax
import jax.numpy as jnp
from jax import lax
from jax.experimental import pallas as pl
from jax.experimental.pallas import tpu as pltpu
from jax.sharding import Mesh
from jax.sharding import PartitionSpec as P

LANES = 128
SLOTS = 2
PLANES = 8
FAR = 1e30
ROW_SHIFTS = (0, 1, -1)
COL_SHIFTS = (0, 1, -1)
MIB = 1024 * 1024
F32, BF16 = jnp.float32, jnp.bfloat16


def tile_of(t):
    return slice(t * LANES, (t + 1) * LANES)


def lane_row():
    return lax.broadcasted_iota(jnp.int32, (1, LANES), 1)


def fold_tile(load, q, tiles, low):
    first, second = load(q // 2), load(tiles // 2 + q // 2)
    half = LANES // 2
    if q % 2 == 0:
        return jnp.where(low, first, pltpu.roll(second, half, 1))
    return jnp.where(low, pltpu.roll(first, half, 1), second)


def unfold_tile(load, t, tiles, low):
    half = LANES // 2
    if t < tiles // 2:
        return jnp.where(low, load(2 * t), pltpu.roll(load(2 * t + 1), half, 1))
    first = 2 * t - tiles
    return jnp.where(low, pltpu.roll(load(first), half, 1), load(first + 1))


def pack_kernel(cand_ref, noise_ref, img_ref, send_ref):
    top, rows = cand_ref.shape
    tiles = img_ref.shape[1] // LANES
    low = lane_row() < LANES // 2
    row_id = lax.broadcasted_iota(jnp.int32, (rows, LANES), 0)
    lane_id = lax.broadcasted_iota(jnp.int32, (rows, LANES), 1)
    diagonal = lax.broadcasted_iota(jnp.int32, (rows, rows), 0) == lax.broadcasted_iota(
        jnp.int32, (rows, rows), 1
    )
    noise = jnp.sum(
        jnp.where(diagonal, noise_ref[...].astype(F32), 0.0), axis=1, keepdims=True
    )
    place = lax.broadcasted_iota(jnp.int32, (top, LANES), 1) == (
        lax.broadcasted_iota(jnp.int32, (top, LANES), 0) + 2
    )
    facts = lax.dot_general(
        cand_ref[...].astype(F32).astype(BF16),
        place.astype(F32).astype(BF16),
        (((0,), (0,)), ((), ())),
        preferred_element_type=F32,
    )
    facts = jnp.where(lane_id == 0, noise, facts)
    facts = jnp.where(lane_id == 1, (row_id + 1).astype(F32), facts)
    send_ref[tiles * rows :] = facts.astype(BF16)
    for q in range(tiles):
        tile = fold_tile(lambda t: img_ref[:, tile_of(t)].astype(F32), q, tiles, low)
        send_ref[q * rows : (q + 1) * rows] = tile.astype(BF16)


def pick_kernel(*refs, steps, top):
    planes = len(steps)
    recv_refs, send_ref, column_ref = refs[:planes], refs[-2], refs[-1]
    owners, depth, _ = send_ref.shape
    rows = column_ref.shape[0] // planes
    tiles = column_ref.shape[1] // LANES
    group = depth // tiles
    slots = owners * group
    for j in range(planes):
        for t in range(tiles):
            column_ref[j * rows : (j + 1) * rows, tile_of(t)] = recv_refs[j][
                t * rows : (t + 1) * rows
            ]
    count = planes * rows
    facts = column_ref[:, tile_of(tiles - 1)].astype(F32)
    here = lax.axis_index("z")
    way = 1 - 2 * lax.axis_index("dp")
    row = lax.broadcasted_iota(jnp.int32, (count, 1), 0)
    sender = jnp.zeros((count, 1), jnp.int32)
    for j in range(planes):
        plane = lax.rem(here + way * steps[j] + planes, planes)
        sender = jnp.where(row // rows == j, plane, sender)
    lane = lax.broadcasted_iota(jnp.int32, (1, slots), 1)
    cls = (here * owners + lane // group).astype(F32)
    member = facts[:, 2:3] == cls
    for k in range(1, top):
        member = member | (facts[:, 2 + k : 3 + k] == cls)
    one, other = (lax.broadcasted_iota(jnp.int32, (count, count), i) for i in range(2))
    earlier = (one > other) & (one // rows == other // rows)
    before = jnp.dot(
        earlier.astype(F32).astype(BF16),
        member.astype(F32).astype(BF16),
        preferred_element_type=F32,
    )
    slot = (lane // planes) % SLOTS
    pick = member & (before == slot.astype(F32)) & (lane % planes == sender)
    pick = pick.astype(F32).T.astype(BF16)
    width = 3
    for t in range(0, tiles, width):
        lanes = slice(t * LANES, (t + width) * LANES)
        got = jnp.dot(pick, column_ref[:, lanes], preferred_element_type=F32).astype(BF16)
        for i in range(width):
            for c in range(owners):
                send_ref[c, (t + i) * group : (t + i + 1) * group] = got[
                    c * group : (c + 1) * group, tile_of(i)
                ]


def shift_kernel(from_ref, packed_ref, out_ref, half_ref, own_ref, rot_ref):
    own_ref[...] = packed_ref[...]
    count, pixels = rot_ref.shape
    rots = from_ref.shape[0]
    half_count, half_rots = count // 2, rots // 2
    to = lax.broadcasted_iota(jnp.int32, (count, rots), 0)
    place = jnp.where(to < half_count, to, to - half_count + half_rots)
    real = to % half_count < half_rots
    own_first = lax.axis_index("dp") * half_rots
    place = jnp.where(place + own_first < rots, place + own_first, place + own_first - rots)
    chosen = (place == lax.broadcasted_iota(jnp.int32, (count, rots), 1)) & real
    picked = jnp.dot(chosen.astype(F32).astype(BF16), from_ref[...], preferred_element_type=F32)
    half = 0.5 * jnp.sum(picked * picked, axis=1, keepdims=True)
    half_ref[...] = jnp.broadcast_to(half, half_ref.shape)
    rot_ref[...] = picked.astype(BF16)
    tiles = pixels // LANES
    side = LANES // 2
    groups = len(COL_SHIFTS) * count
    source = lax.broadcasted_iota(jnp.int32, (2 * LANES, LANES), 0)
    lane = lax.broadcasted_iota(jnp.int32, (2 * LANES, LANES), 1)
    moves = []
    for parity in range(2):
        for shift in COL_SHIFTS:
            col = (lane - shift + side) % side
            home = (lane // side) * LANES + parity * side + col
            moves.append((source == home).astype(F32).astype(BF16))
    moves = jnp.concatenate(moves, axis=1)
    turn = ((lane[:LANES] + side) % LANES == source[:LANES]).astype(F32).astype(BF16)
    for h in range(tiles // 2):
        pair = jnp.concatenate(
            [rot_ref[:, tile_of(h)], rot_ref[:, tile_of(tiles // 2 + h)]], axis=1
        )
        moved = jnp.dot(pair, moves, preferred_element_type=F32).astype(BF16)
        for parity in range(2):
            for i in range(len(COL_SHIFTS)):
                plain = moved[:, tile_of(parity * len(COL_SHIFTS) + i)]
                for j, shift in enumerate(ROW_SHIFTS):
                    at = 2 * h + parity + shift
                    value = plain
                    if not 0 <= at < tiles:
                        at = at % tiles
                        value = jnp.dot(plain, turn, preferred_element_type=F32).astype(BF16)
                    first = j * groups + i * count
                    out_ref[first : first + count, tile_of(at)] = value


def score_kernel(recv_ref, shifted_ref, half_ref, x_ref, s_ref, tile_ref, *, pad):
    owners, depth, _ = recv_ref.shape
    tiles = x_ref.shape[1] // LANES - 2
    group = depth // (tiles + 1)
    slots = owners * group
    groups = s_ref.shape[0]
    count = half_ref.shape[0]
    for c in range(owners):
        for t in range(tiles):
            x_ref[c * group : (c + 1) * group, tile_of(t + 1)] = recv_ref[
                c, t * group : (t + 1) * group
            ]
    half_turn = LANES // 2
    x_ref[:, tile_of(0)] = pltpu.roll(x_ref[:, tile_of(tiles)].astype(F32), half_turn, 1).astype(
        BF16
    )
    x_ref[:, tile_of(tiles + 1)] = pltpu.roll(x_ref[:, tile_of(1)].astype(F32), half_turn, 1).astype(
        BF16
    )
    facts = recv_ref[:, tiles * group :, :].reshape(slots, LANES)
    choose = (
        lax.broadcasted_iota(jnp.int32, (16, LANES), 0)
        == lax.broadcasted_iota(jnp.int32, (16, LANES), 1)
    ).astype(F32).astype(BF16)
    turned = lax.dot_general(
        choose, facts, (((1,), (1,)), ((), ())), preferred_element_type=F32
    )
    noise, number = turned[0:1], turned[1:2]
    products = lax.dot_general(
        shifted_ref[...],
        x_ref[:, LANES : (tiles + 1) * LANES],
        (((1,), (1,)), ((), ())),
        preferred_element_type=F32,
    )
    half = half_ref[:, 0:1]
    row = lax.broadcasted_iota(jnp.int32, half.shape, 0)
    half = jnp.where(row % (count // 2) >= count // 2 - pad, FAR, half)
    half = jnp.concatenate([half] * len(COL_SHIFTS), axis=0)
    peak = None
    for i in range(len(ROW_SHIFTS)):
        scores = noise * (products[i * groups : (i + 1) * groups] - half)
        s_ref[:, i * slots : (i + 1) * slots] = scores
        top = jnp.max(scores, axis=0, keepdims=True)
        peak = top if peak is None else jnp.maximum(peak, top)
    total = jnp.zeros_like(peak)
    for i in range(len(ROW_SHIFTS)):
        scores = s_ref[:, i * slots : (i + 1) * slots]
        total = total + jnp.sum(jnp.exp(scores - peak), axis=0, keepdims=True)
    parts = slots // LANES
    for i, value in enumerate((peak, total, number)):
        for h in range(parts):
            tile_ref[i * parts + h : i * parts + h + 1] = value[:, tile_of(h)]
    tile_ref[3 * parts :] = jnp.zeros_like(tile_ref[3 * parts :])


def sum_half(w_ref, x_ref, out_ref, y_ref):
    slots = x_ref.shape[0]
    pixels = x_ref.shape[1] - 2 * LANES
    count = y_ref.shape[0] // len(COL_SHIFTS)
    side = LANES // 2
    width = y_ref.shape[1]
    column = lane_row() % side
    for first in range(0, pixels, width):
        y_ref[...] = sum(
            jnp.dot(
                w_ref[:, i * slots : (i + 1) * slots],
                x_ref[:, (1 + shift) * LANES + first : (1 + shift) * LANES + first + width],
                preferred_element_type=F32,
            )
            for i, shift in enumerate(ROW_SHIFTS)
        )
        for t in range(width // LANES):
            plain = y_ref[:count, tile_of(t)]
            right = y_ref[count : 2 * count, tile_of(t)]
            left = y_ref[2 * count :, tile_of(t)]
            back = jnp.where(
                column == side - 1,
                pltpu.roll(right, side - 1, 1),
                pltpu.roll(right, LANES - 1, 1),
            )
            forth = jnp.where(
                column == 0, pltpu.roll(left, LANES - side + 1, 1), pltpu.roll(left, 1, 1)
            )
            out_ref[:, first + t * LANES : first + (t + 1) * LANES] = plain + back + forth


def give_kernel(s_ref, x_ref, mine_ref, all_ref, give_ref, w_ref, total_ref, w_give_ref, y_ref):
    groups = s_ref.shape[0]
    slots = x_ref.shape[0]
    pixels = x_ref.shape[1] - 2 * LANES
    owners = all_ref.shape[0] // 8
    count = groups // len(COL_SHIFTS)
    half_count = count // 2
    parts = slots // LANES
    lane = lane_row()
    second = (lane // PLANES) % SLOTS == 1

    def partner(row):
        return jnp.where(second, pltpu.roll(row, PLANES, 1), pltpu.roll(row, LANES - PLANES, 1))

    peaks, scales = [], []
    for h in range(parts):
        own = mine_ref[2 * parts + h : 2 * parts + h + 1]
        across = partner(own)
        shown = [all_ref[pl.ds(i * parts + h, owners, stride=8), :] for i in range(3)]
        found = []
        for slot in range(SLOTS):
            target = jnp.where(second == (slot == 1), own, across)
            same = shown[2] == target
            peak = jnp.max(jnp.where(same, shown[0], -jnp.inf), axis=0, keepdims=True)
            peak = jnp.maximum(peak, partner(peak))
            part = shown[1] * jnp.exp(jnp.minimum(shown[0] - peak, 0.0))
            total = jnp.sum(jnp.where(same, part, 0.0), axis=0, keepdims=True)
            found.append((peak, total + partner(total)))
        peaks.append(jnp.where(second, found[1][0], found[0][0]))
        total = jnp.where(second, found[1][1], found[0][1])
        scales.append(jnp.where(own > 0, 1.0 / total, 0.0))
    peak = jnp.concatenate(peaks, axis=1)
    scale = jnp.concatenate(scales, axis=1)
    for half, to_ref, sums_ref in ((0, w_ref, total_ref), (1, w_give_ref, give_ref.at[:, pixels:])):
        class_total = jnp.zeros((half_count, 1), F32)
        for i in range(len(ROW_SHIFTS)):
            part = slice(i * slots, (i + 1) * slots)
            for j in range(len(COL_SHIFTS)):
                first = j * count + half * half_count
                weights = s_ref[first : first + half_count, part]
                weights = jnp.exp(jnp.minimum(weights - peak, 0.0)) * scale
                weights = weights.astype(BF16).astype(F32)
                class_total = class_total + jnp.sum(weights, axis=1, keepdims=True)
                y_ref[j * half_count : (j + 1) * half_count, :slots] = weights
            to_ref[:, part] = y_ref[:, :slots].astype(BF16)
        sums_ref[...] = jnp.broadcast_to(class_total, (half_count, LANES))
    sum_half(w_give_ref, x_ref, give_ref, y_ref)


def keep_kernel(w_ref, x_ref, keep_ref, y_ref):
    sum_half(w_ref, x_ref, keep_ref, y_ref)


def finish_kernel(keep_ref, total_ref, other_ref, sums_ref, totals_ref):
    rots = totals_ref.shape[1]
    tiles = sums_ref.shape[0] // rots
    low = lane_row() < LANES // 2

    def load(t):
        return keep_ref[:rots, tile_of(t)] + other_ref[:rots, tile_of(t)]

    for t in range(tiles):
        sums_ref[pl.ds(t, rots, stride=tiles), :] = unfold_tile(load, t, tiles, low)
    total = total_ref[:rots] + other_ref[:rots, tile_of(tiles)]
    here = lax.broadcasted_iota(jnp.int32, (rots, LANES), 0) == lax.broadcasted_iota(
        jnp.int32, (rots, LANES), 1
    )
    totals_ref[...] = jnp.sum(jnp.where(here, total, 0.0), axis=0, keepdims=True)[:, :rots]


def call(kernel, out_shape, count, limit, scratch=(), flops=0, moved=0, space=pltpu.VMEM):
    in_vmem = pl.BlockSpec(memory_space=pltpu.VMEM)
    return pl.pallas_call(
        kernel,
        out_shape=out_shape,
        in_specs=[pl.BlockSpec(memory_space=space)] * count,
        out_specs=jax.tree.map(lambda _: in_vmem, out_shape),
        scratch_shapes=list(scratch),
        cost_estimate=pl.CostEstimate(flops=flops, bytes_accessed=moved, transcendentals=0),
        compiler_params=pltpu.CompilerParams(vmem_limit_bytes=limit * MIB),
    )


def on_device(images, references, candidates, inv_noise):
    rows, top = candidates.shape
    cls_dev, rots, pixels = references.shape
    planes, owners = lax.axis_size("z"), lax.axis_size("xy")
    side = math.isqrt(pixels)
    tiles = pixels // LANES
    group = SLOTS * planes
    slots = owners * group
    assert cls_dev == 1 and planes == PLANES and LANES == 2 * side and rows == group
    shape = jax.ShapeDtypeStruct
    exchange = functools.partial(lax.all_to_all, split_axis=0, concat_axis=0, tiled=True)

    packed = call(
        pack_kernel,
        shape(((tiles + 1) * rows, LANES), BF16),
        3,
        54,
        moved=MIB // 4,
    )(candidates.T, inv_noise[None, :], images)

    def move(part, step):
        pairs = []
        for z in range(planes):
            pairs += [
                (2 * z, (z + step) % planes * 2),
                (2 * z + 1, (z - step) % planes * 2 + 1),
            ]
        return lax.ppermute(part, ("z", "dp"), pairs)

    near = [move(packed, step) for step in (1, -1)]
    next_near = [move(packed, step) for step in (2, -2)]

    half_rots = rots // 2
    half_count = -(-half_rots // 8) * 8
    pad = half_count - half_rots
    count = 2 * half_count
    groups = len(COL_SHIFTS) * count
    shifted, half_norm, own = call(
        shift_kernel,
        (
            shape((len(ROW_SHIFTS) * groups, pixels), BF16),
            shape((count, LANES), F32),
            shape(packed.shape, BF16),
        ),
        2,
        6,
        [pltpu.VMEM((count, pixels), BF16)],
        moved=12 * MIB,
    )(references[0], packed)
    next_near, shifted, half_norm, own = lax.optimization_barrier(
        (next_near, shifted, half_norm, own)
    )
    far = [move(next_near[0], 1), move(next_near[1], -1), move(next_near[0], 2)]
    column = [own, *near, *next_near, *far]
    steps = [0, -1, 1, -2, 2, -3, 3, 4]
    picked = call(
        functools.partial(pick_kernel, steps=steps, top=top),
        shape((owners, (tiles + 1) * group, LANES), BF16),
        len(column),
        6,
        [pltpu.VMEM((planes * rows, (tiles + 1) * LANES), BF16)],
        moved=3 * MIB,
    )(*column)
    received = exchange(picked, "xy")
    work = 2 * len(ROW_SHIFTS) * groups * slots * pixels
    x, scores, tile = call(
        functools.partial(score_kernel, pad=pad),
        (
            shape((slots, pixels + 2 * LANES), BF16),
            shape((groups, len(ROW_SHIFTS) * slots), F32),
            shape((8, LANES), F32),
        ),
        3,
        8,
        flops=work,
        moved=10 * MIB,
    )(received, shifted, half_norm)
    by_plane = exchange(jnp.broadcast_to(tile[None], (planes, 8, LANES)), "z")
    by_plane = by_plane.reshape(1, planes * 8, LANES)
    everyone = exchange(jnp.broadcast_to(by_plane, (owners, planes * 8, LANES)), "xy")
    weight_shape = (groups // 2, len(ROW_SHIFTS) * slots)
    scratch = pltpu.VMEM((groups // 2, 4 * LANES), F32)
    give, weights, total = call(
        give_kernel,
        (
            shape((half_count, pixels + LANES), F32),
            shape(weight_shape, BF16),
            shape((half_count, LANES), F32),
        ),
        4,
        8,
        [pltpu.VMEM(weight_shape, BF16), scratch],
        flops=work // 2,
        moved=5 * MIB,
    )(scores, x, tile, everyone.reshape(owners * planes * 8, LANES))
    other = lax.ppermute(give, "dp", [(0, 1), (1, 0)])
    keep = call(
        keep_kernel,
        shape((half_count, pixels), F32),
        2,
        8,
        [scratch],
        flops=work // 2,
        moved=4 * MIB,
    )(weights, x)
    sums, totals = call(
        finish_kernel,
        (shape((half_rots * tiles, LANES), F32), shape((1, half_rots), F32)),
        3,
        8,
        moved=2 * MIB,
    )(keep, total, other)
    return sums.reshape(1, half_rots, pixels), totals


def solution(mesh):
    split = (PLANES, mesh.shape["cls"] // PLANES, mesh.shape["dp"])
    cube = Mesh(mesh.devices.reshape(split), ("z", "xy", "dp"))
    every = ("z", "xy", "dp")
    by_class = ("z", "xy")
    return jax.shard_map(
        on_device,
        mesh=cube,
        in_specs=(P(every, None), P(by_class, None, None), P(every, None), P(every)),
        out_specs=(P(by_class, "dp", None), P(by_class, "dp")),
        check_vma=False,
    )
```

```python
import functools
import math

import jax
import jax.numpy as jnp
from jax import lax
from jax.experimental import pallas as pl
from jax.experimental.pallas import tpu as pltpu
from jax.sharding import Mesh
from jax.sharding import PartitionSpec as P

LANES = 128
SLOTS = 2
PLANES = 8
FAR = 1e30
ROW_SHIFTS = (0, 1, -1)
COL_SHIFTS = (0, 1, -1)
MIB = 1024 * 1024
F32, BF16 = jnp.float32, jnp.bfloat16


def tile_of(t):
    return slice(t * LANES, (t + 1) * LANES)


def lane_row():
    return lax.broadcasted_iota(jnp.int32, (1, LANES), 1)


def fold_tile(load, q, tiles, low):
    first, second = load(q // 2), load(tiles // 2 + q // 2)
    half = LANES // 2
    if q % 2 == 0:
        return jnp.where(low, first, pltpu.roll(second, half, 1))
    return jnp.where(low, pltpu.roll(first, half, 1), second)


def unfold_tile(load, t, tiles, low):
    half = LANES // 2
    if t < tiles // 2:
        return jnp.where(low, load(2 * t), pltpu.roll(load(2 * t + 1), half, 1))
    first = 2 * t - tiles
    return jnp.where(low, pltpu.roll(load(first), half, 1), load(first + 1))


def pack_kernel(cand_ref, noise_ref, img_ref, send_ref):
    top, rows = cand_ref.shape
    tiles = img_ref.shape[1] // LANES
    low = lane_row() < LANES // 2
    row_id = lax.broadcasted_iota(jnp.int32, (rows, LANES), 0)
    lane_id = lax.broadcasted_iota(jnp.int32, (rows, LANES), 1)
    diagonal = lax.broadcasted_iota(jnp.int32, (rows, rows), 0) == lax.broadcasted_iota(
        jnp.int32, (rows, rows), 1
    )
    noise = jnp.sum(
        jnp.where(diagonal, noise_ref[...].astype(F32), 0.0), axis=1, keepdims=True
    )
    place = lax.broadcasted_iota(jnp.int32, (top, LANES), 1) == (
        lax.broadcasted_iota(jnp.int32, (top, LANES), 0) + 2
    )
    facts = lax.dot_general(
        cand_ref[...].astype(F32).astype(BF16),
        place.astype(F32).astype(BF16),
        (((0,), (0,)), ((), ())),
        preferred_element_type=F32,
    )
    facts = jnp.where(lane_id == 0, noise, facts)
    facts = jnp.where(lane_id == 1, (row_id + 1).astype(F32), facts)
    send_ref[tiles * rows :] = facts.astype(BF16)
    for q in range(tiles):
        tile = fold_tile(lambda t: img_ref[:, tile_of(t)].astype(F32), q, tiles, low)
        send_ref[q * rows : (q + 1) * rows] = tile.astype(BF16)


def pick_kernel(*refs, steps, top):
    planes = len(steps)
    recv_refs, send_ref, column_ref = refs[:planes], refs[-2], refs[-1]
    owners, depth, _ = send_ref.shape
    rows = column_ref.shape[0] // planes
    tiles = column_ref.shape[1] // LANES
    group = depth // tiles
    slots = owners * group
    for j in range(planes):
        for t in range(tiles):
            column_ref[j * rows : (j + 1) * rows, tile_of(t)] = recv_refs[j][
                t * rows : (t + 1) * rows
            ]
    count = planes * rows
    facts = column_ref[:, tile_of(tiles - 1)].astype(F32)
    here = lax.axis_index("z")
    way = 1 - 2 * lax.axis_index("dp")
    row = lax.broadcasted_iota(jnp.int32, (count, 1), 0)
    sender = jnp.zeros((count, 1), jnp.int32)
    for j in range(planes):
        plane = lax.rem(here + way * steps[j] + planes, planes)
        sender = jnp.where(row // rows == j, plane, sender)
    lane = lax.broadcasted_iota(jnp.int32, (1, slots), 1)
    cls = (here * owners + lane // group).astype(F32)
    member = facts[:, 2:3] == cls
    for k in range(1, top):
        member = member | (facts[:, 2 + k : 3 + k] == cls)
    one, other = (lax.broadcasted_iota(jnp.int32, (count, count), i) for i in range(2))
    earlier = (one > other) & (one // rows == other // rows)
    before = jnp.dot(
        earlier.astype(F32).astype(BF16),
        member.astype(F32).astype(BF16),
        preferred_element_type=F32,
    )
    slot = (lane // planes) % SLOTS
    pick = member & (before == slot.astype(F32)) & (lane % planes == sender)
    pick = pick.astype(F32).T.astype(BF16)
    width = 3
    for t in range(0, tiles, width):
        lanes = slice(t * LANES, (t + width) * LANES)
        got = jnp.dot(pick, column_ref[:, lanes], preferred_element_type=F32).astype(BF16)
        for i in range(width):
            for c in range(owners):
                send_ref[c, (t + i) * group : (t + i + 1) * group] = got[
                    c * group : (c + 1) * group, tile_of(i)
                ]


def shift_kernel(from_ref, packed_ref, out_ref, half_ref, own_ref, rot_ref):
    own_ref[...] = packed_ref[...]
    count, pixels = rot_ref.shape
    rots = from_ref.shape[0]
    half_count, half_rots = count // 2, rots // 2
    to = lax.broadcasted_iota(jnp.int32, (count, rots), 0)
    place = jnp.where(to < half_count, to, to - half_count + half_rots)
    real = to % half_count < half_rots
    own_first = lax.axis_index("dp") * half_rots
    place = jnp.where(place + own_first < rots, place + own_first, place + own_first - rots)
    chosen = (place == lax.broadcasted_iota(jnp.int32, (count, rots), 1)) & real
    picked = jnp.dot(chosen.astype(F32).astype(BF16), from_ref[...], preferred_element_type=F32)
    half = 0.5 * jnp.sum(picked * picked, axis=1, keepdims=True)
    half_ref[...] = jnp.broadcast_to(half, half_ref.shape)
    rot_ref[...] = picked.astype(BF16)
    tiles = pixels // LANES
    side = LANES // 2
    groups = len(COL_SHIFTS) * count
    source = lax.broadcasted_iota(jnp.int32, (2 * LANES, LANES), 0)
    lane = lax.broadcasted_iota(jnp.int32, (2 * LANES, LANES), 1)
    moves = []
    for parity in range(2):
        for shift in COL_SHIFTS:
            col = (lane - shift + side) % side
            home = (lane // side) * LANES + parity * side + col
            moves.append((source == home).astype(F32).astype(BF16))
    moves = jnp.concatenate(moves, axis=1)
    turn = ((lane[:LANES] + side) % LANES == source[:LANES]).astype(F32).astype(BF16)
    for h in range(tiles // 2):
        pair = jnp.concatenate(
            [rot_ref[:, tile_of(h)], rot_ref[:, tile_of(tiles // 2 + h)]], axis=1
        )
        moved = jnp.dot(pair, moves, preferred_element_type=F32).astype(BF16)
        for parity in range(2):
            for i in range(len(COL_SHIFTS)):
                plain = moved[:, tile_of(parity * len(COL_SHIFTS) + i)]
                for j, shift in enumerate(ROW_SHIFTS):
                    at = 2 * h + parity + shift
                    value = plain
                    if not 0 <= at < tiles:
                        at = at % tiles
                        value = jnp.dot(plain, turn, preferred_element_type=F32).astype(BF16)
                    first = j * groups + i * count
                    out_ref[first : first + count, tile_of(at)] = value


def score_kernel(
    recv_at, shifted_ref, half_ref, x_ref, s_ref, tile_ref, recv_ref, sem, *, pad
):
    load = pltpu.make_async_copy(recv_at, recv_ref, sem)
    load.start()
    load.wait()
    owners, depth, _ = recv_ref.shape
    tiles = x_ref.shape[1] // LANES - 2
    group = depth // (tiles + 1)
    slots = owners * group
    groups = s_ref.shape[0]
    count = half_ref.shape[0]
    for c in range(owners):
        for t in range(tiles):
            x_ref[c * group : (c + 1) * group, tile_of(t + 1)] = recv_ref[
                c, t * group : (t + 1) * group
            ]
    half_turn = LANES // 2
    x_ref[:, tile_of(0)] = pltpu.roll(x_ref[:, tile_of(tiles)].astype(F32), half_turn, 1).astype(
        BF16
    )
    x_ref[:, tile_of(tiles + 1)] = pltpu.roll(x_ref[:, tile_of(1)].astype(F32), half_turn, 1).astype(
        BF16
    )
    facts = recv_ref[:, tiles * group :, :].reshape(slots, LANES)
    choose = (
        lax.broadcasted_iota(jnp.int32, (16, LANES), 0)
        == lax.broadcasted_iota(jnp.int32, (16, LANES), 1)
    ).astype(F32).astype(BF16)
    turned = lax.dot_general(
        choose, facts, (((1,), (1,)), ((), ())), preferred_element_type=F32
    )
    noise, number = turned[0:1], turned[1:2]
    products = lax.dot_general(
        shifted_ref[...],
        x_ref[:, LANES : (tiles + 1) * LANES],
        (((1,), (1,)), ((), ())),
        preferred_element_type=F32,
    )
    half = half_ref[:, 0:1]
    row = lax.broadcasted_iota(jnp.int32, half.shape, 0)
    half = jnp.where(row % (count // 2) >= count // 2 - pad, FAR, half)
    half = jnp.concatenate([half] * len(COL_SHIFTS), axis=0)
    peak = None
    for i in range(len(ROW_SHIFTS)):
        scores = noise * (products[i * groups : (i + 1) * groups] - half)
        s_ref[:, i * slots : (i + 1) * slots] = scores
        top = jnp.max(scores, axis=0, keepdims=True)
        peak = top if peak is None else jnp.maximum(peak, top)
    total = jnp.zeros_like(peak)
    for i in range(len(ROW_SHIFTS)):
        scores = s_ref[:, i * slots : (i + 1) * slots]
        total = total + jnp.sum(jnp.exp(scores - peak), axis=0, keepdims=True)
    parts = slots // LANES
    for i, value in enumerate((peak, total, number)):
        for h in range(parts):
            tile_ref[i * parts + h : i * parts + h + 1] = value[:, tile_of(h)]
    tile_ref[3 * parts :] = jnp.zeros_like(tile_ref[3 * parts :])


def sum_half(w_ref, x_ref, out_ref, y_ref):
    slots = x_ref.shape[0]
    pixels = x_ref.shape[1] - 2 * LANES
    count = y_ref.shape[0] // len(COL_SHIFTS)
    side = LANES // 2
    width = y_ref.shape[1]
    column = lane_row() % side
    for first in range(0, pixels, width):
        y_ref[...] = sum(
            jnp.dot(
                w_ref[:, i * slots : (i + 1) * slots],
                x_ref[:, (1 + shift) * LANES + first : (1 + shift) * LANES + first + width],
                preferred_element_type=F32,
            )
            for i, shift in enumerate(ROW_SHIFTS)
        )
        for t in range(width // LANES):
            plain = y_ref[:count, tile_of(t)]
            right = y_ref[count : 2 * count, tile_of(t)]
            left = y_ref[2 * count :, tile_of(t)]
            back = jnp.where(
                column == side - 1,
                pltpu.roll(right, side - 1, 1),
                pltpu.roll(right, LANES - 1, 1),
            )
            forth = jnp.where(
                column == 0, pltpu.roll(left, LANES - side + 1, 1), pltpu.roll(left, 1, 1)
            )
            out_ref[:, first + t * LANES : first + (t + 1) * LANES] = plain + back + forth


def give_kernel(s_ref, x_ref, mine_ref, all_ref, give_ref, w_ref, total_ref, w_give_ref, y_ref):
    groups = s_ref.shape[0]
    slots = x_ref.shape[0]
    pixels = x_ref.shape[1] - 2 * LANES
    owners = all_ref.shape[0] // 8
    count = groups // len(COL_SHIFTS)
    half_count = count // 2
    parts = slots // LANES
    lane = lane_row()
    second = (lane // PLANES) % SLOTS == 1

    def partner(row):
        return jnp.where(second, pltpu.roll(row, PLANES, 1), pltpu.roll(row, LANES - PLANES, 1))

    peaks, scales = [], []
    for h in range(parts):
        own = mine_ref[2 * parts + h : 2 * parts + h + 1]
        across = partner(own)
        shown = [all_ref[pl.ds(i * parts + h, owners, stride=8), :] for i in range(3)]
        found = []
        for slot in range(SLOTS):
            target = jnp.where(second == (slot == 1), own, across)
            same = shown[2] == target
            peak = jnp.max(jnp.where(same, shown[0], -jnp.inf), axis=0, keepdims=True)
            peak = jnp.maximum(peak, partner(peak))
            part = shown[1] * jnp.exp(jnp.minimum(shown[0] - peak, 0.0))
            total = jnp.sum(jnp.where(same, part, 0.0), axis=0, keepdims=True)
            found.append((peak, total + partner(total)))
        peaks.append(jnp.where(second, found[1][0], found[0][0]))
        total = jnp.where(second, found[1][1], found[0][1])
        scales.append(jnp.where(own > 0, 1.0 / total, 0.0))
    peak = jnp.concatenate(peaks, axis=1)
    scale = jnp.concatenate(scales, axis=1)
    for half, to_ref, sums_ref in ((0, w_ref, total_ref), (1, w_give_ref, give_ref.at[:, pixels:])):
        class_total = jnp.zeros((half_count, 1), F32)
        for i in range(len(ROW_SHIFTS)):
            part = slice(i * slots, (i + 1) * slots)
            for j in range(len(COL_SHIFTS)):
                first = j * count + half * half_count
                weights = s_ref[first : first + half_count, part]
                weights = jnp.exp(jnp.minimum(weights - peak, 0.0)) * scale
                weights = weights.astype(BF16).astype(F32)
                class_total = class_total + jnp.sum(weights, axis=1, keepdims=True)
                y_ref[j * half_count : (j + 1) * half_count, :slots] = weights
            to_ref[:, part] = y_ref[:, :slots].astype(BF16)
        sums_ref[...] = jnp.broadcast_to(class_total, (half_count, LANES))
    sum_half(w_give_ref, x_ref, give_ref, y_ref)


def keep_kernel(w_ref, x_ref, keep_ref, y_ref):
    sum_half(w_ref, x_ref, keep_ref, y_ref)


def finish_kernel(keep_ref, total_ref, other_ref, sums_ref, totals_ref):
    rots = totals_ref.shape[1]
    tiles = sums_ref.shape[0] // rots
    low = lane_row() < LANES // 2

    def load(t):
        return keep_ref[:rots, tile_of(t)] + other_ref[:rots, tile_of(t)]

    for t in range(tiles):
        sums_ref[pl.ds(t, rots, stride=tiles), :] = unfold_tile(load, t, tiles, low)
    total = total_ref[:rots] + other_ref[:rots, tile_of(tiles)]
    here = lax.broadcasted_iota(jnp.int32, (rots, LANES), 0) == lax.broadcasted_iota(
        jnp.int32, (rots, LANES), 1
    )
    totals_ref[...] = jnp.sum(jnp.where(here, total, 0.0), axis=0, keepdims=True)[:, :rots]


def call(kernel, out_shape, count, limit, scratch=(), flops=0, moved=0, far=0):
    in_vmem = pl.BlockSpec(memory_space=pltpu.VMEM)
    return pl.pallas_call(
        kernel,
        out_shape=out_shape,
        in_specs=[pl.BlockSpec(memory_space=pltpu.HBM)] * far + [in_vmem] * (count - far),
        out_specs=jax.tree.map(lambda _: in_vmem, out_shape),
        scratch_shapes=list(scratch),
        cost_estimate=pl.CostEstimate(flops=flops, bytes_accessed=moved, transcendentals=0),
        compiler_params=pltpu.CompilerParams(vmem_limit_bytes=limit * MIB),
    )


def on_device(images, references, candidates, inv_noise):
    rows, top = candidates.shape
    cls_dev, rots, pixels = references.shape
    planes, owners = lax.axis_size("z"), lax.axis_size("xy")
    side = math.isqrt(pixels)
    tiles = pixels // LANES
    group = SLOTS * planes
    slots = owners * group
    assert cls_dev == 1 and planes == PLANES and LANES == 2 * side and rows == group
    shape = jax.ShapeDtypeStruct
    exchange = functools.partial(lax.all_to_all, split_axis=0, concat_axis=0, tiled=True)

    packed = call(
        pack_kernel,
        shape(((tiles + 1) * rows, LANES), BF16),
        3,
        54,
        moved=MIB // 4,
    )(candidates.T, inv_noise[None, :], images)

    def move(part, step):
        pairs = []
        for z in range(planes):
            pairs += [
                (2 * z, (z + step) % planes * 2),
                (2 * z + 1, (z - step) % planes * 2 + 1),
            ]
        return lax.ppermute(part, ("z", "dp"), pairs)

    near = [move(packed, step) for step in (1, -1)]
    next_near = [move(packed, step) for step in (2, -2)]

    half_rots = rots // 2
    half_count = -(-half_rots // 8) * 8
    pad = half_count - half_rots
    count = 2 * half_count
    groups = len(COL_SHIFTS) * count
    shifted, half_norm, own = call(
        shift_kernel,
        (
            shape((len(ROW_SHIFTS) * groups, pixels), BF16),
            shape((count, LANES), F32),
            shape(packed.shape, BF16),
        ),
        2,
        6,
        [pltpu.VMEM((count, pixels), BF16)],
        moved=12 * MIB,
    )(references[0], packed)
    next_near, shifted, half_norm, own = lax.optimization_barrier(
        (next_near, shifted, half_norm, own)
    )
    far = [move(next_near[0], 1), move(next_near[1], -1), move(next_near[0], 2)]
    column = [own, *near, *next_near, *far]
    steps = [0, -1, 1, -2, 2, -3, 3, 4]
    picked = call(
        functools.partial(pick_kernel, steps=steps, top=top),
        shape((owners, (tiles + 1) * group, LANES), BF16),
        len(column),
        6,
        [pltpu.VMEM((planes * rows, (tiles + 1) * LANES), BF16)],
        moved=3 * MIB,
    )(*column)
    received = pltpu.with_memory_space_constraint(exchange(picked, "xy"), pltpu.HBM)
    work = 2 * len(ROW_SHIFTS) * groups * slots * pixels
    x, scores, tile = call(
        functools.partial(score_kernel, pad=pad),
        (
            shape((slots, pixels + 2 * LANES), BF16),
            shape((groups, len(ROW_SHIFTS) * slots), F32),
            shape((8, LANES), F32),
        ),
        3,
        8,
        [pltpu.VMEM(picked.shape, BF16), pltpu.SemaphoreType.DMA],
        flops=work,
        moved=10 * MIB,
        far=1,
    )(received, shifted, half_norm)
    by_plane = exchange(jnp.broadcast_to(tile[None], (planes, 8, LANES)), "z")
    by_plane = by_plane.reshape(1, planes * 8, LANES)
    everyone = exchange(jnp.broadcast_to(by_plane, (owners, planes * 8, LANES)), "xy")
    weight_shape = (groups // 2, len(ROW_SHIFTS) * slots)
    scratch = pltpu.VMEM((groups // 2, 4 * LANES), F32)
    give, weights, total = call(
        give_kernel,
        (
            shape((half_count, pixels + LANES), F32),
            shape(weight_shape, BF16),
            shape((half_count, LANES), F32),
        ),
        4,
        8,
        [pltpu.VMEM(weight_shape, BF16), scratch],
        flops=work // 2,
        moved=5 * MIB,
    )(scores, x, tile, everyone.reshape(owners * planes * 8, LANES))
    other = lax.ppermute(give, "dp", [(0, 1), (1, 0)])
    keep = call(
        keep_kernel,
        shape((half_count, pixels), F32),
        2,
        8,
        [scratch],
        flops=work // 2,
        moved=4 * MIB,
    )(weights, x)
    sums, totals = call(
        finish_kernel,
        (shape((half_rots * tiles, LANES), F32), shape((1, half_rots), F32)),
        3,
        8,
        moved=2 * MIB,
    )(keep, total, other)
    return sums.reshape(1, half_rots, pixels), totals


def solution(mesh):
    split = (PLANES, mesh.shape["cls"] // PLANES, mesh.shape["dp"])
    cube = Mesh(mesh.devices.reshape(split), ("z", "xy", "dp"))
    every = ("z", "xy", "dp")
    by_class = ("z", "xy")
    return jax.shard_map(
        on_device,
        mesh=cube,
        in_specs=(P(every, None), P(by_class, None, None), P(every, None), P(every)),
        out_specs=(P(by_class, "dp", None), P(by_class, "dp")),
        check_vma=False,
    )
```

```python
import functools
import math

import jax
import jax.numpy as jnp
from jax import lax
from jax.experimental import pallas as pl
from jax.experimental.pallas import tpu as pltpu
from jax.sharding import Mesh
from jax.sharding import PartitionSpec as P

LANES = 128
SLOTS = 2
PLANES = 8
FAR = 1e30
ROW_SHIFTS = (0, 1, -1)
COL_SHIFTS = (0, 1, -1)
MIB = 1024 * 1024
F32, BF16 = jnp.float32, jnp.bfloat16


def tile_of(t):
    return slice(t * LANES, (t + 1) * LANES)


def lane_row():
    return lax.broadcasted_iota(jnp.int32, (1, LANES), 1)


def fold_tile(load, q, tiles, low):
    first, second = load(q // 2), load(tiles // 2 + q // 2)
    half = LANES // 2
    if q % 2 == 0:
        return jnp.where(low, first, pltpu.roll(second, half, 1))
    return jnp.where(low, pltpu.roll(first, half, 1), second)


def unfold_tile(load, t, tiles, low):
    half = LANES // 2
    if t < tiles // 2:
        return jnp.where(low, load(2 * t), pltpu.roll(load(2 * t + 1), half, 1))
    first = 2 * t - tiles
    return jnp.where(low, pltpu.roll(load(first), half, 1), load(first + 1))


def pack_kernel(cand_ref, noise_ref, img_ref, send_ref):
    top, rows = cand_ref.shape
    tiles = img_ref.shape[1] // LANES
    low = lane_row() < LANES // 2
    row_id = lax.broadcasted_iota(jnp.int32, (rows, LANES), 0)
    lane_id = lax.broadcasted_iota(jnp.int32, (rows, LANES), 1)
    diagonal = lax.broadcasted_iota(jnp.int32, (rows, rows), 0) == lax.broadcasted_iota(
        jnp.int32, (rows, rows), 1
    )
    noise = jnp.sum(
        jnp.where(diagonal, noise_ref[...].astype(F32), 0.0), axis=1, keepdims=True
    )
    place = lax.broadcasted_iota(jnp.int32, (top, LANES), 1) == (
        lax.broadcasted_iota(jnp.int32, (top, LANES), 0) + 2
    )
    facts = lax.dot_general(
        cand_ref[...].astype(F32).astype(BF16),
        place.astype(F32).astype(BF16),
        (((0,), (0,)), ((), ())),
        preferred_element_type=F32,
    )
    facts = jnp.where(lane_id == 0, noise, facts)
    facts = jnp.where(lane_id == 1, (row_id + 1).astype(F32), facts)
    send_ref[tiles * rows :] = facts.astype(BF16)
    for q in range(tiles):
        tile = fold_tile(lambda t: img_ref[:, tile_of(t)].astype(F32), q, tiles, low)
        send_ref[q * rows : (q + 1) * rows] = tile.astype(BF16)


def pick_kernel(*refs, steps, top):
    planes = len(steps) - 1
    recv_refs, send_ref, column_ref = refs[: len(steps)], refs[-2], refs[-1]
    owners, depth, _ = send_ref.shape
    rows = column_ref.shape[0] // planes
    tiles = column_ref.shape[1] // LANES
    group = depth // tiles
    slots = owners * group
    cut = recv_refs[-2].shape[0] // rows
    for j in range(planes):
        for t in range(tiles):
            from_ref, at = recv_refs[j], t
            if j == planes - 1 and t >= cut:
                from_ref, at = recv_refs[j + 1], t - cut
            column_ref[j * rows : (j + 1) * rows, tile_of(t)] = from_ref[
                at * rows : (at + 1) * rows
            ]
    count = planes * rows
    facts = column_ref[:, tile_of(tiles - 1)].astype(F32)
    here = lax.axis_index("z")
    row = lax.broadcasted_iota(jnp.int32, (count, 1), 0)
    sender = jnp.zeros((count, 1), jnp.int32)
    for j in range(planes):
        plane = lax.rem(here + steps[j] + planes, planes)
        sender = jnp.where(row // rows == j, plane, sender)
    lane = lax.broadcasted_iota(jnp.int32, (1, slots), 1)
    cls = (here * owners + lane // group).astype(F32)
    member = facts[:, 2:3] == cls
    for k in range(1, top):
        member = member | (facts[:, 2 + k : 3 + k] == cls)
    one, other = (lax.broadcasted_iota(jnp.int32, (count, count), i) for i in range(2))
    earlier = (one > other) & (one // rows == other // rows)
    before = jnp.dot(
        earlier.astype(F32).astype(BF16),
        member.astype(F32).astype(BF16),
        preferred_element_type=F32,
    )
    slot = (lane // planes) % SLOTS
    pick = member & (before == slot.astype(F32)) & (lane % planes == sender)
    pick = pick.astype(F32).T.astype(BF16)
    width = 3
    for t in range(0, tiles, width):
        lanes = slice(t * LANES, (t + width) * LANES)
        got = jnp.dot(pick, column_ref[:, lanes], preferred_element_type=F32).astype(BF16)
        for i in range(width):
            for c in range(owners):
                send_ref[c, (t + i) * group : (t + i + 1) * group] = got[
                    c * group : (c + 1) * group, tile_of(i)
                ]


def shift_kernel(from_ref, packed_ref, out_ref, half_ref, own_ref, rot_ref):
    own_ref[...] = packed_ref[...]
    count, pixels = rot_ref.shape
    rots = from_ref.shape[0]
    half_count, half_rots = count // 2, rots // 2
    to = lax.broadcasted_iota(jnp.int32, (count, rots), 0)
    place = jnp.where(to < half_count, to, to - half_count + half_rots)
    real = to % half_count < half_rots
    own_first = lax.axis_index("dp") * half_rots
    place = jnp.where(place + own_first < rots, place + own_first, place + own_first - rots)
    chosen = (place == lax.broadcasted_iota(jnp.int32, (count, rots), 1)) & real
    picked = jnp.dot(chosen.astype(F32).astype(BF16), from_ref[...], preferred_element_type=F32)
    half = 0.5 * jnp.sum(picked * picked, axis=1, keepdims=True)
    half_ref[...] = jnp.broadcast_to(half, half_ref.shape)
    rot_ref[...] = picked.astype(BF16)
    tiles = pixels // LANES
    side = LANES // 2
    groups = len(COL_SHIFTS) * count
    source = lax.broadcasted_iota(jnp.int32, (2 * LANES, LANES), 0)
    lane = lax.broadcasted_iota(jnp.int32, (2 * LANES, LANES), 1)
    moves = []
    for parity in range(2):
        for shift in COL_SHIFTS:
            col = (lane - shift + side) % side
            home = (lane // side) * LANES + parity * side + col
            moves.append((source == home).astype(F32).astype(BF16))
    moves = jnp.concatenate(moves, axis=1)
    turn = ((lane[:LANES] + side) % LANES == source[:LANES]).astype(F32).astype(BF16)
    for h in range(tiles // 2):
        pair = jnp.concatenate(
            [rot_ref[:, tile_of(h)], rot_ref[:, tile_of(tiles // 2 + h)]], axis=1
        )
        moved = jnp.dot(pair, moves, preferred_element_type=F32).astype(BF16)
        for parity in range(2):
            for i in range(len(COL_SHIFTS)):
                plain = moved[:, tile_of(parity * len(COL_SHIFTS) + i)]
                for j, shift in enumerate(ROW_SHIFTS):
                    at = 2 * h + parity + shift
                    value = plain
                    if not 0 <= at < tiles:
                        at = at % tiles
                        value = jnp.dot(plain, turn, preferred_element_type=F32).astype(BF16)
                    first = j * groups + i * count
                    out_ref[first : first + count, tile_of(at)] = value


def score_kernel(recv_ref, shifted_ref, half_ref, x_ref, s_ref, tile_ref, *, pad):
    owners, depth, _ = recv_ref.shape
    tiles = x_ref.shape[1] // LANES - 2
    group = depth // (tiles + 1)
    slots = owners * group
    groups = s_ref.shape[0]
    count = half_ref.shape[0]
    for c in range(owners):
        for t in range(tiles):
            x_ref[c * group : (c + 1) * group, tile_of(t + 1)] = recv_ref[
                c, t * group : (t + 1) * group
            ]
    half_turn = LANES // 2
    x_ref[:, tile_of(0)] = pltpu.roll(x_ref[:, tile_of(tiles)].astype(F32), half_turn, 1).astype(
        BF16
    )
    x_ref[:, tile_of(tiles + 1)] = pltpu.roll(x_ref[:, tile_of(1)].astype(F32), half_turn, 1).astype(
        BF16
    )
    facts = recv_ref[:, tiles * group :, :].reshape(slots, LANES)
    choose = (
        lax.broadcasted_iota(jnp.int32, (16, LANES), 0)
        == lax.broadcasted_iota(jnp.int32, (16, LANES), 1)
    ).astype(F32).astype(BF16)
    turned = lax.dot_general(
        choose, facts, (((1,), (1,)), ((), ())), preferred_element_type=F32
    )
    noise, number = turned[0:1], turned[1:2]
    products = lax.dot_general(
        shifted_ref[...],
        x_ref[:, LANES : (tiles + 1) * LANES],
        (((1,), (1,)), ((), ())),
        preferred_element_type=F32,
    )
    half = half_ref[:, 0:1]
    row = lax.broadcasted_iota(jnp.int32, half.shape, 0)
    half = jnp.where(row % (count // 2) >= count // 2 - pad, FAR, half)
    half = jnp.concatenate([half] * len(COL_SHIFTS), axis=0)
    peak = None
    for i in range(len(ROW_SHIFTS)):
        scores = noise * (products[i * groups : (i + 1) * groups] - half)
        s_ref[:, i * slots : (i + 1) * slots] = scores
        top = jnp.max(scores, axis=0, keepdims=True)
        peak = top if peak is None else jnp.maximum(peak, top)
    total = jnp.zeros_like(peak)
    for i in range(len(ROW_SHIFTS)):
        scores = s_ref[:, i * slots : (i + 1) * slots]
        total = total + jnp.sum(jnp.exp(scores - peak), axis=0, keepdims=True)
    parts = slots // LANES
    for i, value in enumerate((peak, total, number)):
        for h in range(parts):
            tile_ref[0, i * parts + h : i * parts + h + 1] = value[:, tile_of(h)]
    tile_ref[0, 3 * parts :] = jnp.zeros_like(tile_ref[0, 3 * parts :])
    for i in range(1, tile_ref.shape[0]):
        tile_ref[i] = tile_ref[0]


def partner_of(rows):
    second = (lane_row() // PLANES) % SLOTS == 1
    return jnp.where(
        second, pltpu.roll(rows, PLANES, 1), pltpu.roll(rows, LANES - PLANES, 1)
    )


def fold_kernel(shown_ref, out_ref):
    planes = shown_ref.shape[0]
    rows = out_ref.shape[1] // 2
    second = (lane_row() // PLANES) % SLOTS == 1
    parts = 2
    shown = [
        [
            jnp.concatenate(
                [shown_ref[z, i * parts + h : i * parts + h + 1] for z in range(planes)], axis=0
            )
            for h in range(parts)
        ]
        for i in range(3)
    ]
    for p in range(rows):
        found = []
        for h in range(parts):
            same = shown[2][h] == p + 1
            peak = jnp.max(jnp.where(same, shown[0][h], -FAR), axis=0, keepdims=True)
            peak = jnp.maximum(peak, partner_of(peak))
            part = shown[1][h] * jnp.exp(jnp.minimum(shown[0][h] - peak, 0.0))
            total = jnp.sum(jnp.where(same, part, 0.0), axis=0, keepdims=True)
            found.append((peak, total + partner_of(total)))
        out_ref[0, p : p + 1] = jnp.where(second, found[1][0], found[0][0])
        out_ref[0, rows + p : rows + p + 1] = jnp.where(second, found[1][1], found[0][1])
    for i in range(1, out_ref.shape[0]):
        out_ref[i] = out_ref[0]


def sum_half(w_ref, x_ref, out_ref, y_ref):
    slots = x_ref.shape[0]
    pixels = x_ref.shape[1] - 2 * LANES
    count = y_ref.shape[0] // len(COL_SHIFTS)
    side = LANES // 2
    width = y_ref.shape[1]
    column = lane_row() % side
    for first in range(0, pixels, width):
        y_ref[...] = sum(
            jnp.dot(
                w_ref[:, i * slots : (i + 1) * slots],
                x_ref[:, (1 + shift) * LANES + first : (1 + shift) * LANES + first + width],
                preferred_element_type=F32,
            )
            for i, shift in enumerate(ROW_SHIFTS)
        )
        for t in range(width // LANES):
            plain = y_ref[:count, tile_of(t)]
            right = y_ref[count : 2 * count, tile_of(t)]
            left = y_ref[2 * count :, tile_of(t)]
            back = jnp.where(
                column == side - 1,
                pltpu.roll(right, side - 1, 1),
                pltpu.roll(right, LANES - 1, 1),
            )
            forth = jnp.where(
                column == 0, pltpu.roll(left, LANES - side + 1, 1), pltpu.roll(left, 1, 1)
            )
            out_ref[:, first + t * LANES : first + (t + 1) * LANES] = plain + back + forth


def give_kernel(s_ref, x_ref, mine_ref, all_ref, give_ref, w_ref, total_ref, w_give_ref, y_ref):
    groups = s_ref.shape[0]
    slots = x_ref.shape[0]
    pixels = x_ref.shape[1] - 2 * LANES
    rows = all_ref.shape[1] // 2
    count = groups // len(COL_SHIFTS)
    half_count = count // 2
    parts = slots // LANES
    second = (lane_row() // PLANES) % SLOTS == 1
    tables = range(all_ref.shape[0])
    peak = all_ref[0, :rows]
    for i in tables:
        peak = jnp.maximum(peak, all_ref[i, :rows])
    total = jnp.zeros_like(peak)
    for i in tables:
        total = total + all_ref[i, rows:] * jnp.exp(all_ref[i, :rows] - peak)
    number = lax.broadcasted_iota(jnp.int32, (rows, LANES), 0).astype(F32) + 1
    peaks, scales = [], []
    for h in range(parts):
        own = mine_ref[0, 2 * parts + h : 2 * parts + h + 1]
        here = second == (h == 1)
        mine = [
            jnp.sum(
                jnp.where(number == own, jnp.where(here, table, partner_of(table)), 0.0),
                axis=0,
                keepdims=True,
            )
            for table in (peak, total)
        ]
        peaks.append(mine[0])
        scales.append(jnp.where(own > 0, 1.0 / jnp.where(own > 0, mine[1], 1.0), 0.0))
    peak = jnp.concatenate(peaks, axis=1)
    scale = jnp.concatenate(scales, axis=1)
    for half, to_ref, sums_ref in ((0, w_ref, total_ref), (1, w_give_ref, give_ref.at[:, pixels:])):
        class_total = jnp.zeros((half_count, 1), F32)
        for i in range(len(ROW_SHIFTS)):
            part = slice(i * slots, (i + 1) * slots)
            for j in range(len(COL_SHIFTS)):
                first = j * count + half * half_count
                weights = s_ref[first : first + half_count, part]
                weights = jnp.exp(jnp.minimum(weights - peak, 0.0)) * scale
                weights = weights.astype(BF16).astype(F32)
                class_total = class_total + jnp.sum(weights, axis=1, keepdims=True)
                y_ref[j * half_count : (j + 1) * half_count, :slots] = weights
            to_ref[:, part] = y_ref[:, :slots].astype(BF16)
        sums_ref[...] = jnp.broadcast_to(class_total, (half_count, LANES))
    sum_half(w_give_ref, x_ref, give_ref, y_ref)


def keep_kernel(w_ref, x_ref, keep_ref, y_ref):
    sum_half(w_ref, x_ref, keep_ref, y_ref)


def finish_kernel(keep_ref, total_ref, other_ref, sums_ref, totals_ref):
    rots = totals_ref.shape[1]
    tiles = sums_ref.shape[0] // rots
    low = lane_row() < LANES // 2

    def load(t):
        return keep_ref[:rots, tile_of(t)] + other_ref[:rots, tile_of(t)]

    for t in range(tiles):
        sums_ref[pl.ds(t, rots, stride=tiles), :] = unfold_tile(load, t, tiles, low)
    total = total_ref[:rots] + other_ref[:rots, tile_of(tiles)]
    here = lax.broadcasted_iota(jnp.int32, (rots, LANES), 0) == lax.broadcasted_iota(
        jnp.int32, (rots, LANES), 1
    )
    totals_ref[...] = jnp.sum(jnp.where(here, total, 0.0), axis=0, keepdims=True)[:, :rots]


def call(kernel, out_shape, count, limit, scratch=(), flops=0, moved=0, space=pltpu.VMEM):
    in_vmem = pl.BlockSpec(memory_space=pltpu.VMEM)
    return pl.pallas_call(
        kernel,
        out_shape=out_shape,
        in_specs=[pl.BlockSpec(memory_space=space)] * count,
        out_specs=jax.tree.map(lambda _: in_vmem, out_shape),
        scratch_shapes=list(scratch),
        cost_estimate=pl.CostEstimate(flops=flops, bytes_accessed=moved, transcendentals=0),
        compiler_params=pltpu.CompilerParams(vmem_limit_bytes=limit * MIB),
    )


def on_device(images, references, candidates, inv_noise):
    rows, top = candidates.shape
    cls_dev, rots, pixels = references.shape
    planes, owners = lax.axis_size("z"), lax.axis_size("xy")
    side = math.isqrt(pixels)
    tiles = pixels // LANES
    group = SLOTS * planes
    slots = owners * group
    assert cls_dev == 1 and planes == PLANES and LANES == 2 * side and rows == group
    shape = jax.ShapeDtypeStruct
    exchange = functools.partial(lax.all_to_all, split_axis=0, concat_axis=0, tiled=True)

    packed = call(
        pack_kernel,
        shape(((tiles + 1) * rows, LANES), BF16),
        3,
        54,
        moved=MIB // 4,
    )(candidates.T, inv_noise[None, :], images)

    def move(part, step):
        return lax.ppermute(part, "z", [(i, (i + step) % planes) for i in range(planes)])

    near = [move(packed, step) for step in (1, -1)]
    next_near = [move(packed, step) for step in (2, -2)]
    half_rots = rots // 2
    half_count = -(-half_rots // 8) * 8
    pad = half_count - half_rots
    count = 2 * half_count
    groups = len(COL_SHIFTS) * count
    shifted, half_norm, own = call(
        shift_kernel,
        (
            shape((len(ROW_SHIFTS) * groups, pixels), BF16),
            shape((count, LANES), F32),
            shape(packed.shape, BF16),
        ),
        2,
        6,
        [pltpu.VMEM((count, pixels), BF16)],
        moved=12 * MIB,
    )(references[0], packed)
    next_near, shifted, half_norm, own = lax.optimization_barrier(
        (next_near, shifted, half_norm, own)
    )
    cut = (tiles + 1) // 2 * rows
    far = [move(next_near[0], 1), move(next_near[1], -1)]
    far += [move(next_near[0][:cut], 2), move(next_near[1][cut:], -2)]
    column = [own, *near, *next_near, *far]
    steps = [0, -1, 1, -2, 2, -3, 3, 4, 4]
    picked = call(
        functools.partial(pick_kernel, steps=steps, top=top),
        shape((owners, (tiles + 1) * group, LANES), BF16),
        len(column),
        6,
        [pltpu.VMEM((planes * rows, (tiles + 1) * LANES), BF16)],
        moved=3 * MIB,
    )(*column)
    received = exchange(picked, "xy")
    work = 2 * len(ROW_SHIFTS) * groups * slots * pixels
    x, scores, tile = call(
        functools.partial(score_kernel, pad=pad),
        (
            shape((slots, pixels + 2 * LANES), BF16),
            shape((groups, len(ROW_SHIFTS) * slots), F32),
            shape((planes, 8, LANES), F32),
        ),
        3,
        8,
        flops=work,
        moved=10 * MIB,
    )(received, shifted, half_norm)
    folded = call(
        fold_kernel, shape((owners, 2 * rows, LANES), F32), 1, 4, moved=MIB // 4
    )(exchange(tile, "z"))
    everyone = exchange(folded, "xy")
    weight_shape = (groups // 2, len(ROW_SHIFTS) * slots)
    scratch = pltpu.VMEM((groups // 2, 4 * LANES), F32)
    give, weights, total = call(
        give_kernel,
        (
            shape((half_count, pixels + LANES), F32),
            shape(weight_shape, BF16),
            shape((half_count, LANES), F32),
        ),
        4,
        8,
        [pltpu.VMEM(weight_shape, BF16), scratch],
        flops=work // 2,
        moved=5 * MIB,
    )(scores, x, tile, everyone)
    other = lax.ppermute(give, "dp", [(0, 1), (1, 0)])
    keep = call(
        keep_kernel,
        shape((half_count, pixels), F32),
        2,
        8,
        [scratch],
        flops=work // 2,
        moved=4 * MIB,
    )(weights, x)
    sums, totals = call(
        finish_kernel,
        (shape((half_rots * tiles, LANES), F32), shape((1, half_rots), F32)),
        3,
        8,
        moved=2 * MIB,
    )(keep, total, other)
    return sums.reshape(1, half_rots, pixels), totals


def solution(mesh):
    split = (PLANES, mesh.shape["cls"] // PLANES, mesh.shape["dp"])
    cube = Mesh(mesh.devices.reshape(split), ("z", "xy", "dp"))
    every = ("z", "xy", "dp")
    by_class = ("z", "xy")
    return jax.shard_map(
        on_device,
        mesh=cube,
        in_specs=(P(every, None), P(by_class, None, None), P(every, None), P(every)),
        out_specs=(P(by_class, "dp", None), P(by_class, "dp")),
        check_vma=False,
    )
```

```python
import functools
import math

import jax
import jax.numpy as jnp
from jax import lax
from jax.experimental import pallas as pl
from jax.experimental.pallas import tpu as pltpu
from jax.sharding import Mesh
from jax.sharding import PartitionSpec as P

LANES = 128
SLOTS = 2
PLANES = 8
FAR = 1e30
ROW_SHIFTS = (0, 1, -1)
COL_SHIFTS = (0, 1, -1)
MIB = 1024 * 1024
F32, BF16 = jnp.float32, jnp.bfloat16


def tile_of(t):
    return slice(t * LANES, (t + 1) * LANES)


def lane_row():
    return lax.broadcasted_iota(jnp.int32, (1, LANES), 1)


def fold_tile(load, q, tiles, low):
    first, second = load(q // 2), load(tiles // 2 + q // 2)
    half = LANES // 2
    if q % 2 == 0:
        return jnp.where(low, first, pltpu.roll(second, half, 1))
    return jnp.where(low, pltpu.roll(first, half, 1), second)


def unfold_tile(load, t, tiles, low):
    half = LANES // 2
    if t < tiles // 2:
        return jnp.where(low, load(2 * t), pltpu.roll(load(2 * t + 1), half, 1))
    first = 2 * t - tiles
    return jnp.where(low, pltpu.roll(load(first), half, 1), load(first + 1))


def pack_kernel(cand_at, noise_at, img_at, send_ref, cand_ref, noise_ref, img_ref, sems):
    pairs = ((cand_at, cand_ref), (noise_at, noise_ref), (img_at, img_ref))
    loads = [pltpu.make_async_copy(at, ref, sems.at[i]) for i, (at, ref) in enumerate(pairs)]
    for load in loads:
        load.start()
    for load in loads:
        load.wait()
    top, rows = cand_ref.shape
    tiles = img_ref.shape[1] // LANES
    low = lane_row() < LANES // 2
    row_id = lax.broadcasted_iota(jnp.int32, (rows, LANES), 0)
    lane_id = lax.broadcasted_iota(jnp.int32, (rows, LANES), 1)
    diagonal = lax.broadcasted_iota(jnp.int32, (rows, rows), 0) == lax.broadcasted_iota(
        jnp.int32, (rows, rows), 1
    )
    noise = jnp.sum(
        jnp.where(diagonal, noise_ref[...].astype(F32), 0.0), axis=1, keepdims=True
    )
    place = lax.broadcasted_iota(jnp.int32, (top, LANES), 1) == (
        lax.broadcasted_iota(jnp.int32, (top, LANES), 0) + 2
    )
    facts = lax.dot_general(
        cand_ref[...].astype(F32).astype(BF16),
        place.astype(F32).astype(BF16),
        (((0,), (0,)), ((), ())),
        preferred_element_type=F32,
    )
    facts = jnp.where(lane_id == 0, noise, facts)
    facts = jnp.where(lane_id == 1, (row_id + 1).astype(F32), facts)
    send_ref[tiles * rows :] = facts.astype(BF16)
    for q in range(tiles):
        tile = fold_tile(lambda t: img_ref[:, tile_of(t)].astype(F32), q, tiles, low)
        send_ref[q * rows : (q + 1) * rows] = tile.astype(BF16)


def pick_kernel(*refs, steps, top):
    planes = len(steps) - 1
    recv_refs, send_ref, column_ref = refs[: len(steps)], refs[-2], refs[-1]
    owners, depth, _ = send_ref.shape
    rows = column_ref.shape[0] // planes
    tiles = column_ref.shape[1] // LANES
    group = depth // tiles
    slots = owners * group
    cut = recv_refs[-2].shape[0] // rows
    for j in range(planes):
        for t in range(tiles):
            from_ref, at = recv_refs[j], t
            if j == planes - 1 and t >= cut:
                from_ref, at = recv_refs[j + 1], t - cut
            column_ref[j * rows : (j + 1) * rows, tile_of(t)] = from_ref[
                at * rows : (at + 1) * rows
            ]
    count = planes * rows
    facts = column_ref[:, tile_of(tiles - 1)].astype(F32)
    here = lax.axis_index("z")
    row = lax.broadcasted_iota(jnp.int32, (count, 1), 0)
    sender = jnp.zeros((count, 1), jnp.int32)
    for j in range(planes):
        plane = lax.rem(here + steps[j] + planes, planes)
        sender = jnp.where(row // rows == j, plane, sender)
    lane = lax.broadcasted_iota(jnp.int32, (1, slots), 1)
    cls = (here * owners + lane // group).astype(F32)
    member = facts[:, 2:3] == cls
    for k in range(1, top):
        member = member | (facts[:, 2 + k : 3 + k] == cls)
    one, other = (lax.broadcasted_iota(jnp.int32, (count, count), i) for i in range(2))
    earlier = (one > other) & (one // rows == other // rows)
    before = jnp.dot(
        earlier.astype(F32).astype(BF16),
        member.astype(F32).astype(BF16),
        preferred_element_type=F32,
    )
    slot = (lane // planes) % SLOTS
    pick = member & (before == slot.astype(F32)) & (lane % planes == sender)
    pick = pick.astype(F32).T.astype(BF16)
    width = 3
    for t in range(0, tiles, width):
        lanes = slice(t * LANES, (t + width) * LANES)
        got = jnp.dot(pick, column_ref[:, lanes], preferred_element_type=F32).astype(BF16)
        for i in range(width):
            for c in range(owners):
                send_ref[c, (t + i) * group : (t + i + 1) * group] = got[
                    c * group : (c + 1) * group, tile_of(i)
                ]


def shift_kernel(from_at, out_ref, half_ref, from_ref, rot_ref, sem):
    load = pltpu.make_async_copy(from_at, from_ref, sem)
    load.start()
    load.wait()
    count, pixels = rot_ref.shape
    rots = from_ref.shape[0]
    half_count, half_rots = count // 2, rots // 2
    to = lax.broadcasted_iota(jnp.int32, (count, rots), 0)
    place = jnp.where(to < half_count, to, to - half_count + half_rots)
    real = to % half_count < half_rots
    own_first = lax.axis_index("dp") * half_rots
    place = jnp.where(place + own_first < rots, place + own_first, place + own_first - rots)
    chosen = (place == lax.broadcasted_iota(jnp.int32, (count, rots), 1)) & real
    picked = jnp.dot(chosen.astype(F32).astype(BF16), from_ref[...], preferred_element_type=F32)
    half = 0.5 * jnp.sum(picked * picked, axis=1, keepdims=True)
    half_ref[...] = jnp.broadcast_to(half, half_ref.shape)
    rot_ref[...] = picked.astype(BF16)
    tiles = pixels // LANES
    side = LANES // 2
    groups = len(COL_SHIFTS) * count
    source = lax.broadcasted_iota(jnp.int32, (2 * LANES, LANES), 0)
    lane = lax.broadcasted_iota(jnp.int32, (2 * LANES, LANES), 1)
    moves = []
    for parity in range(2):
        for shift in COL_SHIFTS:
            col = (lane - shift + side) % side
            home = (lane // side) * LANES + parity * side + col
            moves.append((source == home).astype(F32).astype(BF16))
    moves = jnp.concatenate(moves, axis=1)
    turn = ((lane[:LANES] + side) % LANES == source[:LANES]).astype(F32).astype(BF16)
    for h in range(tiles // 2):
        pair = jnp.concatenate(
            [rot_ref[:, tile_of(h)], rot_ref[:, tile_of(tiles // 2 + h)]], axis=1
        )
        moved = jnp.dot(pair, moves, preferred_element_type=F32).astype(BF16)
        for parity in range(2):
            for i in range(len(COL_SHIFTS)):
                plain = moved[:, tile_of(parity * len(COL_SHIFTS) + i)]
                for j, shift in enumerate(ROW_SHIFTS):
                    at = 2 * h + parity + shift
                    value = plain
                    if not 0 <= at < tiles:
                        at = at % tiles
                        value = jnp.dot(plain, turn, preferred_element_type=F32).astype(BF16)
                    first = j * groups + i * count
                    out_ref[first : first + count, tile_of(at)] = value


def score_kernel(recv_ref, shifted_ref, half_ref, x_ref, s_ref, tile_ref, *, pad):
    owners, depth, _ = recv_ref.shape
    tiles = x_ref.shape[1] // LANES - 2
    group = depth // (tiles + 1)
    slots = owners * group
    groups = s_ref.shape[0]
    count = half_ref.shape[0]
    for c in range(owners):
        for t in range(tiles):
            x_ref[c * group : (c + 1) * group, tile_of(t + 1)] = recv_ref[
                c, t * group : (t + 1) * group
            ]
    half_turn = LANES // 2
    x_ref[:, tile_of(0)] = pltpu.roll(x_ref[:, tile_of(tiles)].astype(F32), half_turn, 1).astype(
        BF16
    )
    x_ref[:, tile_of(tiles + 1)] = pltpu.roll(x_ref[:, tile_of(1)].astype(F32), half_turn, 1).astype(
        BF16
    )
    facts = recv_ref[:, tiles * group :, :].reshape(slots, LANES)
    choose = (
        lax.broadcasted_iota(jnp.int32, (16, LANES), 0)
        == lax.broadcasted_iota(jnp.int32, (16, LANES), 1)
    ).astype(F32).astype(BF16)
    turned = lax.dot_general(
        choose, facts, (((1,), (1,)), ((), ())), preferred_element_type=F32
    )
    noise, number = turned[0:1], turned[1:2]
    products = lax.dot_general(
        shifted_ref[...],
        x_ref[:, LANES : (tiles + 1) * LANES],
        (((1,), (1,)), ((), ())),
        preferred_element_type=F32,
    )
    half = half_ref[:, 0:1]
    row = lax.broadcasted_iota(jnp.int32, half.shape, 0)
    half = jnp.where(row % (count // 2) >= count // 2 - pad, FAR, half)
    half = jnp.concatenate([half] * len(COL_SHIFTS), axis=0)
    peak = None
    for i in range(len(ROW_SHIFTS)):
        scores = noise * (products[i * groups : (i + 1) * groups] - half)
        s_ref[:, i * slots : (i + 1) * slots] = scores
        top = jnp.max(scores, axis=0, keepdims=True)
        peak = top if peak is None else jnp.maximum(peak, top)
    total = jnp.zeros_like(peak)
    for i in range(len(ROW_SHIFTS)):
        scores = s_ref[:, i * slots : (i + 1) * slots]
        total = total + jnp.sum(jnp.exp(scores - peak), axis=0, keepdims=True)
    parts = slots // LANES
    for i, value in enumerate((peak, total, number)):
        for h in range(parts):
            tile_ref[0, i * parts + h : i * parts + h + 1] = value[:, tile_of(h)]
    tile_ref[0, 3 * parts :] = jnp.zeros_like(tile_ref[0, 3 * parts :])
    for i in range(1, tile_ref.shape[0]):
        tile_ref[i] = tile_ref[0]


def partner_of(rows):
    second = (lane_row() // PLANES) % SLOTS == 1
    return jnp.where(
        second, pltpu.roll(rows, PLANES, 1), pltpu.roll(rows, LANES - PLANES, 1)
    )


def fold_kernel(shown_ref, out_ref):
    planes = shown_ref.shape[0]
    rows = out_ref.shape[1] // 2
    second = (lane_row() // PLANES) % SLOTS == 1
    parts = 2
    shown = [
        [
            jnp.concatenate(
                [shown_ref[z, i * parts + h : i * parts + h + 1] for z in range(planes)], axis=0
            )
            for h in range(parts)
        ]
        for i in range(3)
    ]
    for p in range(rows):
        found = []
        for h in range(parts):
            same = shown[2][h] == p + 1
            peak = jnp.max(jnp.where(same, shown[0][h], -FAR), axis=0, keepdims=True)
            peak = jnp.maximum(peak, partner_of(peak))
            part = shown[1][h] * jnp.exp(jnp.minimum(shown[0][h] - peak, 0.0))
            total = jnp.sum(jnp.where(same, part, 0.0), axis=0, keepdims=True)
            found.append((peak, total + partner_of(total)))
        out_ref[0, p : p + 1] = jnp.where(second, found[1][0], found[0][0])
        out_ref[0, rows + p : rows + p + 1] = jnp.where(second, found[1][1], found[0][1])
    for i in range(1, out_ref.shape[0]):
        out_ref[i] = out_ref[0]


def sum_half(w_ref, x_ref, out_ref, y_ref):
    slots = x_ref.shape[0]
    pixels = x_ref.shape[1] - 2 * LANES
    count = y_ref.shape[0] // len(COL_SHIFTS)
    side = LANES // 2
    width = y_ref.shape[1]
    column = lane_row() % side
    for first in range(0, pixels, width):
        y_ref[...] = sum(
            jnp.dot(
                w_ref[:, i * slots : (i + 1) * slots],
                x_ref[:, (1 + shift) * LANES + first : (1 + shift) * LANES + first + width],
                preferred_element_type=F32,
            )
            for i, shift in enumerate(ROW_SHIFTS)
        )
        for t in range(width // LANES):
            plain = y_ref[:count, tile_of(t)]
            right = y_ref[count : 2 * count, tile_of(t)]
            left = y_ref[2 * count :, tile_of(t)]
            back = jnp.where(
                column == side - 1,
                pltpu.roll(right, side - 1, 1),
                pltpu.roll(right, LANES - 1, 1),
            )
            forth = jnp.where(
                column == 0, pltpu.roll(left, LANES - side + 1, 1), pltpu.roll(left, 1, 1)
            )
            out_ref[:, first + t * LANES : first + (t + 1) * LANES] = plain + back + forth


def give_kernel(s_ref, x_ref, mine_ref, all_ref, give_ref, w_ref, total_ref, w_give_ref, y_ref):
    groups = s_ref.shape[0]
    slots = x_ref.shape[0]
    pixels = x_ref.shape[1] - 2 * LANES
    rows = all_ref.shape[1] // 2
    count = groups // len(COL_SHIFTS)
    half_count = count // 2
    parts = slots // LANES
    second = (lane_row() // PLANES) % SLOTS == 1
    tables = range(all_ref.shape[0])
    peak = all_ref[0, :rows]
    for i in tables:
        peak = jnp.maximum(peak, all_ref[i, :rows])
    total = jnp.zeros_like(peak)
    for i in tables:
        total = total + all_ref[i, rows:] * jnp.exp(all_ref[i, :rows] - peak)
    number = lax.broadcasted_iota(jnp.int32, (rows, LANES), 0).astype(F32) + 1
    peaks, scales = [], []
    for h in range(parts):
        own = mine_ref[0, 2 * parts + h : 2 * parts + h + 1]
        here = second == (h == 1)
        mine = [
            jnp.sum(
                jnp.where(number == own, jnp.where(here, table, partner_of(table)), 0.0),
                axis=0,
                keepdims=True,
            )
            for table in (peak, total)
        ]
        peaks.append(mine[0])
        scales.append(jnp.where(own > 0, 1.0 / jnp.where(own > 0, mine[1], 1.0), 0.0))
    peak = jnp.concatenate(peaks, axis=1)
    scale = jnp.concatenate(scales, axis=1)
    for half, to_ref, sums_ref in ((0, w_ref, total_ref), (1, w_give_ref, give_ref.at[:, pixels:])):
        class_total = jnp.zeros((half_count, 1), F32)
        for i in range(len(ROW_SHIFTS)):
            part = slice(i * slots, (i + 1) * slots)
            for j in range(len(COL_SHIFTS)):
                first = j * count + half * half_count
                weights = s_ref[first : first + half_count, part]
                weights = jnp.exp(jnp.minimum(weights - peak, 0.0)) * scale
                weights = weights.astype(BF16).astype(F32)
                class_total = class_total + jnp.sum(weights, axis=1, keepdims=True)
                y_ref[j * half_count : (j + 1) * half_count, :slots] = weights
            to_ref[:, part] = y_ref[:, :slots].astype(BF16)
        sums_ref[...] = jnp.broadcast_to(class_total, (half_count, LANES))
    sum_half(w_give_ref, x_ref, give_ref, y_ref)


def keep_kernel(w_ref, x_ref, keep_ref, y_ref):
    sum_half(w_ref, x_ref, keep_ref, y_ref)


def finish_kernel(keep_ref, total_ref, other_ref, sums_ref, totals_ref):
    rots = totals_ref.shape[1]
    tiles = sums_ref.shape[0] // rots
    low = lane_row() < LANES // 2

    def load(t):
        return keep_ref[:rots, tile_of(t)] + other_ref[:rots, tile_of(t)]

    for t in range(tiles):
        sums_ref[pl.ds(t, rots, stride=tiles), :] = unfold_tile(load, t, tiles, low)
    total = total_ref[:rots] + other_ref[:rots, tile_of(tiles)]
    here = lax.broadcasted_iota(jnp.int32, (rots, LANES), 0) == lax.broadcasted_iota(
        jnp.int32, (rots, LANES), 1
    )
    totals_ref[...] = jnp.sum(jnp.where(here, total, 0.0), axis=0, keepdims=True)[:, :rots]


def far_away(value):
    return pltpu.with_memory_space_constraint(value, pltpu.HBM)


def call(kernel, out_shape, count, limit, scratch=(), flops=0, moved=0, far=0):
    in_vmem = pl.BlockSpec(memory_space=pltpu.VMEM)
    return pl.pallas_call(
        kernel,
        out_shape=out_shape,
        in_specs=[pl.BlockSpec(memory_space=pltpu.HBM)] * far + [in_vmem] * (count - far),
        out_specs=jax.tree.map(lambda _: in_vmem, out_shape),
        scratch_shapes=list(scratch),
        cost_estimate=pl.CostEstimate(flops=flops, bytes_accessed=moved, transcendentals=0),
        compiler_params=pltpu.CompilerParams(vmem_limit_bytes=limit * MIB),
    )


def on_device(images, references, candidates, inv_noise):
    rows, top = candidates.shape
    cls_dev, rots, pixels = references.shape
    planes, owners = lax.axis_size("z"), lax.axis_size("xy")
    side = math.isqrt(pixels)
    tiles = pixels // LANES
    group = SLOTS * planes
    slots = owners * group
    assert cls_dev == 1 and planes == PLANES and LANES == 2 * side and rows == group
    shape = jax.ShapeDtypeStruct
    exchange = functools.partial(lax.all_to_all, split_axis=0, concat_axis=0, tiled=True)

    packed = call(
        pack_kernel,
        shape(((tiles + 1) * rows, LANES), BF16),
        3,
        4,
        [
            pltpu.VMEM((top, rows), jnp.int32),
            pltpu.VMEM((1, rows), BF16),
            pltpu.VMEM((rows, pixels), BF16),
            pltpu.SemaphoreType.DMA((3,)),
        ],
        moved=MIB // 4,
        far=3,
    )(far_away(candidates.T), far_away(inv_noise[None, :]), far_away(images))

    def move(part, step):
        return lax.ppermute(part, "z", [(i, (i + step) % planes) for i in range(planes)])

    near = [move(packed, step) for step in (1, -1)]
    next_near = [move(packed, step) for step in (2, -2)]
    half_rots = rots // 2
    half_count = -(-half_rots // 8) * 8
    pad = half_count - half_rots
    count = 2 * half_count
    groups = len(COL_SHIFTS) * count
    shifted, half_norm = call(
        shift_kernel,
        (shape((len(ROW_SHIFTS) * groups, pixels), BF16), shape((count, LANES), F32)),
        1,
        6,
        [
            pltpu.VMEM((rots, pixels), BF16),
            pltpu.VMEM((count, pixels), BF16),
            pltpu.SemaphoreType.DMA,
        ],
        moved=12 * MIB,
        far=1,
    )(far_away(references[0]))
    next_near, shifted, half_norm = lax.optimization_barrier((next_near, shifted, half_norm))
    cut = (tiles + 1) // 2 * rows
    far = [move(next_near[0], 1), move(next_near[1], -1)]
    far += [move(next_near[0][:cut], 2), move(next_near[1][cut:], -2)]
    column = [packed, *near, *next_near, *far]
    steps = [0, -1, 1, -2, 2, -3, 3, 4, 4]
    picked = call(
        functools.partial(pick_kernel, steps=steps, top=top),
        shape((owners, (tiles + 1) * group, LANES), BF16),
        len(column),
        6,
        [pltpu.VMEM((planes * rows, (tiles + 1) * LANES), BF16)],
        moved=3 * MIB,
    )(*column)
    received = exchange(picked, "xy")
    work = 2 * len(ROW_SHIFTS) * groups * slots * pixels
    x, scores, tile = call(
        functools.partial(score_kernel, pad=pad),
        (
            shape((slots, pixels + 2 * LANES), BF16),
            shape((groups, len(ROW_SHIFTS) * slots), F32),
            shape((planes, 8, LANES), F32),
        ),
        3,
        8,
        flops=work,
        moved=10 * MIB,
    )(received, shifted, half_norm)
    folded = call(
        fold_kernel, shape((owners, 2 * rows, LANES), F32), 1, 4, moved=MIB // 4
    )(exchange(tile, "z"))
    everyone = exchange(folded, "xy")
    weight_shape = (groups // 2, len(ROW_SHIFTS) * slots)
    scratch = pltpu.VMEM((groups // 2, 4 * LANES), F32)
    give, weights, total = call(
        give_kernel,
        (
            shape((half_count, pixels + LANES), F32),
            shape(weight_shape, BF16),
            shape((half_count, LANES), F32),
        ),
        4,
        8,
        [pltpu.VMEM(weight_shape, BF16), scratch],
        flops=work // 2,
        moved=5 * MIB,
    )(scores, x, tile, everyone)
    other = lax.ppermute(give, "dp", [(0, 1), (1, 0)])
    keep = call(
        keep_kernel,
        shape((half_count, pixels), F32),
        2,
        8,
        [scratch],
        flops=work // 2,
        moved=4 * MIB,
    )(weights, x)
    sums, totals = call(
        finish_kernel,
        (shape((half_rots * tiles, LANES), F32), shape((1, half_rots), F32)),
        3,
        8,
        moved=2 * MIB,
    )(keep, total, other)
    return sums.reshape(1, half_rots, pixels), totals


def solution(mesh):
    split = (PLANES, mesh.shape["cls"] // PLANES, mesh.shape["dp"])
    cube = Mesh(mesh.devices.reshape(split), ("z", "xy", "dp"))
    every = ("z", "xy", "dp")
    by_class = ("z", "xy")
    return jax.shard_map(
        on_device,
        mesh=cube,
        in_specs=(P(every, None), P(by_class, None, None), P(every, None), P(every)),
        out_specs=(P(by_class, "dp", None), P(by_class, "dp")),
        check_vma=False,
    )
```

```python
import functools
import math

import jax
import jax.numpy as jnp
from jax import lax
from jax.experimental import pallas as pl
from jax.experimental.pallas import tpu as pltpu
from jax.sharding import Mesh
from jax.sharding import PartitionSpec as P

LANES = 128
SLOTS = 2
PLANES = 8
FAR = 1e30
ROW_SHIFTS = (0, 1, -1)
COL_SHIFTS = (0, 1, -1)
MIB = 1024 * 1024
F32, BF16 = jnp.float32, jnp.bfloat16


def tile_of(t):
    return slice(t * LANES, (t + 1) * LANES)


def lane_row():
    return lax.broadcasted_iota(jnp.int32, (1, LANES), 1)


def fold_tile(load, q, tiles, low):
    first, second = load(q // 2), load(tiles // 2 + q // 2)
    half = LANES // 2
    if q % 2 == 0:
        return jnp.where(low, first, pltpu.roll(second, half, 1))
    return jnp.where(low, pltpu.roll(first, half, 1), second)


def unfold_tile(load, t, tiles, low):
    half = LANES // 2
    if t < tiles // 2:
        return jnp.where(low, load(2 * t), pltpu.roll(load(2 * t + 1), half, 1))
    first = 2 * t - tiles
    return jnp.where(low, pltpu.roll(load(first), half, 1), load(first + 1))


def pack_kernel(cand_at, noise_at, img_at, send_ref, cand_ref, noise_ref, img_ref, sems):
    pairs = ((cand_at, cand_ref), (noise_at, noise_ref), (img_at, img_ref))
    loads = [pltpu.make_async_copy(at, ref, sems.at[i]) for i, (at, ref) in enumerate(pairs)]
    for load in loads:
        load.start()
    for load in loads:
        load.wait()
    top, rows = cand_ref.shape
    tiles = img_ref.shape[1] // LANES
    low = lane_row() < LANES // 2
    row_id = lax.broadcasted_iota(jnp.int32, (rows, LANES), 0)
    lane_id = lax.broadcasted_iota(jnp.int32, (rows, LANES), 1)
    diagonal = lax.broadcasted_iota(jnp.int32, (rows, rows), 0) == lax.broadcasted_iota(
        jnp.int32, (rows, rows), 1
    )
    noise = jnp.sum(
        jnp.where(diagonal, noise_ref[...].astype(F32), 0.0), axis=1, keepdims=True
    )
    place = lax.broadcasted_iota(jnp.int32, (top, LANES), 1) == (
        lax.broadcasted_iota(jnp.int32, (top, LANES), 0) + 2
    )
    facts = lax.dot_general(
        cand_ref[...].astype(F32).astype(BF16),
        place.astype(F32).astype(BF16),
        (((0,), (0,)), ((), ())),
        preferred_element_type=F32,
    )
    facts = jnp.where(lane_id == 0, noise, facts)
    facts = jnp.where(lane_id == 1, (row_id + 1).astype(F32), facts)
    send_ref[tiles * rows :] = facts.astype(BF16)
    for q in range(tiles):
        tile = fold_tile(lambda t: img_ref[:, tile_of(t)].astype(F32), q, tiles, low)
        send_ref[q * rows : (q + 1) * rows] = tile.astype(BF16)


def pick_kernel(*refs, steps, top):
    planes = len(steps) - 1
    recv_refs, send_ref, column_ref = refs[: len(steps)], refs[-2], refs[-1]
    owners, depth, _ = send_ref.shape
    rows = column_ref.shape[0] // planes
    tiles = column_ref.shape[1] // LANES
    group = depth // tiles
    slots = owners * group
    cut = recv_refs[-2].shape[0] // rows
    for j in range(planes):
        for t in range(tiles):
            from_ref, at = recv_refs[j], t
            if j == planes - 1 and t >= cut:
                from_ref, at = recv_refs[j + 1], t - cut
            column_ref[j * rows : (j + 1) * rows, tile_of(t)] = from_ref[
                at * rows : (at + 1) * rows
            ]
    count = planes * rows
    facts = column_ref[:, tile_of(tiles - 1)].astype(F32)
    here = lax.axis_index("z")
    row = lax.broadcasted_iota(jnp.int32, (count, 1), 0)
    sender = jnp.zeros((count, 1), jnp.int32)
    for j in range(planes):
        plane = lax.rem(here + steps[j] + planes, planes)
        sender = jnp.where(row // rows == j, plane, sender)
    lane = lax.broadcasted_iota(jnp.int32, (1, slots), 1)
    cls = (here * owners + lane // group).astype(F32)
    member = facts[:, 2:3] == cls
    for k in range(1, top):
        member = member | (facts[:, 2 + k : 3 + k] == cls)
    one, other = (lax.broadcasted_iota(jnp.int32, (count, count), i) for i in range(2))
    earlier = (one > other) & (one // rows == other // rows)
    before = jnp.dot(
        earlier.astype(F32).astype(BF16),
        member.astype(F32).astype(BF16),
        preferred_element_type=F32,
    )
    slot = (lane // planes) % SLOTS
    pick = member & (before == slot.astype(F32)) & (lane % planes == sender)
    pick = pick.astype(F32).T.astype(BF16)
    width = 3
    for t in range(0, tiles, width):
        lanes = slice(t * LANES, (t + width) * LANES)
        got = jnp.dot(pick, column_ref[:, lanes], preferred_element_type=F32).astype(BF16)
        for i in range(width):
            for c in range(owners):
                send_ref[c, (t + i) * group : (t + i + 1) * group] = got[
                    c * group : (c + 1) * group, tile_of(i)
                ]


def shift_kernel(from_at, out_ref, half_ref, from_ref, rot_ref, sem):
    load = pltpu.make_async_copy(from_at, from_ref, sem)
    load.start()
    load.wait()
    count, pixels = rot_ref.shape
    rots = from_ref.shape[0]
    half_count, half_rots = count // 2, rots // 2
    to = lax.broadcasted_iota(jnp.int32, (count, rots), 0)
    place = jnp.where(to < half_count, to, to - half_count + half_rots)
    real = to % half_count < half_rots
    own_first = lax.axis_index("dp") * half_rots
    place = jnp.where(place + own_first < rots, place + own_first, place + own_first - rots)
    chosen = (place == lax.broadcasted_iota(jnp.int32, (count, rots), 1)) & real
    picked = jnp.dot(chosen.astype(F32).astype(BF16), from_ref[...], preferred_element_type=F32)
    half = 0.5 * jnp.sum(picked * picked, axis=1, keepdims=True)
    half_ref[...] = jnp.broadcast_to(half, half_ref.shape)
    rot_ref[...] = picked.astype(BF16)
    tiles = pixels // LANES
    side = LANES // 2
    groups = len(COL_SHIFTS) * count
    source = lax.broadcasted_iota(jnp.int32, (2 * LANES, LANES), 0)
    lane = lax.broadcasted_iota(jnp.int32, (2 * LANES, LANES), 1)
    moves = []
    for parity in range(2):
        for shift in COL_SHIFTS:
            col = (lane - shift + side) % side
            home = (lane // side) * LANES + parity * side + col
            moves.append((source == home).astype(F32).astype(BF16))
    moves = jnp.concatenate(moves, axis=1)
    turn = ((lane[:LANES] + side) % LANES == source[:LANES]).astype(F32).astype(BF16)
    for h in range(tiles // 2):
        pair = jnp.concatenate(
            [rot_ref[:, tile_of(h)], rot_ref[:, tile_of(tiles // 2 + h)]], axis=1
        )
        moved = jnp.dot(pair, moves, preferred_element_type=F32).astype(BF16)
        for parity in range(2):
            for i in range(len(COL_SHIFTS)):
                plain = moved[:, tile_of(parity * len(COL_SHIFTS) + i)]
                for j, shift in enumerate(ROW_SHIFTS):
                    at = 2 * h + parity + shift
                    value = plain
                    if not 0 <= at < tiles:
                        at = at % tiles
                        value = jnp.dot(plain, turn, preferred_element_type=F32).astype(BF16)
                    first = j * groups + i * count
                    out_ref[first : first + count, tile_of(at)] = value


def score_kernel(recv_ref, shifted_ref, half_ref, x_ref, s_ref, tile_ref, *, pad):
    owners, depth, _ = recv_ref.shape
    tiles = x_ref.shape[1] // LANES - 2
    group = depth // (tiles + 1)
    slots = owners * group
    groups = s_ref.shape[0]
    count = half_ref.shape[0]
    for c in range(owners):
        for t in range(tiles):
            x_ref[c * group : (c + 1) * group, tile_of(t + 1)] = recv_ref[
                c, t * group : (t + 1) * group
            ]
    half_turn = LANES // 2
    x_ref[:, tile_of(0)] = pltpu.roll(x_ref[:, tile_of(tiles)].astype(F32), half_turn, 1).astype(
        BF16
    )
    x_ref[:, tile_of(tiles + 1)] = pltpu.roll(x_ref[:, tile_of(1)].astype(F32), half_turn, 1).astype(
        BF16
    )
    facts = recv_ref[:, tiles * group :, :].reshape(slots, LANES)
    choose = (
        lax.broadcasted_iota(jnp.int32, (16, LANES), 0)
        == lax.broadcasted_iota(jnp.int32, (16, LANES), 1)
    ).astype(F32).astype(BF16)
    turned = lax.dot_general(
        choose, facts, (((1,), (1,)), ((), ())), preferred_element_type=F32
    )
    noise, number = turned[0:1], turned[1:2]
    products = lax.dot_general(
        shifted_ref[...],
        x_ref[:, LANES : (tiles + 1) * LANES],
        (((1,), (1,)), ((), ())),
        preferred_element_type=F32,
    )
    half = half_ref[:, 0:1]
    row = lax.broadcasted_iota(jnp.int32, half.shape, 0)
    half = jnp.where(row % (count // 2) >= count // 2 - pad, FAR, half)
    half = jnp.concatenate([half] * len(COL_SHIFTS), axis=0)
    peak = None
    for i in range(len(ROW_SHIFTS)):
        scores = noise * (products[i * groups : (i + 1) * groups] - half)
        s_ref[:, i * slots : (i + 1) * slots] = scores
        top = jnp.max(scores, axis=0, keepdims=True)
        peak = top if peak is None else jnp.maximum(peak, top)
    total = jnp.zeros_like(peak)
    for i in range(len(ROW_SHIFTS)):
        scores = s_ref[:, i * slots : (i + 1) * slots]
        total = total + jnp.sum(jnp.exp(scores - peak), axis=0, keepdims=True)
    parts = slots // LANES
    for i, value in enumerate((peak, total, number)):
        for h in range(parts):
            tile_ref[0, i * parts + h : i * parts + h + 1] = value[:, tile_of(h)]
    tile_ref[0, 3 * parts :] = jnp.zeros_like(tile_ref[0, 3 * parts :])
    for i in range(1, tile_ref.shape[0]):
        tile_ref[i] = tile_ref[0]


def partner_of(rows):
    second = (lane_row() // PLANES) % SLOTS == 1
    return jnp.where(
        second, pltpu.roll(rows, PLANES, 1), pltpu.roll(rows, LANES - PLANES, 1)
    )


def fold_kernel(shown_ref, out_ref):
    planes = shown_ref.shape[0]
    rows = out_ref.shape[1] // 2
    second = (lane_row() // PLANES) % SLOTS == 1
    parts = 2
    shown = [
        [
            jnp.concatenate(
                [shown_ref[z, i * parts + h : i * parts + h + 1] for z in range(planes)], axis=0
            )
            for h in range(parts)
        ]
        for i in range(3)
    ]
    for p in range(rows):
        found = []
        for h in range(parts):
            same = shown[2][h] == p + 1
            peak = jnp.max(jnp.where(same, shown[0][h], -FAR), axis=0, keepdims=True)
            peak = jnp.maximum(peak, partner_of(peak))
            part = shown[1][h] * jnp.exp(jnp.minimum(shown[0][h] - peak, 0.0))
            total = jnp.sum(jnp.where(same, part, 0.0), axis=0, keepdims=True)
            found.append((peak, total + partner_of(total)))
        out_ref[0, p : p + 1] = jnp.where(second, found[1][0], found[0][0])
        out_ref[0, rows + p : rows + p + 1] = jnp.where(second, found[1][1], found[0][1])
    for i in range(1, out_ref.shape[0]):
        out_ref[i] = out_ref[0]


def sum_half(w_ref, x_ref, out_ref, y_ref):
    slots = x_ref.shape[0]
    pixels = x_ref.shape[1] - 2 * LANES
    count = y_ref.shape[0] // len(COL_SHIFTS)
    side = LANES // 2
    width = y_ref.shape[1]
    column = lane_row() % side
    for first in range(0, pixels, width):
        y_ref[...] = sum(
            jnp.dot(
                w_ref[:, i * slots : (i + 1) * slots],
                x_ref[:, (1 + shift) * LANES + first : (1 + shift) * LANES + first + width],
                preferred_element_type=F32,
            )
            for i, shift in enumerate(ROW_SHIFTS)
        )
        for t in range(width // LANES):
            plain = y_ref[:count, tile_of(t)]
            right = y_ref[count : 2 * count, tile_of(t)]
            left = y_ref[2 * count :, tile_of(t)]
            back = jnp.where(
                column == side - 1,
                pltpu.roll(right, side - 1, 1),
                pltpu.roll(right, LANES - 1, 1),
            )
            forth = jnp.where(
                column == 0, pltpu.roll(left, LANES - side + 1, 1), pltpu.roll(left, 1, 1)
            )
            out_ref[:, first + t * LANES : first + (t + 1) * LANES] = plain + back + forth


def give_kernel(s_ref, x_ref, mine_ref, all_ref, give_ref, w_ref, total_ref, w_give_ref, y_ref):
    groups = s_ref.shape[0]
    slots = x_ref.shape[0]
    pixels = x_ref.shape[1] - 2 * LANES
    rows = all_ref.shape[1] // 2
    count = groups // len(COL_SHIFTS)
    half_count = count // 2
    parts = slots // LANES
    second = (lane_row() // PLANES) % SLOTS == 1
    tables = range(all_ref.shape[0])
    peak = all_ref[0, :rows]
    for i in tables:
        peak = jnp.maximum(peak, all_ref[i, :rows])
    total = jnp.zeros_like(peak)
    for i in tables:
        total = total + all_ref[i, rows:] * jnp.exp(all_ref[i, :rows] - peak)
    number = lax.broadcasted_iota(jnp.int32, (rows, LANES), 0).astype(F32) + 1
    peaks, scales = [], []
    for h in range(parts):
        own = mine_ref[0, 2 * parts + h : 2 * parts + h + 1]
        here = second == (h == 1)
        mine = [
            jnp.sum(
                jnp.where(number == own, jnp.where(here, table, partner_of(table)), 0.0),
                axis=0,
                keepdims=True,
            )
            for table in (peak, total)
        ]
        peaks.append(mine[0])
        scales.append(jnp.where(own > 0, 1.0 / jnp.where(own > 0, mine[1], 1.0), 0.0))
    peak = jnp.concatenate(peaks, axis=1)
    scale = jnp.concatenate(scales, axis=1)
    for half, to_ref, sums_ref in ((0, w_ref, total_ref), (1, w_give_ref, give_ref.at[:, pixels:])):
        class_total = jnp.zeros((half_count, 1), F32)
        for i in range(len(ROW_SHIFTS)):
            part = slice(i * slots, (i + 1) * slots)
            for j in range(len(COL_SHIFTS)):
                first = j * count + half * half_count
                weights = s_ref[first : first + half_count, part]
                weights = jnp.exp(jnp.minimum(weights - peak, 0.0)) * scale
                weights = weights.astype(BF16).astype(F32)
                class_total = class_total + jnp.sum(weights, axis=1, keepdims=True)
                y_ref[j * half_count : (j + 1) * half_count, :slots] = weights
            to_ref[:, part] = y_ref[:, :slots].astype(BF16)
        sums_ref[...] = jnp.broadcast_to(class_total, (half_count, LANES))
    sum_half(w_give_ref, x_ref, give_ref, y_ref)


def keep_kernel(w_ref, x_ref, keep_ref, y_ref):
    sum_half(w_ref, x_ref, keep_ref, y_ref)


def finish_kernel(keep_ref, total_ref, other_ref, sums_ref, totals_ref):
    rots = totals_ref.shape[1]
    tiles = sums_ref.shape[0] // rots
    low = lane_row() < LANES // 2

    def load(t):
        return keep_ref[:rots, tile_of(t)] + other_ref[:rots, tile_of(t)]

    for t in range(tiles):
        sums_ref[pl.ds(t, rots, stride=tiles), :] = unfold_tile(load, t, tiles, low)
    total = total_ref[:rots] + other_ref[:rots, tile_of(tiles)]
    here = lax.broadcasted_iota(jnp.int32, (rots, LANES), 0) == lax.broadcasted_iota(
        jnp.int32, (rots, LANES), 1
    )
    totals_ref[...] = jnp.sum(jnp.where(here, total, 0.0), axis=0, keepdims=True)[:, :rots]


def far_away(value):
    return pltpu.with_memory_space_constraint(value, pltpu.HBM)


def call(kernel, out_shape, count, limit, scratch=(), flops=0, moved=0, far=0):
    in_vmem = pl.BlockSpec(memory_space=pltpu.VMEM)
    return pl.pallas_call(
        kernel,
        out_shape=out_shape,
        in_specs=[pl.BlockSpec(memory_space=pltpu.HBM)] * far + [in_vmem] * (count - far),
        out_specs=jax.tree.map(lambda _: in_vmem, out_shape),
        scratch_shapes=list(scratch),
        cost_estimate=pl.CostEstimate(flops=flops, bytes_accessed=moved, transcendentals=0),
        compiler_params=pltpu.CompilerParams(vmem_limit_bytes=limit * MIB),
    )


def on_device(images, references, candidates, inv_noise):
    rows, top = candidates.shape
    cls_dev, rots, pixels = references.shape
    planes, owners = lax.axis_size("z"), lax.axis_size("xy")
    side = math.isqrt(pixels)
    tiles = pixels // LANES
    group = SLOTS * planes
    slots = owners * group
    assert cls_dev == 1 and planes == PLANES and LANES == 2 * side and rows == group
    shape = jax.ShapeDtypeStruct
    exchange = functools.partial(lax.all_to_all, split_axis=0, concat_axis=0, tiled=True)

    packed = call(
        pack_kernel,
        shape(((tiles + 1) * rows, LANES), BF16),
        3,
        4,
        [
            pltpu.VMEM((top, rows), jnp.int32),
            pltpu.VMEM((1, rows), BF16),
            pltpu.VMEM((rows, pixels), BF16),
            pltpu.SemaphoreType.DMA((3,)),
        ],
        moved=MIB // 4,
        far=3,
    )(far_away(candidates.T), far_away(inv_noise[None, :]), far_away(images))

    def move(part, step):
        return lax.ppermute(part, "z", [(i, (i + step) % planes) for i in range(planes)])

    near = [move(packed, step) for step in (1, -1)]
    next_near = [move(packed, step) for step in (2, -2)]
    half_rots = rots // 2
    half_count = -(-half_rots // 8) * 8
    pad = half_count - half_rots
    count = 2 * half_count
    groups = len(COL_SHIFTS) * count
    shifted, half_norm = call(
        shift_kernel,
        (shape((len(ROW_SHIFTS) * groups, pixels), BF16), shape((count, LANES), F32)),
        1,
        6,
        [
            pltpu.VMEM((rots, pixels), BF16),
            pltpu.VMEM((count, pixels), BF16),
            pltpu.SemaphoreType.DMA,
        ],
        moved=12 * MIB,
        far=1,
    )(far_away(references[0]))
    cut = (tiles + 1) // 2 * rows
    far = [move(next_near[0], 1), move(next_near[1], -1)]
    far += [move(next_near[0][:cut], 2), move(next_near[1][cut:], -2)]
    column = [packed, *near, *next_near, *far]
    steps = [0, -1, 1, -2, 2, -3, 3, 4, 4]
    column, shifted, half_norm = lax.optimization_barrier((column, shifted, half_norm))
    picked = call(
        functools.partial(pick_kernel, steps=steps, top=top),
        shape((owners, (tiles + 1) * group, LANES), BF16),
        len(column),
        6,
        [pltpu.VMEM((planes * rows, (tiles + 1) * LANES), BF16)],
        moved=3 * MIB,
    )(*column)
    received = exchange(picked, "xy")
    work = 2 * len(ROW_SHIFTS) * groups * slots * pixels
    x, scores, tile = call(
        functools.partial(score_kernel, pad=pad),
        (
            shape((slots, pixels + 2 * LANES), BF16),
            shape((groups, len(ROW_SHIFTS) * slots), F32),
            shape((planes, 8, LANES), F32),
        ),
        3,
        8,
        flops=work,
        moved=10 * MIB,
    )(received, shifted, half_norm)
    folded = call(
        fold_kernel, shape((owners, 2 * rows, LANES), F32), 1, 4, moved=MIB // 4
    )(exchange(tile, "z"))
    everyone = exchange(folded, "xy")
    weight_shape = (groups // 2, len(ROW_SHIFTS) * slots)
    scratch = pltpu.VMEM((groups // 2, 4 * LANES), F32)
    give, weights, total = call(
        give_kernel,
        (
            shape((half_count, pixels + LANES), F32),
            shape(weight_shape, BF16),
            shape((half_count, LANES), F32),
        ),
        4,
        8,
        [pltpu.VMEM(weight_shape, BF16), scratch],
        flops=work // 2,
        moved=5 * MIB,
    )(scores, x, tile, everyone)
    other = lax.ppermute(give, "dp", [(0, 1), (1, 0)])
    keep = call(
        keep_kernel,
        shape((half_count, pixels), F32),
        2,
        8,
        [scratch],
        flops=work // 2,
        moved=4 * MIB,
    )(weights, x)
    sums, totals = call(
        finish_kernel,
        (shape((half_rots * tiles, LANES), F32), shape((1, half_rots), F32)),
        3,
        8,
        moved=2 * MIB,
    )(keep, total, other)
    return sums.reshape(1, half_rots, pixels), totals


def solution(mesh):
    split = (PLANES, mesh.shape["cls"] // PLANES, mesh.shape["dp"])
    cube = Mesh(mesh.devices.reshape(split), ("z", "xy", "dp"))
    every = ("z", "xy", "dp")
    by_class = ("z", "xy")
    return jax.shard_map(
        on_device,
        mesh=cube,
        in_specs=(P(every, None), P(by_class, None, None), P(every, None), P(every)),
        out_specs=(P(by_class, "dp", None), P(by_class, "dp")),
        check_vma=False,
    )
```

```python
import functools
import math

import jax
import jax.numpy as jnp
from jax import lax
from jax.experimental import pallas as pl
from jax.experimental.pallas import tpu as pltpu
from jax.sharding import Mesh
from jax.sharding import PartitionSpec as P

LANES = 128
SLOTS = 2
PLANES = 8
FAR = 1e30
ROW_SHIFTS = (0, 1, -1)
COL_SHIFTS = (0, 1, -1)
MIB = 1024 * 1024
F32, BF16 = jnp.float32, jnp.bfloat16


def tile_of(t):
    return slice(t * LANES, (t + 1) * LANES)


def lane_row():
    return lax.broadcasted_iota(jnp.int32, (1, LANES), 1)


def fold_tile(load, q, tiles, low):
    first, second = load(q // 2), load(tiles // 2 + q // 2)
    half = LANES // 2
    if q % 2 == 0:
        return jnp.where(low, first, pltpu.roll(second, half, 1))
    return jnp.where(low, pltpu.roll(first, half, 1), second)


def unfold_tile(load, t, tiles, low):
    half = LANES // 2
    if t < tiles // 2:
        return jnp.where(low, load(2 * t), pltpu.roll(load(2 * t + 1), half, 1))
    first = 2 * t - tiles
    return jnp.where(low, pltpu.roll(load(first), half, 1), load(first + 1))


def pack_kernel(cand_at, noise_at, img_at, send_ref, cand_ref, noise_ref, img_ref, sems):
    pairs = ((cand_at, cand_ref), (noise_at, noise_ref), (img_at, img_ref))
    loads = [pltpu.make_async_copy(at, ref, sems.at[i]) for i, (at, ref) in enumerate(pairs)]
    for load in loads:
        load.start()
    for load in loads:
        load.wait()
    top, rows = cand_ref.shape
    tiles = img_ref.shape[1] // LANES
    low = lane_row() < LANES // 2
    row_id = lax.broadcasted_iota(jnp.int32, (rows, LANES), 0)
    lane_id = lax.broadcasted_iota(jnp.int32, (rows, LANES), 1)
    diagonal = lax.broadcasted_iota(jnp.int32, (rows, rows), 0) == lax.broadcasted_iota(
        jnp.int32, (rows, rows), 1
    )
    noise = jnp.sum(
        jnp.where(diagonal, noise_ref[...].astype(F32), 0.0), axis=1, keepdims=True
    )
    place = lax.broadcasted_iota(jnp.int32, (top, LANES), 1) == (
        lax.broadcasted_iota(jnp.int32, (top, LANES), 0) + 2
    )
    facts = lax.dot_general(
        cand_ref[...].astype(F32).astype(BF16),
        place.astype(F32).astype(BF16),
        (((0,), (0,)), ((), ())),
        preferred_element_type=F32,
    )
    facts = jnp.where(lane_id == 0, noise, facts)
    facts = jnp.where(lane_id == 1, (row_id + 1).astype(F32), facts)
    send_ref[tiles * rows :] = facts.astype(BF16)
    for q in range(tiles):
        tile = fold_tile(lambda t: img_ref[:, tile_of(t)].astype(F32), q, tiles, low)
        send_ref[q * rows : (q + 1) * rows] = tile.astype(BF16)


def pick_kernel(*refs, steps, top):
    planes = len(steps)
    recv_refs, send_ref, column_ref = refs[:planes], refs[-2], refs[-1]
    owners, depth, _ = send_ref.shape
    rows = column_ref.shape[0] // planes
    tiles = column_ref.shape[1] // LANES
    group = depth // tiles
    slots = owners * group
    for j in range(planes):
        for t in range(tiles):
            column_ref[j * rows : (j + 1) * rows, tile_of(t)] = recv_refs[j][
                t * rows : (t + 1) * rows
            ]
    count = planes * rows
    facts = column_ref[:, tile_of(tiles - 1)].astype(F32)
    here = lax.axis_index("z")
    way = 1 - 2 * lax.axis_index("dp")
    row = lax.broadcasted_iota(jnp.int32, (count, 1), 0)
    sender = jnp.zeros((count, 1), jnp.int32)
    for j in range(planes):
        plane = lax.rem(here + way * steps[j] + planes, planes)
        sender = jnp.where(row // rows == j, plane, sender)
    lane = lax.broadcasted_iota(jnp.int32, (1, slots), 1)
    cls = (here * owners + lane // group).astype(F32)
    member = facts[:, 2:3] == cls
    for k in range(1, top):
        member = member | (facts[:, 2 + k : 3 + k] == cls)
    one, other = (lax.broadcasted_iota(jnp.int32, (count, count), i) for i in range(2))
    earlier = (one > other) & (one // rows == other // rows)
    before = jnp.dot(
        earlier.astype(F32).astype(BF16),
        member.astype(F32).astype(BF16),
        preferred_element_type=F32,
    )
    slot = (lane // planes) % SLOTS
    pick = member & (before == slot.astype(F32)) & (lane % planes == sender)
    pick = pick.astype(F32).T.astype(BF16)
    width = 3
    for t in range(0, tiles, width):
        lanes = slice(t * LANES, (t + width) * LANES)
        got = jnp.dot(pick, column_ref[:, lanes], preferred_element_type=F32).astype(BF16)
        for i in range(width):
            for c in range(owners):
                send_ref[c, (t + i) * group : (t + i + 1) * group] = got[
                    c * group : (c + 1) * group, tile_of(i)
                ]


def shift_kernel(from_at, out_ref, half_ref, from_ref, rot_ref, sem):
    load = pltpu.make_async_copy(from_at, from_ref, sem)
    load.start()
    load.wait()
    count, pixels = rot_ref.shape
    rots = from_ref.shape[0]
    half_count, half_rots = count // 2, rots // 2
    to = lax.broadcasted_iota(jnp.int32, (count, rots), 0)
    place = jnp.where(to < half_count, to, to - half_count + half_rots)
    real = to % half_count < half_rots
    own_first = lax.axis_index("dp") * half_rots
    place = jnp.where(place + own_first < rots, place + own_first, place + own_first - rots)
    chosen = (place == lax.broadcasted_iota(jnp.int32, (count, rots), 1)) & real
    picked = jnp.dot(chosen.astype(F32).astype(BF16), from_ref[...], preferred_element_type=F32)
    half = 0.5 * jnp.sum(picked * picked, axis=1, keepdims=True)
    half_ref[...] = jnp.broadcast_to(half, half_ref.shape)
    rot_ref[...] = picked.astype(BF16)
    tiles = pixels // LANES
    side = LANES // 2
    groups = len(COL_SHIFTS) * count
    source = lax.broadcasted_iota(jnp.int32, (2 * LANES, LANES), 0)
    lane = lax.broadcasted_iota(jnp.int32, (2 * LANES, LANES), 1)
    moves = []
    for parity in range(2):
        for shift in COL_SHIFTS:
            col = (lane - shift + side) % side
            home = (lane // side) * LANES + parity * side + col
            moves.append((source == home).astype(F32).astype(BF16))
    moves = jnp.concatenate(moves, axis=1)
    turn = ((lane[:LANES] + side) % LANES == source[:LANES]).astype(F32).astype(BF16)
    for h in range(tiles // 2):
        pair = jnp.concatenate(
            [rot_ref[:, tile_of(h)], rot_ref[:, tile_of(tiles // 2 + h)]], axis=1
        )
        moved = jnp.dot(pair, moves, preferred_element_type=F32).astype(BF16)
        for parity in range(2):
            for i in range(len(COL_SHIFTS)):
                plain = moved[:, tile_of(parity * len(COL_SHIFTS) + i)]
                for j, shift in enumerate(ROW_SHIFTS):
                    at = 2 * h + parity + shift
                    value = plain
                    if not 0 <= at < tiles:
                        at = at % tiles
                        value = jnp.dot(plain, turn, preferred_element_type=F32).astype(BF16)
                    first = j * groups + i * count
                    out_ref[first : first + count, tile_of(at)] = value


def score_kernel(recv_ref, shifted_ref, half_ref, x_ref, s_ref, tile_ref, *, pad):
    owners, depth, _ = recv_ref.shape
    tiles = x_ref.shape[1] // LANES - 2
    group = depth // (tiles + 1)
    slots = owners * group
    groups = s_ref.shape[0]
    count = half_ref.shape[0]
    for c in range(owners):
        for t in range(tiles):
            x_ref[c * group : (c + 1) * group, tile_of(t + 1)] = recv_ref[
                c, t * group : (t + 1) * group
            ]
    half_turn = LANES // 2
    x_ref[:, tile_of(0)] = pltpu.roll(x_ref[:, tile_of(tiles)].astype(F32), half_turn, 1).astype(
        BF16
    )
    x_ref[:, tile_of(tiles + 1)] = pltpu.roll(x_ref[:, tile_of(1)].astype(F32), half_turn, 1).astype(
        BF16
    )
    facts = recv_ref[:, tiles * group :, :].reshape(slots, LANES)
    choose = (
        lax.broadcasted_iota(jnp.int32, (16, LANES), 0)
        == lax.broadcasted_iota(jnp.int32, (16, LANES), 1)
    ).astype(F32).astype(BF16)
    turned = lax.dot_general(
        choose, facts, (((1,), (1,)), ((), ())), preferred_element_type=F32
    )
    noise, number = turned[0:1], turned[1:2]
    products = lax.dot_general(
        shifted_ref[...],
        x_ref[:, LANES : (tiles + 1) * LANES],
        (((1,), (1,)), ((), ())),
        preferred_element_type=F32,
    )
    half = half_ref[:, 0:1]
    row = lax.broadcasted_iota(jnp.int32, half.shape, 0)
    half = jnp.where(row % (count // 2) >= count // 2 - pad, FAR, half)
    half = jnp.concatenate([half] * len(COL_SHIFTS), axis=0)
    peak = None
    for i in range(len(ROW_SHIFTS)):
        scores = noise * (products[i * groups : (i + 1) * groups] - half)
        s_ref[:, i * slots : (i + 1) * slots] = scores
        top = jnp.max(scores, axis=0, keepdims=True)
        peak = top if peak is None else jnp.maximum(peak, top)
    total = jnp.zeros_like(peak)
    for i in range(len(ROW_SHIFTS)):
        scores = s_ref[:, i * slots : (i + 1) * slots]
        total = total + jnp.sum(jnp.exp(scores - peak), axis=0, keepdims=True)
    parts = slots // LANES
    for i, value in enumerate((peak, total, number)):
        for h in range(parts):
            tile_ref[0, i * parts + h : i * parts + h + 1] = value[:, tile_of(h)]
    tile_ref[0, 3 * parts :] = jnp.zeros_like(tile_ref[0, 3 * parts :])
    for i in range(1, tile_ref.shape[0]):
        tile_ref[i] = tile_ref[0]


def partner_of(rows):
    second = (lane_row() // PLANES) % SLOTS == 1
    return jnp.where(
        second, pltpu.roll(rows, PLANES, 1), pltpu.roll(rows, LANES - PLANES, 1)
    )


def fold_kernel(shown_ref, out_ref):
    planes = shown_ref.shape[0]
    rows = out_ref.shape[1] // 2
    second = (lane_row() // PLANES) % SLOTS == 1
    parts = 2
    shown = [
        [
            jnp.concatenate(
                [shown_ref[z, i * parts + h : i * parts + h + 1] for z in range(planes)], axis=0
            )
            for h in range(parts)
        ]
        for i in range(3)
    ]
    for p in range(rows):
        found = []
        for h in range(parts):
            same = shown[2][h] == p + 1
            peak = jnp.max(jnp.where(same, shown[0][h], -FAR), axis=0, keepdims=True)
            peak = jnp.maximum(peak, partner_of(peak))
            part = shown[1][h] * jnp.exp(jnp.minimum(shown[0][h] - peak, 0.0))
            total = jnp.sum(jnp.where(same, part, 0.0), axis=0, keepdims=True)
            found.append((peak, total + partner_of(total)))
        out_ref[0, p : p + 1] = jnp.where(second, found[1][0], found[0][0])
        out_ref[0, rows + p : rows + p + 1] = jnp.where(second, found[1][1], found[0][1])
    for i in range(1, out_ref.shape[0]):
        out_ref[i] = out_ref[0]


def sum_half(w_ref, x_ref, out_ref, y_ref):
    slots = x_ref.shape[0]
    pixels = x_ref.shape[1] - 2 * LANES
    count = y_ref.shape[0] // len(COL_SHIFTS)
    side = LANES // 2
    width = y_ref.shape[1]
    column = lane_row() % side
    for first in range(0, pixels, width):
        y_ref[...] = sum(
            jnp.dot(
                w_ref[:, i * slots : (i + 1) * slots],
                x_ref[:, (1 + shift) * LANES + first : (1 + shift) * LANES + first + width],
                preferred_element_type=F32,
            )
            for i, shift in enumerate(ROW_SHIFTS)
        )
        for t in range(width // LANES):
            plain = y_ref[:count, tile_of(t)]
            right = y_ref[count : 2 * count, tile_of(t)]
            left = y_ref[2 * count :, tile_of(t)]
            back = jnp.where(
                column == side - 1,
                pltpu.roll(right, side - 1, 1),
                pltpu.roll(right, LANES - 1, 1),
            )
            forth = jnp.where(
                column == 0, pltpu.roll(left, LANES - side + 1, 1), pltpu.roll(left, 1, 1)
            )
            out_ref[:, first + t * LANES : first + (t + 1) * LANES] = plain + back + forth


def give_kernel(s_ref, x_ref, mine_ref, all_ref, give_ref, w_ref, total_ref, w_give_ref, y_ref):
    groups = s_ref.shape[0]
    slots = x_ref.shape[0]
    pixels = x_ref.shape[1] - 2 * LANES
    rows = all_ref.shape[1] // 2
    count = groups // len(COL_SHIFTS)
    half_count = count // 2
    parts = slots // LANES
    second = (lane_row() // PLANES) % SLOTS == 1
    tables = range(all_ref.shape[0])
    peak = all_ref[0, :rows]
    for i in tables:
        peak = jnp.maximum(peak, all_ref[i, :rows])
    total = jnp.zeros_like(peak)
    for i in tables:
        total = total + all_ref[i, rows:] * jnp.exp(all_ref[i, :rows] - peak)
    number = lax.broadcasted_iota(jnp.int32, (rows, LANES), 0).astype(F32) + 1
    peaks, scales = [], []
    for h in range(parts):
        own = mine_ref[0, 2 * parts + h : 2 * parts + h + 1]
        here = second == (h == 1)
        mine = [
            jnp.sum(
                jnp.where(number == own, jnp.where(here, table, partner_of(table)), 0.0),
                axis=0,
                keepdims=True,
            )
            for table in (peak, total)
        ]
        peaks.append(mine[0])
        scales.append(jnp.where(own > 0, 1.0 / jnp.where(own > 0, mine[1], 1.0), 0.0))
    peak = jnp.concatenate(peaks, axis=1)
    scale = jnp.concatenate(scales, axis=1)
    for half, to_ref, sums_ref in ((0, w_ref, total_ref), (1, w_give_ref, give_ref.at[:, pixels:])):
        class_total = jnp.zeros((half_count, 1), F32)
        for i in range(len(ROW_SHIFTS)):
            part = slice(i * slots, (i + 1) * slots)
            for j in range(len(COL_SHIFTS)):
                first = j * count + half * half_count
                weights = s_ref[first : first + half_count, part]
                weights = jnp.exp(jnp.minimum(weights - peak, 0.0)) * scale
                weights = weights.astype(BF16).astype(F32)
                class_total = class_total + jnp.sum(weights, axis=1, keepdims=True)
                y_ref[j * half_count : (j + 1) * half_count, :slots] = weights
            to_ref[:, part] = y_ref[:, :slots].astype(BF16)
        sums_ref[...] = jnp.broadcast_to(class_total, (half_count, LANES))
    sum_half(w_give_ref, x_ref, give_ref, y_ref)


def keep_kernel(w_ref, x_ref, keep_ref, y_ref):
    sum_half(w_ref, x_ref, keep_ref, y_ref)


def finish_kernel(keep_ref, total_ref, other_ref, sums_ref, totals_ref):
    rots = totals_ref.shape[1]
    tiles = sums_ref.shape[0] // rots
    low = lane_row() < LANES // 2

    def load(t):
        return keep_ref[:rots, tile_of(t)] + other_ref[:rots, tile_of(t)]

    for t in range(tiles):
        sums_ref[pl.ds(t, rots, stride=tiles), :] = unfold_tile(load, t, tiles, low)
    total = total_ref[:rots] + other_ref[:rots, tile_of(tiles)]
    here = lax.broadcasted_iota(jnp.int32, (rots, LANES), 0) == lax.broadcasted_iota(
        jnp.int32, (rots, LANES), 1
    )
    totals_ref[...] = jnp.sum(jnp.where(here, total, 0.0), axis=0, keepdims=True)[:, :rots]


def far_away(value):
    return pltpu.with_memory_space_constraint(value, pltpu.HBM)


def call(kernel, out_shape, count, limit, scratch=(), flops=0, moved=0, far=0):
    in_vmem = pl.BlockSpec(memory_space=pltpu.VMEM)
    return pl.pallas_call(
        kernel,
        out_shape=out_shape,
        in_specs=[pl.BlockSpec(memory_space=pltpu.HBM)] * far + [in_vmem] * (count - far),
        out_specs=jax.tree.map(lambda _: in_vmem, out_shape),
        scratch_shapes=list(scratch),
        cost_estimate=pl.CostEstimate(flops=flops, bytes_accessed=moved, transcendentals=0),
        compiler_params=pltpu.CompilerParams(vmem_limit_bytes=limit * MIB),
    )


def on_device(images, references, candidates, inv_noise):
    rows, top = candidates.shape
    cls_dev, rots, pixels = references.shape
    planes, owners = lax.axis_size("z"), lax.axis_size("xy")
    side = math.isqrt(pixels)
    tiles = pixels // LANES
    group = SLOTS * planes
    slots = owners * group
    assert cls_dev == 1 and planes == PLANES and LANES == 2 * side and rows == group
    shape = jax.ShapeDtypeStruct
    exchange = functools.partial(lax.all_to_all, split_axis=0, concat_axis=0, tiled=True)

    packed = call(
        pack_kernel,
        shape(((tiles + 1) * rows, LANES), BF16),
        3,
        4,
        [
            pltpu.VMEM((top, rows), jnp.int32),
            pltpu.VMEM((1, rows), BF16),
            pltpu.VMEM((rows, pixels), BF16),
            pltpu.SemaphoreType.DMA((3,)),
        ],
        moved=MIB // 4,
        far=3,
    )(far_away(candidates.T), far_away(inv_noise[None, :]), far_away(images))

    def move(part, step):
        pairs = []
        for z in range(planes):
            pairs += [
                (2 * z, (z + step) % planes * 2),
                (2 * z + 1, (z - step) % planes * 2 + 1),
            ]
        return lax.ppermute(part, ("z", "dp"), pairs)

    near = [move(packed, step) for step in (1, -1)]
    next_near = [move(packed, step) for step in (2, -2)]
    half_rots = rots // 2
    half_count = -(-half_rots // 8) * 8
    pad = half_count - half_rots
    count = 2 * half_count
    groups = len(COL_SHIFTS) * count
    shifted, half_norm = call(
        shift_kernel,
        (shape((len(ROW_SHIFTS) * groups, pixels), BF16), shape((count, LANES), F32)),
        1,
        6,
        [
            pltpu.VMEM((rots, pixels), BF16),
            pltpu.VMEM((count, pixels), BF16),
            pltpu.SemaphoreType.DMA,
        ],
        moved=12 * MIB,
        far=1,
    )(far_away(references[0]))
    far = [move(next_near[0], 1), move(next_near[1], -1), move(next_near[0], 2)]
    column = [packed, *near, *next_near, *far]
    steps = [0, -1, 1, -2, 2, -3, 3, 4]
    column, shifted, half_norm = lax.optimization_barrier((column, shifted, half_norm))
    picked = call(
        functools.partial(pick_kernel, steps=steps, top=top),
        shape((owners, (tiles + 1) * group, LANES), BF16),
        len(column),
        6,
        [pltpu.VMEM((planes * rows, (tiles + 1) * LANES), BF16)],
        moved=3 * MIB,
    )(*column)
    received = exchange(picked, "xy")
    work = 2 * len(ROW_SHIFTS) * groups * slots * pixels
    x, scores, tile = call(
        functools.partial(score_kernel, pad=pad),
        (
            shape((slots, pixels + 2 * LANES), BF16),
            shape((groups, len(ROW_SHIFTS) * slots), F32),
            shape((planes, 8, LANES), F32),
        ),
        3,
        8,
        flops=work,
        moved=10 * MIB,
    )(received, shifted, half_norm)
    folded = call(
        fold_kernel, shape((owners, 2 * rows, LANES), F32), 1, 4, moved=MIB // 4
    )(exchange(tile, "z"))
    everyone = exchange(folded, "xy")
    weight_shape = (groups // 2, len(ROW_SHIFTS) * slots)
    scratch = pltpu.VMEM((groups // 2, 4 * LANES), F32)
    give, weights, total = call(
        give_kernel,
        (
            shape((half_count, pixels + LANES), F32),
            shape(weight_shape, BF16),
            shape((half_count, LANES), F32),
        ),
        4,
        8,
        [pltpu.VMEM(weight_shape, BF16), scratch],
        flops=work // 2,
        moved=5 * MIB,
    )(scores, x, tile, everyone)
    other = lax.ppermute(give, "dp", [(0, 1), (1, 0)])
    keep = call(
        keep_kernel,
        shape((half_count, pixels), F32),
        2,
        8,
        [scratch],
        flops=work // 2,
        moved=4 * MIB,
    )(weights, x)
    sums, totals = call(
        finish_kernel,
        (shape((half_rots * tiles, LANES), F32), shape((1, half_rots), F32)),
        3,
        8,
        moved=2 * MIB,
    )(keep, total, other)
    return sums.reshape(1, half_rots, pixels), totals


def solution(mesh):
    split = (PLANES, mesh.shape["cls"] // PLANES, mesh.shape["dp"])
    cube = Mesh(mesh.devices.reshape(split), ("z", "xy", "dp"))
    every = ("z", "xy", "dp")
    by_class = ("z", "xy")
    return jax.shard_map(
        on_device,
        mesh=cube,
        in_specs=(P(every, None), P(by_class, None, None), P(every, None), P(every)),
        out_specs=(P(by_class, "dp", None), P(by_class, "dp")),
        check_vma=False,
    )
```
